32 devices in a mesh: gz: 8 (over z, y), gx: 4 (over x, core).
Axes of the slice: x: 2, y: 2, z: 4, core: 2. Of those that a mesh axis runs over, the one named last changes fastest.
Arguments:
- density: float32 [16, 256, 256], P('gz', 'gx'), may hold values from -6 to 6
- green: float32 [2, 32, 512, 512], P(None, None, 'gz', 'gx'), may hold values from -12 to 12
- image_green: float32 [2, 32, 512, 512], P(None, None, 'gz', 'gx'), may hold values from -12 to 12
Outputs:
- grad_x: float32 [16, 256, 256], P('gz', 'gx')
- grad_y: float32 [16, 256, 256], P('gz', 'gx')
- grad_z: float32 [16, 256, 256], P('gz', 'gx')
The draws below stay inside these ranges and needn't reach their ends.
All inputs are finite; a program needn't handle non-finite values.
Results may differ from the reference program's by a relative error of at most 0.00007.
Values sent between devices are 32-bit elements; how exact they have to be, the bound alone decides.
No kernel may reach another device: no remote copies, remote signals or barrier semaphores. Data moves between devices by JAX's collectives and lax.ppermute only.
A program may use at most 64 MiB of HBM per device.

```python
import jax
import jax.numpy as jnp
from jax import lax

NX = 256
NY = 256
NZ = 16


def block_scale(own_key, dims, cuts, least, high):
    def one(dim, parts):
        steps = jax.random.uniform(jax.random.fold_in(jax.random.fold_in(own_key, 6), dim), (parts,), jnp.float32, least / len(cuts), high / len(cuts))
        return jnp.repeat(jnp.exp(steps), dims[dim] // parts).reshape((-1,) + (1,) * (len(dims) - dim - 1))

    loudness = one(*cuts[0])
    for cut in cuts[1:]:
        loudness = loudness * one(*cut)
    return loudness


def scatter_about(rng, extent, scale, bound, shards=(), kind=jnp.bfloat16):
    array = jax.random.normal(rng, extent, jnp.float32) * scale
    if len(shards) > 0:
        array = block_scale(rng, extent, shards, -0.22, 0.18) * array
    return jnp.clip(array, min=-bound, max=bound).astype(kind)


def setup_inputs(seed: int = 0) -> dict:
    key_of = jax.random.split(jax.random.key(seed), 4)
    density = scatter_about(key_of[0], (NZ, NX, NY), 1.0, 6.0, ((0, 8), (1, 4)), jnp.float32)
    green = scatter_about(key_of[1], (2, 2 * NZ, 2 * NX, 2 * NY), 2.0, 12.0, ((2, 8), (3, 4)), jnp.float32)
    image_green = scatter_about(key_of[2], (2, 2 * NZ, 2 * NX, 2 * NY), 2.0, 12.0, ((2, 8), (3, 4)), jnp.float32)
    return {"density": density, "green": green, "image_green": image_green}


def difference(field, axis):
    count = field.shape[axis]
    inner = (lax.slice_in_dim(field, 2, count, axis=axis) - lax.slice_in_dim(field, 0, count - 2, axis=axis)) * 0.5
    first = lax.slice_in_dim(field, 1, 2, axis=axis) - lax.slice_in_dim(field, 0, 1, axis=axis)
    last = lax.slice_in_dim(field, count - 1, count, axis=axis) - lax.slice_in_dim(field, count - 2, count - 1, axis=axis)
    return jnp.concatenate([first, inner, last], axis=axis)


def reference(density, green, image_green):
    depth, width, height = density.shape
    mirrored = density[::-1]
    padded_real = jnp.zeros((2 * depth, 2 * width, 2 * height), density.dtype).at[:depth, :width, :height].set(density)
    padded_image = jnp.zeros((2 * depth, 2 * width, 2 * height), density.dtype).at[:depth, :width, :height].set(mirrored)
    real_spec = jnp.fft.fftn(padded_real)
    image_spec = jnp.fft.fftn(padded_image)
    product = lax.complex(green[0], green[1]) * real_spec + lax.complex(image_green[0], image_green[1]) * image_spec
    potential = jnp.real(jnp.fft.ifftn(product))[:depth, :width, :height].astype(density.dtype)
    return difference(potential, 1), difference(potential, 2), difference(potential, 0)
```

```python
import functools
import math

import jax
import jax.numpy as jnp
import numpy as np
from jax import lax
from jax.experimental import pallas as pl
from jax.experimental.pallas import tpu as pltpu
from jax.sharding import PartitionSpec as P

VMEM = pltpu.VMEM
SMEM = pltpu.SMEM


def halves(table):
    high = table.astype(jnp.bfloat16)
    low = (table - high.astype(np.float64)).astype(jnp.bfloat16)
    return high, low


def split(value):
    high = value.astype(jnp.bfloat16)
    return high, (value - high.astype(jnp.float32)).astype(jnp.bfloat16)


def product3(left, right, dims):
    one = functools.partial(
        lax.dot_general, dimension_numbers=(dims, ((), ())), preferred_element_type=jnp.float32
    )
    return one(left[0], right[0]) + (one(left[1], right[0]) + one(left[0], right[1]))


def turned(value):
    wide = value.shape[1] // 2
    swapped = jnp.concatenate([-value[:, wide:], value[:, :wide]], axis=1)
    return jnp.concatenate([value, swapped], axis=0)


def angles(space, freq):
    turns = np.outer(np.arange(freq), np.arange(space)) % freq
    return turns * (2.0 * math.pi / freq)


def column_table(space, blocks):
    angle = angles(space, 2 * space).reshape(blocks, -1, space)
    return halves(np.concatenate([np.cos(angle), -np.sin(angle)], axis=1))


def forward_table(space):
    angle = angles(space, 2 * space)
    return halves(np.concatenate([np.cos(angle), -np.sin(angle)], axis=1))


def inverse_table(space):
    angle = angles(space, 2 * space).T
    return halves(np.concatenate([np.cos(angle), np.sin(angle)], axis=1))


def times(value, turns, length):
    turns %= length
    re, im = value
    if turns == 0:
        return value
    if 4 * turns == length:
        return -im, re
    if 2 * turns == length:
        return -re, -im
    if 4 * turns == 3 * length:
        return im, -re
    c = math.cos(2.0 * math.pi * turns / length)
    s = math.sin(2.0 * math.pi * turns / length)
    if 8 * turns % length == 0:
        r = math.sqrt(0.5)
        if c * s > 0:
            return math.copysign(r, c) * (re - im), math.copysign(r, c) * (re + im)
        return math.copysign(r, c) * (re + im), math.copysign(r, c) * (im - re)
    return c * re - s * im, c * im + s * re


def add(a, b):
    return a[0] + b[0], a[1] + b[1]


def sub(a, b):
    return a[0] - b[0], a[1] - b[1]


def fft(values, sign):
    count = len(values)
    if count == 1:
        return values
    even, odd = fft(values[0::2], sign), fft(values[1::2], sign)
    odd = [times(v, sign * k, count) for k, v in enumerate(odd)]
    return [add(a, b) for a, b in zip(even, odd)] + [sub(a, b) for a, b in zip(even, odd)]


def forward_kernel(x_ref, yh_ref, yl_ref, th_ref, tl_ref, out_ref):
    table_y = (yh_ref[...], yl_ref[...])
    table_x = (th_ref[...], tl_ref[...])
    spec = product3(split(x_ref[0]), table_y, ((1,), (1,)))
    both = product3(table_x, split(turned(spec)), ((1,), (0,)))
    out_ref[:, 0] = both.reshape(out_ref.shape[0], *out_ref.shape[2:])


def forward(rows, table_y, table_x, blocks):
    slabs, width, height = rows.shape
    wide = table_y[0].shape[0]
    kx = 2 * width // blocks
    whole = lambda a: pl.BlockSpec(a.shape, lambda z: (0,) * a.ndim)
    return pl.pallas_call(
        forward_kernel,
        grid=(slabs,),
        in_specs=[pl.BlockSpec((1, width, height), lambda z: (z, 0, 0))]
        + [whole(a) for a in (*table_y, *table_x)],
        out_specs=pl.BlockSpec((blocks, 1, kx, wide), lambda z: (0, z, 0, 0)),
        out_shape=jax.ShapeDtypeStruct((blocks, slabs, kx, wide), jnp.float32),
        name="forward_xy",
    )(rows, *table_y, *table_x)


def middle_kernel(f_ref, g_ref, h_ref, out_ref):
    slabs = f_ref.shape[1]
    depth = f_ref.shape[0] * slabs
    length = 2 * depth
    half = f_ref.shape[3] // 2
    field = [
        (f_ref[z // slabs, z % slabs, :, :half], f_ref[z // slabs, z % slabs, :, half:])
        for z in range(depth)
    ]
    even = fft(field, -1)
    odd = fft([times(v, -z, length) for z, v in enumerate(field)], -1)
    spec = [v for pair in zip(even, odd) for v in pair]
    product = []
    for k in range(length):
        re, im = spec[k]
        mre, mim = times(spec[-k % length], -k * (depth - 1), length)
        gre, gim, hre, him = g_ref[0, k], g_ref[1, k], h_ref[0, k], h_ref[1, k]
        product.append(
            (
                gre * re - gim * im + hre * mre - him * mim,
                gre * im + gim * re + hre * mim + him * mre,
            )
        )
    even = fft(product[0::2], 1)
    odd = fft(product[1::2], 1)
    for z in range(depth):
        re, im = add(even[z], times(odd[z], z, length))
        out_ref[z // slabs, z % slabs, :, :half] = re
        out_ref[z // slabs, z % slabs, :, half:] = im


def middle(field, green, image_green):
    blocks, slabs, kx, wide = field.shape
    tile = 8
    spec = pl.BlockSpec((blocks, slabs, tile, wide), lambda i: (0, 0, i, 0))
    gspec = pl.BlockSpec((*green.shape[:2], tile, green.shape[3]), lambda i: (0, 0, i, 0))
    return pl.pallas_call(
        middle_kernel,
        grid=(kx // tile,),
        in_specs=[spec, gspec, gspec],
        out_specs=spec,
        out_shape=jax.ShapeDtypeStruct(field.shape, jnp.float32),
        name="middle_z",
    )(field, green, image_green)


def inverse_x_kernel(q_ref, th_ref, tl_ref, out_ref):
    field = q_ref[:, 0].reshape(-1, q_ref.shape[3])
    rows = product3((th_ref[...], tl_ref[...]), split(turned(field)), ((1,), (0,)))
    parts = out_ref.shape[0]
    count = rows.shape[0] // parts
    for part in range(parts):
        start = part * count
        before, after = max(start - 1, 0), min(start + count, rows.shape[0] - 1)
        out_ref[part, 0, :count] = rows[start : start + count]
        out_ref[part, 0, count : count + 8] = jnp.concatenate(
            [rows[before : before + 1], rows[after : after + 1], rows[:6]], axis=0
        )


def inverse_x(field, table, parts):
    blocks, slabs, kx, wide = field.shape
    width = blocks * kx // 2
    whole = lambda a: pl.BlockSpec(a.shape, lambda z: (0,) * a.ndim)
    shape = (parts, slabs, width // parts + 8, wide)
    return pl.pallas_call(
        inverse_x_kernel,
        grid=(slabs,),
        in_specs=[pl.BlockSpec((blocks, 1, kx, wide), lambda z: (0, z, 0, 0))]
        + [whole(a) for a in table],
        out_specs=pl.BlockSpec((parts, 1, *shape[2:]), lambda z: (0, z, 0, 0)),
        out_shape=jax.ShapeDtypeStruct(shape, jnp.float32),
        name="inverse_x",
    )(field, *table)


def inverse_y_kernel(scale, parts, me_ref, s_ref, th_ref, tl_ref, pot_ref, gx_ref, gy_ref):
    me = me_ref[0]
    count = s_ref.shape[2] - 8
    height = th_ref.shape[2]
    for z in range(s_ref.shape[1]):
        total = None
        for part in range(parts):
            term = product3(
                split(s_ref[part, z]), (th_ref[part], tl_ref[part]), ((1,), (0,))
            )
            total = term if total is None else total + term
        total = total * scale
        main = total[:count]
        row = lax.broadcasted_iota(jnp.int32, main.shape, 0)
        before = jnp.where(row == 0, total[count : count + 1], pltpu.roll(main, 1, 0))
        after = jnp.where(
            row == count - 1, total[count + 1 : count + 2], pltpu.roll(main, count - 1, 0)
        )
        edge = ((row == 0) & (me == 0)) | ((row == count - 1) & (me == parts - 1))
        gx_ref[z] = (after - before) * jnp.where(edge, 1.0, 0.5)
        col = lax.broadcasted_iota(jnp.int32, main.shape, 1)
        before = jnp.where(col == 0, main, pltpu.roll(main, 1, 1))
        after = jnp.where(col == height - 1, main, pltpu.roll(main, height - 1, 1))
        gy_ref[z] = (after - before) * jnp.where((col == 0) | (col == height - 1), 1.0, 0.5)
        pot_ref[z] = main


def inverse_y(rows, table, me, scale):
    parts, slabs, count, _ = rows.shape
    shape = jax.ShapeDtypeStruct((slabs, count - 8, table[0].shape[2]), jnp.float32)
    vmem = pl.BlockSpec(memory_space=VMEM)
    return pl.pallas_call(
        functools.partial(inverse_y_kernel, scale, parts),
        in_specs=[pl.BlockSpec(memory_space=SMEM), vmem, vmem, vmem],
        out_specs=(vmem, vmem, vmem),
        out_shape=(shape, shape, shape),
        name="inverse_y",
    )(me, rows, *table)


def slope_z(pot):
    slabs = pot.shape[0]
    size, me = lax.axis_size("gz"), lax.axis_index("gz")
    below = lax.ppermute(pot[-1], "gz", [(i, i + 1) for i in range(size - 1)])
    above = lax.ppermute(pot[0], "gz", [(i + 1, i) for i in range(size - 1)])
    below = jnp.where(me == 0, pot[0], below)
    above = jnp.where(me == size - 1, pot[-1], above)
    padded = jnp.concatenate([below[None], pot, above[None]])
    row = lax.broadcasted_iota(jnp.int32, (slabs, 1, 1), 0)
    edge = ((row == 0) & (me == 0)) | ((row == slabs - 1) & (me == size - 1))
    return (padded[2:] - padded[:-2]) * jnp.where(edge, 1.0, 0.5)


def per_device(density, green, image_green):
    slabs, _, height = density.shape
    gz, gx = lax.axis_size("gz"), lax.axis_size("gx")
    width = density.shape[1] * gx
    depth = slabs * gz
    column = column_table(height, gx)
    me = lax.axis_index("gx")
    own = tuple(lax.dynamic_index_in_dim(jnp.asarray(t), me, 0, keepdims=False) for t in column)
    rows = lax.all_gather(density, "gx", axis=1, tiled=True)
    field = forward(rows, own, forward_table(width), gz)
    field = lax.all_to_all(field, "gz", split_axis=0, concat_axis=0, tiled=True)
    field = middle(field, green, image_green)
    field = lax.all_to_all(field, "gz", split_axis=0, concat_axis=0, tiled=True)
    part = inverse_x(field, inverse_table(width), gx)
    part = lax.all_to_all(part, "gx", split_axis=0, concat_axis=0, tiled=True)
    scale = 1.0 / (8.0 * depth * width * height)
    pot, grad_x, grad_y = inverse_y(part, column, me.astype(jnp.int32).reshape(1), scale)
    return grad_x, grad_y, slope_z(pot)


def solution(mesh):
    return jax.shard_map(
        per_device,
        mesh=mesh,
        in_specs=(P("gz", "gx", None), P(None, None, "gz", "gx"), P(None, None, "gz", "gx")),
        out_specs=(P("gz", "gx", None), P("gz", "gx", None), P("gz", "gx", None)),
        check_vma=False,
    )
```

```python
import functools
import math

import jax
import jax.numpy as jnp
import numpy as np
from jax import lax
from jax.experimental import pallas as pl
from jax.experimental.pallas import tpu as pltpu
from jax.sharding import PartitionSpec as P

VMEM = pltpu.VMEM
SMEM = pltpu.SMEM


def halves(table):
    high = table.astype(jnp.bfloat16)
    low = (table - high.astype(np.float64)).astype(jnp.bfloat16)
    return high, low


def split(value):
    high = value.astype(jnp.bfloat16)
    return high, (value - high.astype(jnp.float32)).astype(jnp.bfloat16)


def product3(left, right, dims):
    one = functools.partial(
        lax.dot_general, dimension_numbers=(dims, ((), ())), preferred_element_type=jnp.float32
    )
    return one(left[0], right[0]) + (one(left[1], right[0]) + one(left[0], right[1]))


def turned(value):
    wide = value.shape[1] // 2
    swapped = jnp.concatenate([-value[:, wide:], value[:, :wide]], axis=1)
    return jnp.concatenate([value, swapped], axis=0)


def angles(space, freq):
    turns = np.outer(np.arange(freq), np.arange(space)) % freq
    return turns * (2.0 * math.pi / freq)


def column_table(space, blocks):
    angle = angles(space, 2 * space).reshape(blocks, -1, space)
    return halves(np.concatenate([np.cos(angle), -np.sin(angle)], axis=1))


def forward_table(space):
    angle = angles(space, 2 * space)
    return halves(np.concatenate([np.cos(angle), -np.sin(angle)], axis=1))


def inverse_table(space):
    angle = angles(space, 2 * space).T
    return halves(np.concatenate([np.cos(angle), np.sin(angle)], axis=1))


def half_inverse_table(space, parts):
    angle = angles(space, 2 * space).T
    count = space // parts
    rows = []
    for start in range(0, space, count):
        rows += [*range(start, start + count), max(start - 1, 0), min(start + count, space - 1)]
        rows += [start] * 6
    angle = angle[np.array(rows)].reshape(len(rows), 2, space).transpose(1, 0, 2)
    return halves(np.concatenate([np.cos(angle), np.sin(angle)], axis=2))


def times(value, turns, length):
    turns %= length
    re, im = value
    if turns == 0:
        return value
    if 4 * turns == length:
        return -im, re
    if 2 * turns == length:
        return -re, -im
    if 4 * turns == 3 * length:
        return im, -re
    c = math.cos(2.0 * math.pi * turns / length)
    s = math.sin(2.0 * math.pi * turns / length)
    if 8 * turns % length == 0:
        r = math.sqrt(0.5)
        if c * s > 0:
            return math.copysign(r, c) * (re - im), math.copysign(r, c) * (re + im)
        return math.copysign(r, c) * (re + im), math.copysign(r, c) * (im - re)
    return c * re - s * im, c * im + s * re


def add(a, b):
    return a[0] + b[0], a[1] + b[1]


def sub(a, b):
    return a[0] - b[0], a[1] - b[1]


def fft(values, sign):
    count = len(values)
    if count == 1:
        return values
    even, odd = fft(values[0::2], sign), fft(values[1::2], sign)
    odd = [times(v, sign * k, count) for k, v in enumerate(odd)]
    return [add(a, b) for a, b in zip(even, odd)] + [sub(a, b) for a, b in zip(even, odd)]


def forward_kernel(x_ref, yh_ref, yl_ref, th_ref, tl_ref, out_ref):
    table_y = (yh_ref[...], yl_ref[...])
    table_x = (th_ref[...], tl_ref[...])
    spec = product3(split(x_ref[0]), table_y, ((1,), (1,)))
    both = product3(table_x, split(turned(spec)), ((1,), (0,)))
    out_ref[:, 0] = both.reshape(out_ref.shape[0], *out_ref.shape[2:])


def forward(rows, table_y, table_x, blocks):
    slabs, width, height = rows.shape
    wide = table_y[0].shape[0]
    kx = 2 * width // blocks
    whole = lambda a: pl.BlockSpec(a.shape, lambda z: (0,) * a.ndim)
    return pl.pallas_call(
        forward_kernel,
        grid=(slabs,),
        in_specs=[pl.BlockSpec((1, width, height), lambda z: (z, 0, 0))]
        + [whole(a) for a in (*table_y, *table_x)],
        out_specs=pl.BlockSpec((blocks, 1, kx, wide), lambda z: (0, z, 0, 0)),
        out_shape=jax.ShapeDtypeStruct((blocks, slabs, kx, wide), jnp.float32),
        name="forward_xy",
    )(rows, *table_y, *table_x)


def middle_kernel(f_ref, g_ref, h_ref, out_ref):
    slabs = f_ref.shape[1]
    depth = f_ref.shape[0] * slabs
    length = 2 * depth
    half = f_ref.shape[3] // 2
    field = [
        (f_ref[z // slabs, z % slabs, :, :half], f_ref[z // slabs, z % slabs, :, half:])
        for z in range(depth)
    ]
    even = fft(field, -1)
    odd = fft([times(v, -z, length) for z, v in enumerate(field)], -1)
    spec = [v for pair in zip(even, odd) for v in pair]
    product = []
    for k in range(length):
        re, im = spec[k]
        mre, mim = times(spec[-k % length], -k * (depth - 1), length)
        gre, gim, hre, him = g_ref[0, k], g_ref[1, k], h_ref[0, k], h_ref[1, k]
        product.append(
            (
                gre * re - gim * im + hre * mre - him * mim,
                gre * im + gim * re + hre * mim + him * mre,
            )
        )
    even = fft(product[0::2], 1)
    odd = fft(product[1::2], 1)
    for z in range(depth):
        re, im = add(even[z], times(odd[z], z, length))
        out_ref[z // slabs, z % slabs, :, :half] = re
        out_ref[z // slabs, z % slabs, :, half:] = im


def middle(field, green, image_green):
    blocks, slabs, kx, wide = field.shape
    tile = 8
    spec = pl.BlockSpec((blocks, slabs, tile, wide), lambda i: (0, 0, i, 0))
    gspec = pl.BlockSpec((*green.shape[:2], tile, green.shape[3]), lambda i: (0, 0, i, 0))
    return pl.pallas_call(
        middle_kernel,
        grid=(kx // tile,),
        in_specs=[spec, gspec, gspec],
        out_specs=spec,
        out_shape=jax.ShapeDtypeStruct(field.shape, jnp.float32),
        name="middle_z",
    )(field, green, image_green)


def inverse_x_kernel(q_ref, th_ref, tl_ref, out_ref):
    field = q_ref[:, 0].reshape(-1, q_ref.shape[3])
    rows = product3((th_ref[...], tl_ref[...]), split(turned(field)), ((1,), (0,)))
    parts = out_ref.shape[0]
    count = rows.shape[0] // parts
    for part in range(parts):
        start = part * count
        before, after = max(start - 1, 0), min(start + count, rows.shape[0] - 1)
        out_ref[part, 0, :count] = rows[start : start + count]
        out_ref[part, 0, count : count + 8] = jnp.concatenate(
            [rows[before : before + 1], rows[after : after + 1], rows[:6]], axis=0
        )


def inverse_x(field, table, parts):
    blocks, slabs, kx, wide = field.shape
    width = blocks * kx // 2
    whole = lambda a: pl.BlockSpec(a.shape, lambda z: (0,) * a.ndim)
    shape = (parts, slabs, width // parts + 8, wide)
    return pl.pallas_call(
        inverse_x_kernel,
        grid=(slabs,),
        in_specs=[pl.BlockSpec((blocks, 1, kx, wide), lambda z: (0, z, 0, 0))]
        + [whole(a) for a in table],
        out_specs=pl.BlockSpec((parts, 1, *shape[2:]), lambda z: (0, z, 0, 0)),
        out_shape=jax.ShapeDtypeStruct(shape, jnp.float32),
        name="inverse_x",
    )(field, *table)


def differences(total, me, parts, gx_ref, gy_ref):
    count, height = total.shape[0] - 8, total.shape[1]
    main = total[:count]
    row = lax.broadcasted_iota(jnp.int32, main.shape, 0)
    before = jnp.where(row == 0, total[count : count + 1], pltpu.roll(main, 1, 0))
    after = jnp.where(row == count - 1, total[count + 1 : count + 2], pltpu.roll(main, count - 1, 0))
    edge = ((row == 0) & (me == 0)) | ((row == count - 1) & (me == parts - 1))
    gx_ref[...] = (after - before) * jnp.where(edge, 1.0, 0.5)
    col = lax.broadcasted_iota(jnp.int32, main.shape, 1)
    before = jnp.where(col == 0, main, pltpu.roll(main, 1, 1))
    after = jnp.where(col == height - 1, main, pltpu.roll(main, height - 1, 1))
    gy_ref[...] = (after - before) * jnp.where((col == 0) | (col == height - 1), 1.0, 0.5)
    return main


def inverse_y_kernel(scale, parts, me_ref, s_ref, th_ref, tl_ref, pot_ref, gx_ref, gy_ref):
    me = me_ref[0]
    for z in range(s_ref.shape[1]):
        total = None
        for part in range(parts):
            term = product3(
                split(s_ref[part, z]), (th_ref[part], tl_ref[part]), ((1,), (0,))
            )
            total = term if total is None else total + term
        total = total * scale
        main = differences(total, me, parts, gx_ref.at[z], gy_ref.at[z])
        pot_ref[z] = main


def inverse_y(rows, table, me, scale):
    parts, slabs, count, _ = rows.shape
    shape = jax.ShapeDtypeStruct((slabs, count - 8, table[0].shape[2]), jnp.float32)
    vmem = pl.BlockSpec(memory_space=VMEM)
    return pl.pallas_call(
        functools.partial(inverse_y_kernel, scale, parts),
        in_specs=[pl.BlockSpec(memory_space=SMEM), vmem, vmem, vmem],
        out_specs=(vmem, vmem, vmem),
        out_shape=(shape, shape, shape),
        name="inverse_y",
    )(me, rows, *table)


def slope_z(*pot):
    slabs = len(pot)
    size, me = lax.axis_size("gz"), lax.axis_index("gz")
    below = lax.ppermute(pot[-1], "gz", [(i, i + 1) for i in range(size - 1)])
    above = lax.ppermute(pot[0], "gz", [(i + 1, i) for i in range(size - 1)])
    below = jnp.where(me == 0, pot[0], below)
    above = jnp.where(me == size - 1, pot[-1], above)
    padded = jnp.stack([below, *pot, above])
    row = lax.broadcasted_iota(jnp.int32, (slabs, 1, 1), 0)
    edge = ((row == 0) & (me == 0)) | ((row == slabs - 1) & (me == size - 1))
    return (padded[2:] - padded[:-2]) * jnp.where(edge, 1.0, 0.5)


def pieces_spec(count):
    return [pl.BlockSpec(memory_space=VMEM)] * count


def place():
    half = lax.axis_size("gz") // 2
    mine = lax.axis_index("gz")
    return jnp.stack([lax.axis_index("gx"), mine // half, mine % half]).astype(jnp.int32)


def forward_half_kernel(at_ref, *refs):
    parts = lax.axis_size("gx")
    group = lax.axis_size("gz") // 2
    me, side, member = at_ref[0], at_ref[1], at_ref[2]
    rows, refs = refs[:parts], refs[parts:]
    yh_ref, yl_ref, th_ref, tl_ref, *refs = refs
    outs, (high_ref, low_ref, res_ref) = refs[:group], refs[group:]
    table_y = (yh_ref[me], yl_ref[me])
    table_x = (th_ref[side], tl_ref[side])
    count = rows[0].shape[1]
    width = count * parts
    for z in range(rows[0].shape[0]):
        both = jnp.concatenate([r[z] for r in rows], axis=0)
        spec = product3(split(both), table_y, ((1,), (1,)))
        wide = spec.shape[1] // 2
        high, low = split(spec)
        for k in range(parts):
            start = pl.multiple_of((me ^ k) * count, count)
            for ref, value in ((high_ref, high), (low_ref, low)):
                value = value[k * count : (k + 1) * count]
                ref[z, pl.ds(start, count), :] = value
                ref[z, pl.ds(width + start, count), :wide] = -value[:, wide:]
                ref[z, pl.ds(width + start, count), wide:] = value[:, :wide]
        res = product3(table_x, (high_ref[z], low_ref[z]), ((1,), (0,)))
        res_ref[z] = res.reshape(res_ref.shape[1:])
        for k in range(group):
            outs[k][z] = res_ref[z, member ^ k]


def cost(flops, arrays):
    size = sum(math.prod(a.shape) * a.dtype.itemsize for a in arrays)
    return pl.CostEstimate(flops=flops, bytes_accessed=size, transcendentals=0)


def forward_half(at, rows, table_y, table_x, group):
    slabs, count, height = rows[0].shape
    width = count * len(rows)
    wide = table_y[0].shape[1]
    kx = width // group
    shape = jax.ShapeDtypeStruct((slabs, kx, wide), jnp.float32)
    ins = (*rows, *table_y, *table_x)
    return pl.pallas_call(
        forward_half_kernel,
        in_specs=[pl.BlockSpec(memory_space=SMEM)] + pieces_spec(len(ins)),
        out_specs=pieces_spec(group),
        out_shape=[shape] * group,
        scratch_shapes=[
            VMEM((slabs, 2 * width, wide), jnp.bfloat16),
            VMEM((slabs, 2 * width, wide), jnp.bfloat16),
            VMEM((slabs, group, kx, wide), jnp.float32),
        ],
        cost_estimate=cost(6 * slabs * width * wide * (height + 2 * width), (*ins, *[shape] * group)),
        name="forward_half",
    )(at, *ins)


def middle_half_kernel(at_ref, *refs):
    group = lax.axis_size("gz") // 2
    side, member = at_ref[1], at_ref[2]
    ins, (g_ref, h_ref), refs = refs[: 2 * group], refs[2 * group : 2 * group + 2], refs[2 * group + 2 :]
    outs, (in_ref, out_ref) = refs[: 2 * group], refs[2 * group :]
    for k in range(2 * group):
        slab = (side ^ (k // group)) * group + (member ^ (k % group))
        in_ref[slab] = ins[k][...]
    middle_kernel(in_ref, g_ref, h_ref, out_ref)
    for k in range(2 * group):
        slab = (side ^ (k // group)) * group + (member ^ (k % group))
        outs[k][...] = out_ref[slab]


def middle_half(at, field, green, image_green):
    slabs, kx, wide = field[0].shape
    tile = 8
    spec = pl.BlockSpec((slabs, tile, wide), lambda i: (0, i, 0))
    gspec = pl.BlockSpec((*green.shape[:2], tile, green.shape[3]), lambda i: (0, 0, i, 0))
    ins = (*field, green, image_green)
    shape = jax.ShapeDtypeStruct(field[0].shape, jnp.float32)
    return pl.pallas_call(
        middle_half_kernel,
        grid=(kx // tile,),
        in_specs=[pl.BlockSpec(memory_space=SMEM)] + [spec] * len(field) + [gspec, gspec],
        out_specs=[spec] * len(field),
        out_shape=[shape] * len(field),
        scratch_shapes=[VMEM((len(field), slabs, tile, wide), jnp.float32)] * 2,
        cost_estimate=cost(30000 * kx * wide, (*ins, *[shape] * len(field))),
        name="middle_half",
    )(at, *ins)


def inverse_x_half_kernel(at_ref, *refs):
    parts = lax.axis_size("gx")
    group = lax.axis_size("gz") // 2
    me, side, member = at_ref[0], at_ref[1], at_ref[2]
    ins, (th_ref, tl_ref), refs = refs[:group], refs[group : group + 2], refs[group + 2 :]
    outs, (high_ref, low_ref, res_ref) = refs[:parts], refs[parts:]
    table = (th_ref[side], tl_ref[side])
    _, kx, wide = ins[0].shape
    wide //= 2
    for z in range(ins[0].shape[0]):
        for k in range(group):
            start = pl.multiple_of((member ^ k) * kx, kx)
            for ref, value in zip((high_ref, low_ref), split(ins[k][z])):
                ref[z, pl.ds(start, kx), :] = value
                ref[z, pl.ds(group * kx + start, kx), :wide] = -value[:, wide:]
                ref[z, pl.ds(group * kx + start, kx), wide:] = value[:, :wide]
        res = product3(table, (high_ref[z], low_ref[z]), ((1,), (0,)))
        res_ref[z] = res.reshape(res_ref.shape[1:])
        for k in range(parts):
            outs[k][z] = res_ref[z, me ^ k]


def inverse_x_half(at, field, table, parts):
    slabs, kx, wide = field[0].shape
    width = len(field) * kx
    count = width // parts + 8
    shape = jax.ShapeDtypeStruct((slabs, count, wide), jnp.float32)
    ins = (*field, *table)
    return pl.pallas_call(
        inverse_x_half_kernel,
        in_specs=[pl.BlockSpec(memory_space=SMEM)] + pieces_spec(len(ins)),
        out_specs=pieces_spec(parts),
        out_shape=[shape] * parts,
        scratch_shapes=[
            VMEM((slabs, 2 * width, wide), jnp.bfloat16),
            VMEM((slabs, 2 * width, wide), jnp.bfloat16),
            VMEM((slabs, parts, count, wide), jnp.float32),
        ],
        cost_estimate=cost(12 * slabs * parts * count * width * wide, (*ins, *[shape] * parts)),
        name="inverse_x_half",
    )(at, *ins)


def rows_of(ins, th_ref, tl_ref, me, z):
    total = None
    for k, ref in enumerate(ins):
        term = product3(split(ref[z]), (th_ref[me ^ k], tl_ref[me ^ k]), ((1,), (0,)))
        total = term if total is None else total + term
    return total


def inverse_y_partial_kernel(at_ref, *refs):
    parts = lax.axis_size("gx")
    ins, (th_ref, tl_ref, out_ref) = refs[:parts], refs[parts:]
    me = at_ref[0]
    for z in range(out_ref.shape[0]):
        out_ref[z] = rows_of(ins, th_ref, tl_ref, me, z)


def inverse_y_partial(at, rows, table):
    slabs, count, wide = rows[0].shape
    shape = jax.ShapeDtypeStruct((slabs, count, table[0].shape[2]), jnp.float32)
    ins = (*rows, *table)
    return pl.pallas_call(
        inverse_y_partial_kernel,
        in_specs=[pl.BlockSpec(memory_space=SMEM)] + pieces_spec(len(ins)),
        out_specs=pl.BlockSpec(memory_space=VMEM),
        out_shape=shape,
        cost_estimate=cost(6 * slabs * count * wide * len(rows) * shape.shape[2], (*ins, shape)),
        name="inverse_y_partial",
    )(at, *ins)


def inverse_y_half_kernel(scale, at_ref, *refs):
    parts = lax.axis_size("gx")
    ins, (other_ref, th_ref, tl_ref, low_ref, high_ref, gx_ref, gy_ref) = refs[:parts], refs[parts:]
    me = at_ref[0]
    slabs = gx_ref.shape[0]
    for z in range(slabs):
        total = (rows_of(ins, th_ref, tl_ref, me, z) + other_ref[z]) * scale
        main = differences(total, me, parts, gx_ref.at[z], gy_ref.at[z])
        if z == 0:
            low_ref[...] = main
        if z == slabs - 1:
            high_ref[...] = main


def inverse_y_half(at, rows, other, table, scale):
    slabs, count, wide = rows[0].shape
    height = table[0].shape[2]
    full = jax.ShapeDtypeStruct((slabs, count - 8, height), jnp.float32)
    one = jax.ShapeDtypeStruct((count - 8, height), jnp.float32)
    ins = (*rows, other, *table)
    shapes = [one, one, full, full]
    return pl.pallas_call(
        functools.partial(inverse_y_half_kernel, scale),
        in_specs=[pl.BlockSpec(memory_space=SMEM)] + pieces_spec(len(ins)),
        out_specs=pieces_spec(4),
        out_shape=shapes,
        cost_estimate=cost(6 * slabs * count * wide * len(rows) * height, (*ins, *shapes)),
        name="inverse_y_half",
    )(at, *ins)


def swap(value, axis, mask):
    return lax.ppermute(value, axis, [(s, s ^ mask) for s in range(lax.axis_size(axis))])


def gather_rows(own):
    pieces = [own]
    for k in range(1, lax.axis_size("gx")):
        low = k & -k
        pieces.append(swap(pieces[k - low], "gx", low))
    return pieces


def exchange(pieces, axis):
    return [pieces[0]] + [swap(p, axis, k) for k, p in enumerate(pieces) if k > 0]


def halves_device(density, green, image_green):
    slabs, _, height = density.shape
    gz, gx = lax.axis_size("gz"), lax.axis_size("gx")
    group = gz // 2
    width = density.shape[1] * gx
    column = column_table(height, gx)
    ahead = [t.reshape(2, width, 2 * width) for t in forward_table(width)]
    back = half_inverse_table(width, gx)
    at = place()
    other = swap(density, "gz", group)
    field = []
    for raw in (density, other):
        pieces = forward_half(at, gather_rows(raw), column, ahead, group)
        field += exchange(pieces, "gz")
    field = middle_half(at, field, green, image_green)
    part = inverse_x_half(at, exchange(field[group:], "gz"), back, gx)
    part = inverse_y_partial(at, exchange(part, "gx"), column)
    part = swap(part, "gz", group)
    rows = inverse_x_half(at, exchange(field[:group], "gz"), back, gx)
    scale = 1.0 / (8.0 * slabs * gz * width * height)
    low, high, grad_x, grad_y = inverse_y_half(at, exchange(rows, "gx"), part, column, scale)
    return grad_x, grad_y, slope_z(low, high)


def per_device(density, green, image_green):
    slabs, _, height = density.shape
    if lax.axis_size("gz") <= 8 and slabs == 2:
        return halves_device(density, green, image_green)
    gz, gx = lax.axis_size("gz"), lax.axis_size("gx")
    width = density.shape[1] * gx
    depth = slabs * gz
    column = column_table(height, gx)
    me = lax.axis_index("gx")
    own = tuple(lax.dynamic_index_in_dim(jnp.asarray(t), me, 0, keepdims=False) for t in column)
    rows = lax.all_gather(density, "gx", axis=1, tiled=True)
    field = forward(rows, own, forward_table(width), gz)
    field = lax.all_to_all(field, "gz", split_axis=0, concat_axis=0, tiled=True)
    field = middle(field, green, image_green)
    field = lax.all_to_all(field, "gz", split_axis=0, concat_axis=0, tiled=True)
    part = inverse_x(field, inverse_table(width), gx)
    part = lax.all_to_all(part, "gx", split_axis=0, concat_axis=0, tiled=True)
    scale = 1.0 / (8.0 * depth * width * height)
    pot, grad_x, grad_y = inverse_y(part, column, me.astype(jnp.int32).reshape(1), scale)
    return grad_x, grad_y, slope_z(*pot)


def solution(mesh):
    return jax.shard_map(
        per_device,
        mesh=mesh,
        in_specs=(P("gz", "gx", None), P(None, None, "gz", "gx"), P(None, None, "gz", "gx")),
        out_specs=(P("gz", "gx", None), P("gz", "gx", None), P("gz", "gx", None)),
        check_vma=False,
    )
```

```python
import functools
import math

import jax
import jax.numpy as jnp
import numpy as np
from jax import lax
from jax.experimental import pallas as pl
from jax.experimental.pallas import tpu as pltpu
from jax.sharding import PartitionSpec as P

VMEM = pltpu.VMEM
SMEM = pltpu.SMEM
LIMIT = 16 * 2**20


def halves(table):
    high = table.astype(jnp.bfloat16)
    low = (table - high.astype(np.float64)).astype(jnp.bfloat16)
    return high, low


def split(value):
    high = value.astype(jnp.bfloat16)
    return high, (value - high.astype(jnp.float32)).astype(jnp.bfloat16)


def product3(left, right, dims):
    one = functools.partial(
        lax.dot_general, dimension_numbers=(dims, ((), ())), preferred_element_type=jnp.float32
    )
    return one(left[0], right[0]) + (one(left[1], right[0]) + one(left[0], right[1]))


def turned(value):
    wide = value.shape[1] // 2
    swapped = jnp.concatenate([-value[:, wide:], value[:, :wide]], axis=1)
    return jnp.concatenate([value, swapped], axis=0)


def angles(space, freq):
    turns = np.outer(np.arange(freq), np.arange(space)) % freq
    return turns * (2.0 * math.pi / freq)


def column_table(space, blocks):
    angle = angles(space, 2 * space).reshape(blocks, -1, space)
    return halves(np.concatenate([np.cos(angle), -np.sin(angle)], axis=1))


def forward_table(space):
    angle = angles(space, 2 * space)
    return halves(np.concatenate([np.cos(angle), -np.sin(angle)], axis=1))


def inverse_table(space):
    angle = angles(space, 2 * space).T
    return halves(np.concatenate([np.cos(angle), np.sin(angle)], axis=1))


def half_inverse_table(space, parts):
    angle = angles(space, 2 * space).T
    count = space // parts
    rows = []
    for start in range(0, space, count):
        rows += [*range(start, start + count), max(start - 1, 0), min(start + count, space - 1)]
        rows += [start] * 6
    angle = angle[np.array(rows)].reshape(len(rows), 2, space).transpose(1, 0, 2)
    return halves(np.concatenate([np.cos(angle), np.sin(angle)], axis=2))


def times(value, turns, length):
    turns %= length
    re, im = value
    if turns == 0:
        return value
    if 4 * turns == length:
        return -im, re
    if 2 * turns == length:
        return -re, -im
    if 4 * turns == 3 * length:
        return im, -re
    c = math.cos(2.0 * math.pi * turns / length)
    s = math.sin(2.0 * math.pi * turns / length)
    if 8 * turns % length == 0:
        r = math.sqrt(0.5)
        if c * s > 0:
            return math.copysign(r, c) * (re - im), math.copysign(r, c) * (re + im)
        return math.copysign(r, c) * (re + im), math.copysign(r, c) * (im - re)
    return c * re - s * im, c * im + s * re


def add(a, b):
    return a[0] + b[0], a[1] + b[1]


def sub(a, b):
    return a[0] - b[0], a[1] - b[1]


def fft(values, sign):
    count = len(values)
    if count == 1:
        return values
    even, odd = fft(values[0::2], sign), fft(values[1::2], sign)
    odd = [times(v, sign * k, count) for k, v in enumerate(odd)]
    return [add(a, b) for a, b in zip(even, odd)] + [sub(a, b) for a, b in zip(even, odd)]


def forward_kernel(x_ref, yh_ref, yl_ref, th_ref, tl_ref, out_ref):
    table_y = (yh_ref[...], yl_ref[...])
    table_x = (th_ref[...], tl_ref[...])
    spec = product3(split(x_ref[0]), table_y, ((1,), (1,)))
    both = product3(table_x, split(turned(spec)), ((1,), (0,)))
    out_ref[:, 0] = both.reshape(out_ref.shape[0], *out_ref.shape[2:])


def forward(rows, table_y, table_x, blocks):
    slabs, width, height = rows.shape
    wide = table_y[0].shape[0]
    kx = 2 * width // blocks
    whole = lambda a: pl.BlockSpec(a.shape, lambda z: (0,) * a.ndim)
    return pl.pallas_call(
        forward_kernel,
        grid=(slabs,),
        in_specs=[pl.BlockSpec((1, width, height), lambda z: (z, 0, 0))]
        + [whole(a) for a in (*table_y, *table_x)],
        out_specs=pl.BlockSpec((blocks, 1, kx, wide), lambda z: (0, z, 0, 0)),
        out_shape=jax.ShapeDtypeStruct((blocks, slabs, kx, wide), jnp.float32),
        name="forward_xy",
    )(rows, *table_y, *table_x)


def middle_kernel(f_ref, g_ref, h_ref, out_ref):
    slabs = f_ref.shape[1]
    depth = f_ref.shape[0] * slabs
    length = 2 * depth
    half = f_ref.shape[3] // 2
    field = [
        (f_ref[z // slabs, z % slabs, :, :half], f_ref[z // slabs, z % slabs, :, half:])
        for z in range(depth)
    ]
    even = fft(field, -1)
    odd = fft([times(v, -z, length) for z, v in enumerate(field)], -1)
    spec = [v for pair in zip(even, odd) for v in pair]
    product = []
    for k in range(length):
        re, im = spec[k]
        mre, mim = times(spec[-k % length], -k * (depth - 1), length)
        gre, gim, hre, him = g_ref[0, k], g_ref[1, k], h_ref[0, k], h_ref[1, k]
        product.append(
            (
                gre * re - gim * im + hre * mre - him * mim,
                gre * im + gim * re + hre * mim + him * mre,
            )
        )
    even = fft(product[0::2], 1)
    odd = fft(product[1::2], 1)
    for z in range(depth):
        re, im = add(even[z], times(odd[z], z, length))
        out_ref[z // slabs, z % slabs, :, :half] = re
        out_ref[z // slabs, z % slabs, :, half:] = im


def middle(field, green, image_green):
    blocks, slabs, kx, wide = field.shape
    tile = 8
    spec = pl.BlockSpec((blocks, slabs, tile, wide), lambda i: (0, 0, i, 0))
    gspec = pl.BlockSpec((*green.shape[:2], tile, green.shape[3]), lambda i: (0, 0, i, 0))
    return pl.pallas_call(
        middle_kernel,
        grid=(kx // tile,),
        in_specs=[spec, gspec, gspec],
        out_specs=spec,
        out_shape=jax.ShapeDtypeStruct(field.shape, jnp.float32),
        name="middle_z",
    )(field, green, image_green)


def inverse_x_kernel(q_ref, th_ref, tl_ref, out_ref):
    field = q_ref[:, 0].reshape(-1, q_ref.shape[3])
    rows = product3((th_ref[...], tl_ref[...]), split(turned(field)), ((1,), (0,)))
    parts = out_ref.shape[0]
    count = rows.shape[0] // parts
    for part in range(parts):
        start = part * count
        before, after = max(start - 1, 0), min(start + count, rows.shape[0] - 1)
        out_ref[part, 0, :count] = rows[start : start + count]
        out_ref[part, 0, count : count + 8] = jnp.concatenate(
            [rows[before : before + 1], rows[after : after + 1], rows[:6]], axis=0
        )


def inverse_x(field, table, parts):
    blocks, slabs, kx, wide = field.shape
    width = blocks * kx // 2
    whole = lambda a: pl.BlockSpec(a.shape, lambda z: (0,) * a.ndim)
    shape = (parts, slabs, width // parts + 8, wide)
    return pl.pallas_call(
        inverse_x_kernel,
        grid=(slabs,),
        in_specs=[pl.BlockSpec((blocks, 1, kx, wide), lambda z: (0, z, 0, 0))]
        + [whole(a) for a in table],
        out_specs=pl.BlockSpec((parts, 1, *shape[2:]), lambda z: (0, z, 0, 0)),
        out_shape=jax.ShapeDtypeStruct(shape, jnp.float32),
        name="inverse_x",
    )(field, *table)


def differences(total, me, parts, gx_ref, gy_ref):
    count, height = total.shape[0] - 8, total.shape[1]
    main = total[:count]
    row = lax.broadcasted_iota(jnp.int32, main.shape, 0)
    before = jnp.where(row == 0, total[count : count + 1], pltpu.roll(main, 1, 0))
    after = jnp.where(row == count - 1, total[count + 1 : count + 2], pltpu.roll(main, count - 1, 0))
    edge = ((row == 0) & (me == 0)) | ((row == count - 1) & (me == parts - 1))
    gx_ref[...] = (after - before) * jnp.where(edge, 1.0, 0.5)
    col = lax.broadcasted_iota(jnp.int32, main.shape, 1)
    before = jnp.where(col == 0, main, pltpu.roll(main, 1, 1))
    after = jnp.where(col == height - 1, main, pltpu.roll(main, height - 1, 1))
    gy_ref[...] = (after - before) * jnp.where((col == 0) | (col == height - 1), 1.0, 0.5)
    return main


def inverse_y_kernel(scale, parts, me_ref, s_ref, th_ref, tl_ref, pot_ref, gx_ref, gy_ref):
    me = me_ref[0]
    for z in range(s_ref.shape[1]):
        total = None
        for part in range(parts):
            term = product3(
                split(s_ref[part, z]), (th_ref[part], tl_ref[part]), ((1,), (0,))
            )
            total = term if total is None else total + term
        total = total * scale
        main = differences(total, me, parts, gx_ref.at[z], gy_ref.at[z])
        pot_ref[z] = main


def inverse_y(rows, table, me, scale):
    parts, slabs, count, _ = rows.shape
    shape = jax.ShapeDtypeStruct((slabs, count - 8, table[0].shape[2]), jnp.float32)
    vmem = pl.BlockSpec(memory_space=VMEM)
    return pl.pallas_call(
        functools.partial(inverse_y_kernel, scale, parts),
        in_specs=[pl.BlockSpec(memory_space=SMEM), vmem, vmem, vmem],
        out_specs=(vmem, vmem, vmem),
        out_shape=(shape, shape, shape),
        name="inverse_y",
    )(me, rows, *table)


def slope_z(*pot):
    slabs = len(pot)
    size, me = lax.axis_size("gz"), lax.axis_index("gz")
    below = lax.ppermute(pot[-1], "gz", [(i, i + 1) for i in range(size - 1)])
    above = lax.ppermute(pot[0], "gz", [(i + 1, i) for i in range(size - 1)])
    below = jnp.where(me == 0, pot[0], below)
    above = jnp.where(me == size - 1, pot[-1], above)
    padded = jnp.stack([below, *pot, above])
    row = lax.broadcasted_iota(jnp.int32, (slabs, 1, 1), 0)
    edge = ((row == 0) & (me == 0)) | ((row == slabs - 1) & (me == size - 1))
    return (padded[2:] - padded[:-2]) * jnp.where(edge, 1.0, 0.5)


def pieces_spec(count):
    return [pl.BlockSpec(memory_space=VMEM)] * count


def place():
    half = lax.axis_size("gz") // 2
    mine = lax.axis_index("gz")
    return jnp.stack([lax.axis_index("gx"), mine // half, mine % half]).astype(jnp.int32)


def forward_half_kernel(at_ref, *refs):
    parts = lax.axis_size("gx")
    group = lax.axis_size("gz") // 2
    me, side, member = at_ref[0], at_ref[1], at_ref[2]
    rows, refs = refs[:parts], refs[parts:]
    yh_ref, yl_ref, th_ref, tl_ref, *refs = refs
    outs, (high_ref, low_ref, res_ref) = refs[:group], refs[group:]
    table_y = (yh_ref[me], yl_ref[me])
    table_x = (th_ref[side], tl_ref[side])
    count = rows[0].shape[1]
    width = count * parts
    for z in range(rows[0].shape[0]):
        both = jnp.concatenate([r[z] for r in rows], axis=0)
        spec = product3(split(both), table_y, ((1,), (1,)))
        wide = spec.shape[1] // 2
        high, low = split(spec)
        for k in range(parts):
            start = pl.multiple_of((me ^ k) * count, count)
            for ref, value in ((high_ref, high), (low_ref, low)):
                value = value[k * count : (k + 1) * count]
                ref[z, pl.ds(start, count), :] = value
                ref[z, pl.ds(width + start, count), :wide] = -value[:, wide:]
                ref[z, pl.ds(width + start, count), wide:] = value[:, :wide]
        res = product3(table_x, (high_ref[z], low_ref[z]), ((1,), (0,)))
        res_ref[z] = res.reshape(res_ref.shape[1:])
        for k in range(group):
            outs[k][z] = res_ref[z, member ^ k]


def cost(flops, arrays):
    size = sum(math.prod(a.shape) * a.dtype.itemsize for a in arrays)
    return pl.CostEstimate(flops=flops, bytes_accessed=size, transcendentals=0)


def forward_half(at, rows, table_y, table_x, group):
    slabs, count, height = rows[0].shape
    width = count * len(rows)
    wide = table_y[0].shape[1]
    kx = width // group
    shape = jax.ShapeDtypeStruct((slabs, kx, wide), jnp.float32)
    ins = (*rows, *table_y, *table_x)
    return pl.pallas_call(
        forward_half_kernel,
        in_specs=[pl.BlockSpec(memory_space=SMEM)] + pieces_spec(len(ins)),
        out_specs=pieces_spec(group),
        out_shape=[shape] * group,
        scratch_shapes=[
            VMEM((slabs, 2 * width, wide), jnp.bfloat16),
            VMEM((slabs, 2 * width, wide), jnp.bfloat16),
            VMEM((slabs, group, kx, wide), jnp.float32),
        ],
        cost_estimate=cost(6 * slabs * width * wide * (height + 2 * width), (*ins, *[shape] * group)),
        compiler_params=pltpu.CompilerParams(vmem_limit_bytes=LIMIT),
        name="forward_half",
    )(at, *ins)


def middle_half_kernel(at_ref, *refs):
    group = lax.axis_size("gz") // 2
    side, member = at_ref[1], at_ref[2]
    ins, (g_ref, h_ref), refs = refs[: 2 * group], refs[2 * group : 2 * group + 2], refs[2 * group + 2 :]
    outs, (in_ref, out_ref) = refs[: 2 * group], refs[2 * group :]
    for k in range(2 * group):
        slab = (side ^ (k // group)) * group + (member ^ (k % group))
        in_ref[slab] = ins[k][...]
    middle_kernel(in_ref, g_ref, h_ref, out_ref)
    for k in range(2 * group):
        slab = (side ^ (k // group)) * group + (member ^ (k % group))
        outs[k][...] = out_ref[slab]


def middle_half(at, field, green, image_green):
    slabs, kx, wide = field[0].shape
    tile = 8
    spec = pl.BlockSpec((slabs, tile, wide), lambda i: (0, i, 0))
    gspec = pl.BlockSpec((*green.shape[:2], tile, green.shape[3]), lambda i: (0, 0, i, 0))
    ins = (*field, green, image_green)
    shape = jax.ShapeDtypeStruct(field[0].shape, jnp.float32)
    return pl.pallas_call(
        middle_half_kernel,
        grid=(kx // tile,),
        in_specs=[pl.BlockSpec(memory_space=SMEM)] + [spec] * len(field) + [gspec, gspec],
        out_specs=[spec] * len(field),
        out_shape=[shape] * len(field),
        scratch_shapes=[VMEM((len(field), slabs, tile, wide), jnp.float32)] * 2,
        cost_estimate=cost(30000 * kx * wide, (*ins, *[shape] * len(field))),
        compiler_params=pltpu.CompilerParams(vmem_limit_bytes=LIMIT),
        name="middle_half",
    )(at, *ins)


def inverse_x_half_kernel(at_ref, *refs):
    parts = lax.axis_size("gx")
    group = lax.axis_size("gz") // 2
    me, side, member = at_ref[0], at_ref[1], at_ref[2]
    ins, (th_ref, tl_ref), refs = refs[:group], refs[group : group + 2], refs[group + 2 :]
    outs, (high_ref, low_ref, res_ref) = refs[:parts], refs[parts:]
    table = (th_ref[side], tl_ref[side])
    _, kx, wide = ins[0].shape
    wide //= 2
    for z in range(ins[0].shape[0]):
        for k in range(group):
            start = pl.multiple_of((member ^ k) * kx, kx)
            for ref, value in zip((high_ref, low_ref), split(ins[k][z])):
                ref[z, pl.ds(start, kx), :] = value
                ref[z, pl.ds(group * kx + start, kx), :wide] = -value[:, wide:]
                ref[z, pl.ds(group * kx + start, kx), wide:] = value[:, :wide]
        res = product3(table, (high_ref[z], low_ref[z]), ((1,), (0,)))
        res_ref[z] = res.reshape(res_ref.shape[1:])
        for k in range(parts):
            outs[k][z] = res_ref[z, me ^ k]


def inverse_x_half(at, field, table, parts):
    slabs, kx, wide = field[0].shape
    width = len(field) * kx
    count = width // parts + 8
    shape = jax.ShapeDtypeStruct((slabs, count, wide), jnp.float32)
    ins = (*field, *table)
    return pl.pallas_call(
        inverse_x_half_kernel,
        in_specs=[pl.BlockSpec(memory_space=SMEM)] + pieces_spec(len(ins)),
        out_specs=pieces_spec(parts),
        out_shape=[shape] * parts,
        scratch_shapes=[
            VMEM((slabs, 2 * width, wide), jnp.bfloat16),
            VMEM((slabs, 2 * width, wide), jnp.bfloat16),
            VMEM((slabs, parts, count, wide), jnp.float32),
        ],
        cost_estimate=cost(12 * slabs * parts * count * width * wide, (*ins, *[shape] * parts)),
        compiler_params=pltpu.CompilerParams(vmem_limit_bytes=LIMIT),
        name="inverse_x_half",
    )(at, *ins)


def rows_of(ins, th_ref, tl_ref, me, z):
    total = None
    for k, ref in enumerate(ins):
        term = product3(split(ref[z]), (th_ref[me ^ k], tl_ref[me ^ k]), ((1,), (0,)))
        total = term if total is None else total + term
    return total


def inverse_y_partial_kernel(at_ref, *refs):
    parts = lax.axis_size("gx")
    ins, (th_ref, tl_ref, out_ref) = refs[:parts], refs[parts:]
    me = at_ref[0]
    for z in range(out_ref.shape[0]):
        out_ref[z] = rows_of(ins, th_ref, tl_ref, me, z)


def inverse_y_partial(at, rows, table):
    slabs, count, wide = rows[0].shape
    shape = jax.ShapeDtypeStruct((slabs, count, table[0].shape[2]), jnp.float32)
    ins = (*rows, *table)
    return pl.pallas_call(
        inverse_y_partial_kernel,
        in_specs=[pl.BlockSpec(memory_space=SMEM)] + pieces_spec(len(ins)),
        out_specs=pl.BlockSpec(memory_space=VMEM),
        out_shape=shape,
        cost_estimate=cost(6 * slabs * count * wide * len(rows) * shape.shape[2], (*ins, shape)),
        compiler_params=pltpu.CompilerParams(vmem_limit_bytes=LIMIT),
        name="inverse_y_partial",
    )(at, *ins)


def inverse_y_half_kernel(scale, at_ref, *refs):
    parts = lax.axis_size("gx")
    ins, (other_ref, th_ref, tl_ref, low_ref, high_ref, gx_ref, gy_ref) = refs[:parts], refs[parts:]
    me = at_ref[0]
    slabs = gx_ref.shape[0]
    for z in range(slabs):
        total = (rows_of(ins, th_ref, tl_ref, me, z) + other_ref[z]) * scale
        main = differences(total, me, parts, gx_ref.at[z], gy_ref.at[z])
        if z == 0:
            low_ref[...] = main
        if z == slabs - 1:
            high_ref[...] = main


def inverse_y_half(at, rows, other, table, scale):
    slabs, count, wide = rows[0].shape
    height = table[0].shape[2]
    full = jax.ShapeDtypeStruct((slabs, count - 8, height), jnp.float32)
    one = jax.ShapeDtypeStruct((count - 8, height), jnp.float32)
    ins = (*rows, other, *table)
    shapes = [one, one, full, full]
    return pl.pallas_call(
        functools.partial(inverse_y_half_kernel, scale),
        in_specs=[pl.BlockSpec(memory_space=SMEM)] + pieces_spec(len(ins)),
        out_specs=pieces_spec(4),
        out_shape=shapes,
        cost_estimate=cost(6 * slabs * count * wide * len(rows) * height, (*ins, *shapes)),
        compiler_params=pltpu.CompilerParams(vmem_limit_bytes=LIMIT),
        name="inverse_y_half",
    )(at, *ins)


def swap(value, axis, mask):
    return lax.ppermute(value, axis, [(s, s ^ mask) for s in range(lax.axis_size(axis))])


def gather_rows(own):
    pieces = [own]
    for k in range(1, lax.axis_size("gx")):
        low = k & -k
        pieces.append(swap(pieces[k - low], "gx", low))
    return pieces


def exchange(pieces, axis):
    return [pieces[0]] + [swap(p, axis, k) for k, p in enumerate(pieces) if k > 0]


def halves_device(density, green, image_green):
    slabs, _, height = density.shape
    gz, gx = lax.axis_size("gz"), lax.axis_size("gx")
    group = gz // 2
    width = density.shape[1] * gx
    column = column_table(height, gx)
    ahead = [t.reshape(2, width, 2 * width) for t in forward_table(width)]
    back = half_inverse_table(width, gx)
    at = place()
    other = swap(density, "gz", group)
    field = []
    for raw in (density, other):
        pieces = forward_half(at, gather_rows(raw), column, ahead, group)
        field += exchange(pieces, "gz")
    field = middle_half(at, field, green, image_green)
    part = inverse_x_half(at, exchange(field[group:], "gz"), back, gx)
    part = inverse_y_partial(at, exchange(part, "gx"), column)
    part = swap(part, "gz", group)
    rows = inverse_x_half(at, exchange(field[:group], "gz"), back, gx)
    scale = 1.0 / (8.0 * slabs * gz * width * height)
    low, high, grad_x, grad_y = inverse_y_half(at, exchange(rows, "gx"), part, column, scale)
    return grad_x, grad_y, slope_z(low, high)


def per_device(density, green, image_green):
    slabs, _, height = density.shape
    if lax.axis_size("gz") <= 8 and slabs == 2:
        return halves_device(density, green, image_green)
    gz, gx = lax.axis_size("gz"), lax.axis_size("gx")
    width = density.shape[1] * gx
    depth = slabs * gz
    column = column_table(height, gx)
    me = lax.axis_index("gx")
    own = tuple(lax.dynamic_index_in_dim(jnp.asarray(t), me, 0, keepdims=False) for t in column)
    rows = lax.all_gather(density, "gx", axis=1, tiled=True)
    field = forward(rows, own, forward_table(width), gz)
    field = lax.all_to_all(field, "gz", split_axis=0, concat_axis=0, tiled=True)
    field = middle(field, green, image_green)
    field = lax.all_to_all(field, "gz", split_axis=0, concat_axis=0, tiled=True)
    part = inverse_x(field, inverse_table(width), gx)
    part = lax.all_to_all(part, "gx", split_axis=0, concat_axis=0, tiled=True)
    scale = 1.0 / (8.0 * depth * width * height)
    pot, grad_x, grad_y = inverse_y(part, column, me.astype(jnp.int32).reshape(1), scale)
    return grad_x, grad_y, slope_z(*pot)


def solution(mesh):
    return jax.shard_map(
        per_device,
        mesh=mesh,
        in_specs=(P("gz", "gx", None), P(None, None, "gz", "gx"), P(None, None, "gz", "gx")),
        out_specs=(P("gz", "gx", None), P("gz", "gx", None), P("gz", "gx", None)),
        check_vma=False,
    )
```

```python
import functools
import math

import jax
import jax.numpy as jnp
import numpy as np
from jax import lax
from jax.experimental import pallas as pl
from jax.experimental.pallas import tpu as pltpu
from jax.sharding import PartitionSpec as P

VMEM = pltpu.VMEM
SMEM = pltpu.SMEM
LIMIT = 16 * 2**20


def halves(table):
    high = table.astype(jnp.bfloat16)
    low = (table - high.astype(np.float64)).astype(jnp.bfloat16)
    return high, low


def split(value):
    high = value.astype(jnp.bfloat16)
    return high, (value - high.astype(jnp.float32)).astype(jnp.bfloat16)


def product3(left, right, dims):
    one = functools.partial(
        lax.dot_general, dimension_numbers=(dims, ((), ())), preferred_element_type=jnp.float32
    )
    return one(left[0], right[0]) + (one(left[1], right[0]) + one(left[0], right[1]))


def turned(value):
    wide = value.shape[1] // 2
    swapped = jnp.concatenate([-value[:, wide:], value[:, :wide]], axis=1)
    return jnp.concatenate([value, swapped], axis=0)


def angles(space, freq):
    turns = np.outer(np.arange(freq), np.arange(space)) % freq
    return turns * (2.0 * math.pi / freq)


def column_table(space, blocks):
    angle = angles(space, 2 * space).reshape(blocks, -1, space)
    return halves(np.concatenate([np.cos(angle), -np.sin(angle)], axis=1))


def forward_table(space):
    angle = angles(space, 2 * space)
    return halves(np.concatenate([np.cos(angle), -np.sin(angle)], axis=1))


def inverse_table(space):
    angle = angles(space, 2 * space).T
    return halves(np.concatenate([np.cos(angle), np.sin(angle)], axis=1))


def times(value, turns, length):
    turns %= length
    re, im = value
    if turns == 0:
        return value
    if 4 * turns == length:
        return -im, re
    if 2 * turns == length:
        return -re, -im
    if 4 * turns == 3 * length:
        return im, -re
    c = math.cos(2.0 * math.pi * turns / length)
    s = math.sin(2.0 * math.pi * turns / length)
    if 8 * turns % length == 0:
        r = math.sqrt(0.5)
        if c * s > 0:
            return math.copysign(r, c) * (re - im), math.copysign(r, c) * (re + im)
        return math.copysign(r, c) * (re + im), math.copysign(r, c) * (im - re)
    return c * re - s * im, c * im + s * re


def add(a, b):
    return a[0] + b[0], a[1] + b[1]


def sub(a, b):
    return a[0] - b[0], a[1] - b[1]


def fft(values, sign):
    count = len(values)
    if count == 1:
        return values
    even, odd = fft(values[0::2], sign), fft(values[1::2], sign)
    odd = [times(v, sign * k, count) for k, v in enumerate(odd)]
    return [add(a, b) for a, b in zip(even, odd)] + [sub(a, b) for a, b in zip(even, odd)]


def forward_kernel(x_ref, yh_ref, yl_ref, th_ref, tl_ref, out_ref):
    table_y = (yh_ref[...], yl_ref[...])
    table_x = (th_ref[...], tl_ref[...])
    spec = product3(split(x_ref[0]), table_y, ((1,), (1,)))
    both = product3(table_x, split(turned(spec)), ((1,), (0,)))
    out_ref[:, 0] = both.reshape(out_ref.shape[0], *out_ref.shape[2:])


def forward(rows, table_y, table_x, blocks):
    slabs, width, height = rows.shape
    wide = table_y[0].shape[0]
    kx = 2 * width // blocks
    whole = lambda a: pl.BlockSpec(a.shape, lambda z: (0,) * a.ndim)
    return pl.pallas_call(
        forward_kernel,
        grid=(slabs,),
        in_specs=[pl.BlockSpec((1, width, height), lambda z: (z, 0, 0))]
        + [whole(a) for a in (*table_y, *table_x)],
        out_specs=pl.BlockSpec((blocks, 1, kx, wide), lambda z: (0, z, 0, 0)),
        out_shape=jax.ShapeDtypeStruct((blocks, slabs, kx, wide), jnp.float32),
        name="forward_xy",
    )(rows, *table_y, *table_x)


def through_z(field, green, image_green):
    depth = len(field)
    length = 2 * depth
    even = fft(field, -1)
    odd = fft([times(v, -z, length) for z, v in enumerate(field)], -1)
    spec = [v for pair in zip(even, odd) for v in pair]
    product = []
    for k in range(length):
        re, im = spec[k]
        mre, mim = times(spec[-k % length], -k * (depth - 1), length)
        (gre, gim), (hre, him) = green(k), image_green(k)
        product.append(
            (
                gre * re - gim * im + hre * mre - him * mim,
                gre * im + gim * re + hre * mim + him * mre,
            )
        )
    even = fft(product[0::2], 1)
    odd = fft(product[1::2], 1)
    return [add(even[z], times(odd[z], z, length)) for z in range(depth)]


def middle_kernel(f_ref, g_ref, h_ref, out_ref):
    slabs = f_ref.shape[1]
    half = f_ref.shape[3] // 2
    at = [(z // slabs, z % slabs) for z in range(f_ref.shape[0] * slabs)]
    field = [(f_ref[a, b, :, :half], f_ref[a, b, :, half:]) for a, b in at]
    both = lambda ref: lambda k: (ref[0, k], ref[1, k])
    for (a, b), (re, im) in zip(at, through_z(field, both(g_ref), both(h_ref))):
        out_ref[a, b, :, :half] = re
        out_ref[a, b, :, half:] = im


def middle(field, green, image_green):
    blocks, slabs, kx, wide = field.shape
    tile = 8
    spec = pl.BlockSpec((blocks, slabs, tile, wide), lambda i: (0, 0, i, 0))
    gspec = pl.BlockSpec((*green.shape[:2], tile, green.shape[3]), lambda i: (0, 0, i, 0))
    return pl.pallas_call(
        middle_kernel,
        grid=(kx // tile,),
        in_specs=[spec, gspec, gspec],
        out_specs=spec,
        out_shape=jax.ShapeDtypeStruct(field.shape, jnp.float32),
        name="middle_z",
    )(field, green, image_green)


def inverse_x_kernel(q_ref, th_ref, tl_ref, out_ref):
    field = q_ref[:, 0].reshape(-1, q_ref.shape[3])
    rows = product3((th_ref[...], tl_ref[...]), split(turned(field)), ((1,), (0,)))
    parts = out_ref.shape[0]
    count = rows.shape[0] // parts
    for part in range(parts):
        start = part * count
        before, after = max(start - 1, 0), min(start + count, rows.shape[0] - 1)
        out_ref[part, 0, :count] = rows[start : start + count]
        out_ref[part, 0, count : count + 8] = jnp.concatenate(
            [rows[before : before + 1], rows[after : after + 1], rows[:6]], axis=0
        )


def inverse_x(field, table, parts):
    blocks, slabs, kx, wide = field.shape
    width = blocks * kx // 2
    whole = lambda a: pl.BlockSpec(a.shape, lambda z: (0,) * a.ndim)
    shape = (parts, slabs, width // parts + 8, wide)
    return pl.pallas_call(
        inverse_x_kernel,
        grid=(slabs,),
        in_specs=[pl.BlockSpec((blocks, 1, kx, wide), lambda z: (0, z, 0, 0))]
        + [whole(a) for a in table],
        out_specs=pl.BlockSpec((parts, 1, *shape[2:]), lambda z: (0, z, 0, 0)),
        out_shape=jax.ShapeDtypeStruct(shape, jnp.float32),
        name="inverse_x",
    )(field, *table)


def differences(total, me, parts, gx_ref, gy_ref):
    count, height = total.shape[0] - 8, total.shape[1]
    main = total[:count]
    row = lax.broadcasted_iota(jnp.int32, main.shape, 0)
    before = jnp.where(row == 0, total[count : count + 1], pltpu.roll(main, 1, 0))
    after = jnp.where(row == count - 1, total[count + 1 : count + 2], pltpu.roll(main, count - 1, 0))
    edge = ((row == 0) & (me == 0)) | ((row == count - 1) & (me == parts - 1))
    gx_ref[...] = (after - before) * jnp.where(edge, 1.0, 0.5)
    col = lax.broadcasted_iota(jnp.int32, main.shape, 1)
    before = jnp.where(col == 0, main, pltpu.roll(main, 1, 1))
    after = jnp.where(col == height - 1, main, pltpu.roll(main, height - 1, 1))
    gy_ref[...] = (after - before) * jnp.where((col == 0) | (col == height - 1), 1.0, 0.5)
    return main


def inverse_y_kernel(scale, parts, me_ref, s_ref, th_ref, tl_ref, pot_ref, gx_ref, gy_ref):
    me = me_ref[0]
    for z in range(s_ref.shape[1]):
        total = None
        for part in range(parts):
            term = product3(
                split(s_ref[part, z]), (th_ref[part], tl_ref[part]), ((1,), (0,))
            )
            total = term if total is None else total + term
        total = total * scale
        main = differences(total, me, parts, gx_ref.at[z], gy_ref.at[z])
        pot_ref[z] = main


def inverse_y(rows, table, me, scale):
    parts, slabs, count, _ = rows.shape
    shape = jax.ShapeDtypeStruct((slabs, count - 8, table[0].shape[2]), jnp.float32)
    vmem = pl.BlockSpec(memory_space=VMEM)
    return pl.pallas_call(
        functools.partial(inverse_y_kernel, scale, parts),
        in_specs=[pl.BlockSpec(memory_space=SMEM), vmem, vmem, vmem],
        out_specs=(vmem, vmem, vmem),
        out_shape=(shape, shape, shape),
        name="inverse_y",
    )(me, rows, *table)


def slope_z(*pot):
    slabs = len(pot)
    size, me = lax.axis_size("gz"), lax.axis_index("gz")
    below = lax.ppermute(pot[-1], "gz", [(i, i + 1) for i in range(size - 1)])
    above = lax.ppermute(pot[0], "gz", [(i + 1, i) for i in range(size - 1)])
    below = jnp.where(me == 0, pot[0], below)
    above = jnp.where(me == size - 1, pot[-1], above)
    padded = jnp.stack([below, *pot, above])
    row = lax.broadcasted_iota(jnp.int32, (slabs, 1, 1), 0)
    edge = ((row == 0) & (me == 0)) | ((row == slabs - 1) & (me == size - 1))
    return (padded[2:] - padded[:-2]) * jnp.where(edge, 1.0, 0.5)


def pieces_spec(count):
    return [pl.BlockSpec(memory_space=VMEM)] * count


def place():
    half = lax.axis_size("gz") // 2
    mine = lax.axis_index("gz")
    return jnp.stack([lax.axis_index("gx"), mine // half, mine % half]).astype(jnp.int32)


def turn_table(space):
    rows = np.concatenate([np.arange(0, 2 * space, 8), np.arange(8)])
    angle = np.outer(rows, np.arange(space)) % (2 * space) * (math.pi / space)
    return np.concatenate([np.cos(angle), np.sin(angle)], axis=1).astype(np.float32)


def tables_kernel(space, parts, at_ref, turn_ref, density_ref, *outs):
    outs[8][...] = density_ref[...]
    me, side = at_ref[0], at_ref[1]
    coarse = 2 * space // 8
    cos, sin = turn_ref[coarse:, :space], turn_ref[coarse:, space:]
    odd = lax.broadcasted_iota(jnp.int32, cos.shape, 0) % 2 == 1
    sign = jnp.where(odd & (side == 1), -1.0, 1.0)
    flip_cos, flip_sin = cos * sign, sin * sign

    def turned_by(row, cos, sin):
        c, s = turn_ref[pl.ds(row, 1), :space], turn_ref[pl.ds(row, 1), space:]
        return c * cos - s * sin, c * sin + s * cos

    def put(pair, at, lanes, values):
        for ref, value in zip(pair, split(jnp.concatenate(values, axis=0))):
            ref[at : at + 16, lanes] = value

    every = slice(0, space)
    first, second = slice(0, space), slice(space, 2 * space)
    count = space // parts
    freq = 2 * space // parts
    for k in range(2):
        base = (me ^ k) * (freq // 8)
        pair = outs[2 * k : 2 * k + 2]
        for row in range(0, freq, 16):
            two = [turned_by(base + row // 8 + i, cos, sin) for i in range(2)]
            put(pair, row, every, [v[0] for v in two])
            put(pair, freq + row, every, [-v[1] for v in two])
    pair = outs[4:6]
    for row in range(0, space, 16):
        two = [turned_by(side * (space // 8) + row // 8 + i, cos, sin) for i in range(2)]
        put(pair, row, first, [v[0] for v in two])
        put(pair, row, second, [-v[1] for v in two])
    tiles = []
    which = lax.broadcasted_iota(jnp.int32, cos.shape, 0)
    for part in range(parts):
        start = part * count
        tiles += [turned_by(row // 8, flip_cos, flip_sin) for row in range(start, start + count, 8)]
        edge = []
        for row in (max(start - 1, 0), min(start + count, space - 1)):
            fine = row % 8
            edge.append(turned_by(row // 8, flip_cos[fine : fine + 1], flip_sin[fine : fine + 1]))
        tiles.append(tuple(jnp.where(which == 0, edge[0][i], edge[1][i]) for i in range(2)))
    for row in range(0, 8 * len(tiles), 16):
        two = tiles[row // 8 : row // 8 + 2]
        put(outs[6:8], row, first, [v[0] for v in two])
        put(outs[6:], row, second, [v[1] for v in two])


def tables(at, density, parts):
    space = density.shape[2]
    turn = turn_table(space)
    high = lambda *shape: [jax.ShapeDtypeStruct(shape, jnp.bfloat16)] * 2
    shapes = high(4 * space // parts, space) * 2 + high(space, 2 * space)
    shapes += high(space + 8 * parts, 2 * space)
    shapes += [jax.ShapeDtypeStruct(density.shape, density.dtype)]
    out = pl.pallas_call(
        functools.partial(tables_kernel, space, parts),
        in_specs=[pl.BlockSpec(memory_space=SMEM)] + pieces_spec(2),
        out_specs=pieces_spec(len(shapes)),
        out_shape=shapes,
        compiler_params=pltpu.CompilerParams(vmem_limit_bytes=LIMIT),
        cost_estimate=cost(0, (turn, *shapes)),
        name="tables",
    )(at, turn, density)
    return out[8], *[out[i : i + 2] for i in range(0, 8, 2)]


def forward_half_kernel(at_ref, *refs):
    parts = lax.axis_size("gx")
    group = lax.axis_size("gz") // 2
    me, member = at_ref[0], at_ref[2]
    rows, refs = refs[:parts], refs[parts:]
    yh_ref, yl_ref, th_ref, tl_ref, *refs = refs
    outs, (high_ref, low_ref, res_ref) = refs[:group], refs[group:]
    table_y = (yh_ref[...], yl_ref[...])
    table_x = (th_ref[...], tl_ref[...])
    count = rows[0].shape[1]
    width = count * parts
    for z in range(rows[0].shape[0]):
        both = jnp.concatenate([r[z] for r in rows], axis=0)
        spec = product3(split(both), table_y, ((1,), (1,)))
        wide = spec.shape[1] // 2
        high, low = split(spec)
        for k in range(parts):
            start = pl.multiple_of((me ^ k) * count, count)
            for ref, value in ((high_ref, high), (low_ref, low)):
                value = value[k * count : (k + 1) * count]
                ref[z, pl.ds(start, count), :] = value
                ref[z, pl.ds(width + start, count), :wide] = -value[:, wide:]
                ref[z, pl.ds(width + start, count), wide:] = value[:, :wide]
        res = product3(table_x, (high_ref[z], low_ref[z]), ((1,), (0,)))
        res_ref[z] = res.reshape(res_ref.shape[1:])
        for k in range(group):
            outs[k][z] = res_ref[z, member ^ k]


def cost(flops, arrays):
    size = sum(math.prod(a.shape) * a.dtype.itemsize for a in arrays)
    return pl.CostEstimate(flops=flops, bytes_accessed=size, transcendentals=0)


def forward_half(at, rows, table_y, table_x, group):
    slabs, count, height = rows[0].shape
    width = count * len(rows)
    wide = table_y[0].shape[0]
    kx = width // group
    shape = jax.ShapeDtypeStruct((slabs, kx, wide), jnp.float32)
    ins = (*rows, *table_y, *table_x)
    return pl.pallas_call(
        forward_half_kernel,
        in_specs=[pl.BlockSpec(memory_space=SMEM)] + pieces_spec(len(ins)),
        out_specs=pieces_spec(group),
        out_shape=[shape] * group,
        scratch_shapes=[
            VMEM((slabs, 2 * width, wide), jnp.bfloat16),
            VMEM((slabs, 2 * width, wide), jnp.bfloat16),
            VMEM((slabs, group, kx, wide), jnp.float32),
        ],
        cost_estimate=cost(6 * slabs * width * wide * (height + 2 * width), (*ins, *[shape] * group)),
        compiler_params=pltpu.CompilerParams(vmem_limit_bytes=LIMIT),
        name="forward_half",
    )(at, *ins)


def middle_half_kernel(at_ref, *refs):
    group = lax.axis_size("gz") // 2
    side, member = at_ref[1], at_ref[2]
    ins, (g_ref, h_ref), refs = refs[: 2 * group], refs[2 * group : 2 * group + 2], refs[2 * group + 2 :]
    outs, (in_ref, out_ref) = refs[: 2 * group], refs[2 * group :]
    slabs, kx, wide = ins[0].shape
    half = wide // 2
    place = [(side ^ (k // group)) * group + (member ^ (k % group)) for k in range(2 * group)]
    at = [(z // slabs, z % slabs) for z in range(2 * group * slabs)]

    def tile(i, carry):
        rows = pl.ds(pl.multiple_of(8 * i, 8), 8)
        for k, slab in enumerate(place):
            in_ref[slab] = ins[k][:, rows, :]
        field = [(in_ref[a, b, :, :half], in_ref[a, b, :, half:]) for a, b in at]
        both = lambda ref: lambda k: (ref[0, k, rows, :], ref[1, k, rows, :])
        for (a, b), (re, im) in zip(at, through_z(field, both(g_ref), both(h_ref))):
            out_ref[a, b, :, :half] = re
            out_ref[a, b, :, half:] = im
        for k, slab in enumerate(place):
            outs[k][:, rows, :] = out_ref[slab]
        return carry

    lax.fori_loop(0, kx // 8, tile, 0)


def middle_half(at, field, green, image_green):
    slabs, kx, wide = field[0].shape
    ins = (*field, green, image_green)
    shape = jax.ShapeDtypeStruct(field[0].shape, jnp.float32)
    return pl.pallas_call(
        middle_half_kernel,
        in_specs=[pl.BlockSpec(memory_space=SMEM)] + pieces_spec(len(ins)),
        out_specs=pieces_spec(len(field)),
        out_shape=[shape] * len(field),
        scratch_shapes=[VMEM((len(field), slabs, 8, wide), jnp.float32)] * 2,
        cost_estimate=cost(0, (*ins, *[shape] * len(field))),
        compiler_params=pltpu.CompilerParams(vmem_limit_bytes=LIMIT),
        name="middle_half",
    )(at, *ins)


def inverse_x_half_kernel(at_ref, *refs):
    parts = lax.axis_size("gx")
    group = lax.axis_size("gz") // 2
    me, member = at_ref[0], at_ref[2]
    ins, (th_ref, tl_ref), refs = refs[:group], refs[group : group + 2], refs[group + 2 :]
    outs, (high_ref, low_ref, res_ref) = refs[:2], refs[2:]
    table = (th_ref[...], tl_ref[...])
    _, kx, wide = ins[0].shape
    wide //= 2
    for z in range(ins[0].shape[0]):
        for k in range(group):
            start = pl.multiple_of((member ^ k) * kx, kx)
            for ref, value in zip((high_ref, low_ref), split(ins[k][z])):
                ref[z, pl.ds(start, kx), :] = value
                ref[z, pl.ds(group * kx + start, kx), :wide] = -value[:, wide:]
                ref[z, pl.ds(group * kx + start, kx), wide:] = value[:, :wide]
        res = product3(table, (high_ref[z], low_ref[z]), ((1,), (0,)))
        res_ref[z] = res.reshape(res_ref.shape[1:])
        for k in range(parts):
            outs[k % 2][k // 2, z] = res_ref[z, me ^ k]


def inverse_x_half(at, field, table, parts):
    slabs, kx, wide = field[0].shape
    width = len(field) * kx
    count = width // parts + 8
    shape = jax.ShapeDtypeStruct((parts // 2, slabs, count, wide), jnp.float32)
    ins = (*field, *table)
    return pl.pallas_call(
        inverse_x_half_kernel,
        in_specs=[pl.BlockSpec(memory_space=SMEM)] + pieces_spec(len(ins)),
        out_specs=pieces_spec(2),
        out_shape=[shape] * 2,
        scratch_shapes=[
            VMEM((slabs, 2 * width, wide), jnp.bfloat16),
            VMEM((slabs, 2 * width, wide), jnp.bfloat16),
            VMEM((slabs, parts, count, wide), jnp.float32),
        ],
        cost_estimate=cost(12 * slabs * parts * count * width * wide, (*ins, *[shape] * 2)),
        compiler_params=pltpu.CompilerParams(vmem_limit_bytes=LIMIT),
        name="inverse_x_half",
    )(at, *ins)


def inverse_y_partial_kernel(keep_ref, near_ref, *refs):
    outs = refs[4:]
    total = None
    for k, ref in enumerate((keep_ref, near_ref)):
        rows = ref[...].reshape(-1, ref.shape[3])
        table = (refs[2 * k][...], refs[2 * k + 1][...])
        term = product3(split(rows), table, ((1,), (0,)))
        total = term if total is None else total + term
    total = total.reshape(len(outs), *outs[0].shape)
    for k, ref in enumerate(outs):
        ref[...] = total[k]


def inverse_y_partial(keep, near, table):
    chips, slabs, count, wide = keep.shape
    shape = jax.ShapeDtypeStruct((slabs, count, table[0].shape[1]), jnp.float32)
    ins = (keep, near, *table)
    return pl.pallas_call(
        inverse_y_partial_kernel,
        in_specs=pieces_spec(len(ins)),
        out_specs=pieces_spec(chips),
        out_shape=[shape] * chips,
        cost_estimate=cost(12 * chips * slabs * count * wide * shape.shape[2], (*ins, *[shape] * chips)),
        compiler_params=pltpu.CompilerParams(vmem_limit_bytes=LIMIT),
        name="inverse_y_partial",
    )(*ins)


def combine_kernel(scale, at_ref, mine_ref, near_ref, other_ref, first_ref, second_ref, rows_ref):
    odd = at_ref[2] % 2 == 1
    count = first_ref.shape[0]
    low = ((mine_ref[0] + near_ref[0]) + other_ref[0]) * scale
    high = ((mine_ref[1] + near_ref[1]) + other_ref[1]) * scale
    first_ref[...] = jnp.where(odd, low[:count], high[:count])
    second_ref[...] = jnp.where(odd, high[:count], low[:count])
    rows_ref[0] = low[count:]
    rows_ref[1] = high[count:]


def combine(at, mine, near, other, scale):
    slabs, count, height = mine.shape
    one = jax.ShapeDtypeStruct((count - 8, height), jnp.float32)
    shapes = [one, one, jax.ShapeDtypeStruct((slabs, 8, height), jnp.float32)]
    return pl.pallas_call(
        functools.partial(combine_kernel, scale),
        in_specs=[pl.BlockSpec(memory_space=SMEM)] + pieces_spec(3),
        out_specs=pieces_spec(3),
        out_shape=shapes,
        compiler_params=pltpu.CompilerParams(vmem_limit_bytes=LIMIT),
        cost_estimate=cost(0, (mine, near, other, *shapes)),
        name="combine",
    )(at, mine, near, other)


def slopes_kernel(at_ref, first_ref, second_ref, rows_ref, gx_ref, gy_ref):
    parts = lax.axis_size("gx")
    odd = at_ref[2] % 2 == 1
    first, second = first_ref[...], second_ref[...]
    for z, main in enumerate((jnp.where(odd, first, second), jnp.where(odd, second, first))):
        total = jnp.concatenate([main, rows_ref[z]], axis=0)
        differences(total, at_ref[0], parts, gx_ref.at[z], gy_ref.at[z])


def slopes(at, first, second, rows):
    shape = jax.ShapeDtypeStruct((2, *first.shape), jnp.float32)
    return pl.pallas_call(
        slopes_kernel,
        in_specs=[pl.BlockSpec(memory_space=SMEM)] + pieces_spec(3),
        out_specs=pieces_spec(2),
        out_shape=[shape, shape],
        compiler_params=pltpu.CompilerParams(vmem_limit_bytes=LIMIT),
        cost_estimate=cost(0, (first, second, rows, shape, shape)),
        name="slopes",
    )(at, first, second, rows)


def slope_z_pairs(first, second):
    size, mine = lax.axis_size("gz"), lax.axis_index("gz")
    odd, start, end = mine % 2 == 1, mine == 0, mine == size - 1
    near = swap(first, "gz", 1)
    pairs = [(i, i + 1) for i in range(1, size - 1, 2)]
    far = lax.ppermute(second, "gz", pairs + [(b, a) for a, b in pairs])
    low, high = jnp.where(odd, first, second), jnp.where(odd, second, first)
    below, above = jnp.where(odd, near, far), jnp.where(odd, far, near)
    bottom = (high - jnp.where(start, low, below)) * jnp.where(start, 1.0, 0.5)
    top = (jnp.where(end, high, above) - low) * jnp.where(end, 1.0, 0.5)
    return jnp.stack([bottom, top])


def swap(value, axis, mask):
    return lax.ppermute(value, axis, [(s, s ^ mask) for s in range(lax.axis_size(axis))])


def exchange(pieces, axis):
    return [pieces[0]] + [swap(p, axis, k) for k, p in enumerate(pieces) if k > 0]


def after(value, *others):
    return lax.optimization_barrier((value, others))[0]


def halves_device(density, green, image_green):
    slabs, _, height = density.shape
    gz, gx = lax.axis_size("gz"), lax.axis_size("gx")
    group = gz // 2
    width = density.shape[1] * gx
    at = place()
    other = swap(density, "gz", group)
    raw = exchange([density] * gx, "gx")
    local, near_y, far_y, ahead, back = tables(at, density, gx)
    other = after(other, near_y)
    low, high = swap(other, "gx", 1), swap(other, "gx", 2)
    field = forward_half(at, [local, *raw[1:]], near_y, ahead, group)
    raw = [other, low, high, swap(after(high, field), "gx", 1)]
    field = exchange(field, "gz")
    field += exchange(forward_half(at, raw, near_y, ahead, group), "gz")
    field = middle_half(at, field, green, image_green)
    own, far = field[:group], field[group:]
    column = (*near_y, *far_y)
    keep, give = inverse_x_half(at, exchange(far, "gz"), back, gx)
    own = exchange(after(own, give), "gz")
    part, give = inverse_y_partial(keep, swap(give, "gx", 1), column)
    part = part + swap(give, "gx", 2)
    own = after(own, part)
    keep, give = inverse_x_half(at, own, back, gx)
    keep = after(keep, part)
    part = swap(part, "gz", group)
    mine, give = inverse_y_partial(keep, swap(give, "gx", 1), column)
    scale = 1.0 / (8.0 * slabs * gz * width * height)
    first, second, rows = combine(at, mine, swap(give, "gx", 2), part, scale)
    grad_z = slope_z_pairs(first, second)
    return *slopes(at, first, second, rows), grad_z


def per_device(density, green, image_green):
    slabs, count, height = density.shape
    width = count * lax.axis_size("gx")
    if lax.axis_size("gz") == 8 and lax.axis_size("gx") == 4 and slabs == 2 and width == height:
        return halves_device(density, green, image_green)
    gz, gx = lax.axis_size("gz"), lax.axis_size("gx")
    depth = slabs * gz
    column = column_table(height, gx)
    me = lax.axis_index("gx")
    own = tuple(lax.dynamic_index_in_dim(jnp.asarray(t), me, 0, keepdims=False) for t in column)
    rows = lax.all_gather(density, "gx", axis=1, tiled=True)
    field = forward(rows, own, forward_table(width), gz)
    field = lax.all_to_all(field, "gz", split_axis=0, concat_axis=0, tiled=True)
    field = middle(field, green, image_green)
    field = lax.all_to_all(field, "gz", split_axis=0, concat_axis=0, tiled=True)
    part = inverse_x(field, inverse_table(width), gx)
    part = lax.all_to_all(part, "gx", split_axis=0, concat_axis=0, tiled=True)
    scale = 1.0 / (8.0 * depth * width * height)
    pot, grad_x, grad_y = inverse_y(part, column, me.astype(jnp.int32).reshape(1), scale)
    return grad_x, grad_y, slope_z(*pot)


def solution(mesh):
    return jax.shard_map(
        per_device,
        mesh=mesh,
        in_specs=(P("gz", "gx", None), P(None, None, "gz", "gx"), P(None, None, "gz", "gx")),
        out_specs=(P("gz", "gx", None), P("gz", "gx", None), P("gz", "gx", None)),
        check_vma=False,
    )
```

```python
import functools
import math

import jax
import jax.numpy as jnp
import numpy as np
from jax import lax
from jax.experimental import pallas as pl
from jax.experimental.pallas import tpu as pltpu
from jax.sharding import PartitionSpec as P

VMEM = pltpu.VMEM
SMEM = pltpu.SMEM
LIMIT = 16 * 2**20


def halves(table):
    high = table.astype(jnp.bfloat16)
    low = (table - high.astype(np.float64)).astype(jnp.bfloat16)
    return high, low


def split(value):
    high = value.astype(jnp.bfloat16)
    return high, (value - high.astype(jnp.float32)).astype(jnp.bfloat16)


def product3(left, right, dims):
    one = functools.partial(
        lax.dot_general, dimension_numbers=(dims, ((), ())), preferred_element_type=jnp.float32
    )
    return one(left[0], right[0]) + (one(left[1], right[0]) + one(left[0], right[1]))


def turned(value):
    wide = value.shape[1] // 2
    swapped = jnp.concatenate([-value[:, wide:], value[:, :wide]], axis=1)
    return jnp.concatenate([value, swapped], axis=0)


def angles(space, freq):
    turns = np.outer(np.arange(freq), np.arange(space)) % freq
    return turns * (2.0 * math.pi / freq)


def column_table(space, blocks):
    angle = angles(space, 2 * space).reshape(blocks, -1, space)
    return halves(np.concatenate([np.cos(angle), -np.sin(angle)], axis=1))


def forward_table(space):
    angle = angles(space, 2 * space)
    return halves(np.concatenate([np.cos(angle), -np.sin(angle)], axis=1))


def inverse_table(space):
    angle = angles(space, 2 * space).T
    return halves(np.concatenate([np.cos(angle), np.sin(angle)], axis=1))


def times(value, turns, length):
    turns %= length
    re, im = value
    if turns == 0:
        return value
    if 4 * turns == length:
        return -im, re
    if 2 * turns == length:
        return -re, -im
    if 4 * turns == 3 * length:
        return im, -re
    c = math.cos(2.0 * math.pi * turns / length)
    s = math.sin(2.0 * math.pi * turns / length)
    if 8 * turns % length == 0:
        r = math.sqrt(0.5)
        if c * s > 0:
            return math.copysign(r, c) * (re - im), math.copysign(r, c) * (re + im)
        return math.copysign(r, c) * (re + im), math.copysign(r, c) * (im - re)
    return c * re - s * im, c * im + s * re


def add(a, b):
    return a[0] + b[0], a[1] + b[1]


def sub(a, b):
    return a[0] - b[0], a[1] - b[1]


def fft(values, sign):
    count = len(values)
    if count == 1:
        return values
    even, odd = fft(values[0::2], sign), fft(values[1::2], sign)
    odd = [times(v, sign * k, count) for k, v in enumerate(odd)]
    return [add(a, b) for a, b in zip(even, odd)] + [sub(a, b) for a, b in zip(even, odd)]


def forward_kernel(x_ref, yh_ref, yl_ref, th_ref, tl_ref, out_ref):
    table_y = (yh_ref[...], yl_ref[...])
    table_x = (th_ref[...], tl_ref[...])
    spec = product3(split(x_ref[0]), table_y, ((1,), (1,)))
    both = product3(table_x, split(turned(spec)), ((1,), (0,)))
    out_ref[:, 0] = both.reshape(out_ref.shape[0], *out_ref.shape[2:])


def forward(rows, table_y, table_x, blocks):
    slabs, width, height = rows.shape
    wide = table_y[0].shape[0]
    kx = 2 * width // blocks
    whole = lambda a: pl.BlockSpec(a.shape, lambda z: (0,) * a.ndim)
    return pl.pallas_call(
        forward_kernel,
        grid=(slabs,),
        in_specs=[pl.BlockSpec((1, width, height), lambda z: (z, 0, 0))]
        + [whole(a) for a in (*table_y, *table_x)],
        out_specs=pl.BlockSpec((blocks, 1, kx, wide), lambda z: (0, z, 0, 0)),
        out_shape=jax.ShapeDtypeStruct((blocks, slabs, kx, wide), jnp.float32),
        name="forward_xy",
    )(rows, *table_y, *table_x)


def through_z(field, green, image_green):
    depth = len(field)
    length = 2 * depth
    even = fft(field, -1)
    odd = fft([times(v, -z, length) for z, v in enumerate(field)], -1)
    spec = [v for pair in zip(even, odd) for v in pair]
    product = []
    for k in range(length):
        re, im = spec[k]
        mre, mim = times(spec[-k % length], -k * (depth - 1), length)
        (gre, gim), (hre, him) = green(k), image_green(k)
        product.append(
            (
                gre * re - gim * im + hre * mre - him * mim,
                gre * im + gim * re + hre * mim + him * mre,
            )
        )
    even = fft(product[0::2], 1)
    odd = fft(product[1::2], 1)
    return [add(even[z], times(odd[z], z, length)) for z in range(depth)]


def middle_kernel(f_ref, g_ref, h_ref, out_ref):
    slabs = f_ref.shape[1]
    half = f_ref.shape[3] // 2
    at = [(z // slabs, z % slabs) for z in range(f_ref.shape[0] * slabs)]
    field = [(f_ref[a, b, :, :half], f_ref[a, b, :, half:]) for a, b in at]
    both = lambda ref: lambda k: (ref[0, k], ref[1, k])
    for (a, b), (re, im) in zip(at, through_z(field, both(g_ref), both(h_ref))):
        out_ref[a, b, :, :half] = re
        out_ref[a, b, :, half:] = im


def middle(field, green, image_green):
    blocks, slabs, kx, wide = field.shape
    tile = 8
    spec = pl.BlockSpec((blocks, slabs, tile, wide), lambda i: (0, 0, i, 0))
    gspec = pl.BlockSpec((*green.shape[:2], tile, green.shape[3]), lambda i: (0, 0, i, 0))
    return pl.pallas_call(
        middle_kernel,
        grid=(kx // tile,),
        in_specs=[spec, gspec, gspec],
        out_specs=spec,
        out_shape=jax.ShapeDtypeStruct(field.shape, jnp.float32),
        name="middle_z",
    )(field, green, image_green)


def inverse_x_kernel(q_ref, th_ref, tl_ref, out_ref):
    field = q_ref[:, 0].reshape(-1, q_ref.shape[3])
    rows = product3((th_ref[...], tl_ref[...]), split(turned(field)), ((1,), (0,)))
    parts = out_ref.shape[0]
    count = rows.shape[0] // parts
    for part in range(parts):
        start = part * count
        before, after = max(start - 1, 0), min(start + count, rows.shape[0] - 1)
        out_ref[part, 0, :count] = rows[start : start + count]
        out_ref[part, 0, count : count + 8] = jnp.concatenate(
            [rows[before : before + 1], rows[after : after + 1], rows[:6]], axis=0
        )


def inverse_x(field, table, parts):
    blocks, slabs, kx, wide = field.shape
    width = blocks * kx // 2
    whole = lambda a: pl.BlockSpec(a.shape, lambda z: (0,) * a.ndim)
    shape = (parts, slabs, width // parts + 8, wide)
    return pl.pallas_call(
        inverse_x_kernel,
        grid=(slabs,),
        in_specs=[pl.BlockSpec((blocks, 1, kx, wide), lambda z: (0, z, 0, 0))]
        + [whole(a) for a in table],
        out_specs=pl.BlockSpec((parts, 1, *shape[2:]), lambda z: (0, z, 0, 0)),
        out_shape=jax.ShapeDtypeStruct(shape, jnp.float32),
        name="inverse_x",
    )(field, *table)


def differences(total, me, parts, gx_ref, gy_ref):
    count, height = total.shape[0] - 8, total.shape[1]
    main = total[:count]
    row = lax.broadcasted_iota(jnp.int32, main.shape, 0)
    before = jnp.where(row == 0, total[count : count + 1], pltpu.roll(main, 1, 0))
    after = jnp.where(row == count - 1, total[count + 1 : count + 2], pltpu.roll(main, count - 1, 0))
    edge = ((row == 0) & (me == 0)) | ((row == count - 1) & (me == parts - 1))
    gx_ref[...] = (after - before) * jnp.where(edge, 1.0, 0.5)
    col = lax.broadcasted_iota(jnp.int32, main.shape, 1)
    before = jnp.where(col == 0, main, pltpu.roll(main, 1, 1))
    after = jnp.where(col == height - 1, main, pltpu.roll(main, height - 1, 1))
    gy_ref[...] = (after - before) * jnp.where((col == 0) | (col == height - 1), 1.0, 0.5)
    return main


def inverse_y_kernel(scale, parts, me_ref, s_ref, th_ref, tl_ref, pot_ref, gx_ref, gy_ref):
    me = me_ref[0]
    for z in range(s_ref.shape[1]):
        total = None
        for part in range(parts):
            term = product3(
                split(s_ref[part, z]), (th_ref[part], tl_ref[part]), ((1,), (0,))
            )
            total = term if total is None else total + term
        total = total * scale
        main = differences(total, me, parts, gx_ref.at[z], gy_ref.at[z])
        pot_ref[z] = main


def inverse_y(rows, table, me, scale):
    parts, slabs, count, _ = rows.shape
    shape = jax.ShapeDtypeStruct((slabs, count - 8, table[0].shape[2]), jnp.float32)
    vmem = pl.BlockSpec(memory_space=VMEM)
    return pl.pallas_call(
        functools.partial(inverse_y_kernel, scale, parts),
        in_specs=[pl.BlockSpec(memory_space=SMEM), vmem, vmem, vmem],
        out_specs=(vmem, vmem, vmem),
        out_shape=(shape, shape, shape),
        name="inverse_y",
    )(me, rows, *table)


def slope_z(*pot):
    slabs = len(pot)
    size, me = lax.axis_size("gz"), lax.axis_index("gz")
    below = lax.ppermute(pot[-1], "gz", [(i, i + 1) for i in range(size - 1)])
    above = lax.ppermute(pot[0], "gz", [(i + 1, i) for i in range(size - 1)])
    below = jnp.where(me == 0, pot[0], below)
    above = jnp.where(me == size - 1, pot[-1], above)
    padded = jnp.stack([below, *pot, above])
    row = lax.broadcasted_iota(jnp.int32, (slabs, 1, 1), 0)
    edge = ((row == 0) & (me == 0)) | ((row == slabs - 1) & (me == size - 1))
    return (padded[2:] - padded[:-2]) * jnp.where(edge, 1.0, 0.5)


def pieces_spec(count):
    return [pl.BlockSpec(memory_space=VMEM)] * count


def place():
    half = lax.axis_size("gz") // 2
    mine = lax.axis_index("gz")
    return jnp.stack([lax.axis_index("gx"), mine // half, mine % half]).astype(jnp.int32)


def turn_table(space):
    rows = np.concatenate([np.arange(0, 2 * space, 8), np.arange(8)])
    angle = np.outer(rows, np.arange(space)) % (2 * space) * (math.pi / space)
    return np.concatenate([np.cos(angle), np.sin(angle)], axis=1).astype(np.float32)


def tables_kernel(space, parts, at_ref, turn_ref, density_ref, *outs):
    outs[8][...] = density_ref[...]
    me, side = at_ref[0], at_ref[1]
    coarse = 2 * space // 8
    cos, sin = turn_ref[coarse:, :space], turn_ref[coarse:, space:]
    odd = lax.broadcasted_iota(jnp.int32, cos.shape, 0) % 2 == 1
    sign = jnp.where(odd & (side == 1), -1.0, 1.0)
    flip_cos, flip_sin = cos * sign, sin * sign

    def turned_by(row, cos, sin):
        c, s = turn_ref[pl.ds(row, 1), :space], turn_ref[pl.ds(row, 1), space:]
        return c * cos - s * sin, c * sin + s * cos

    def put(pair, at, lanes, values):
        for ref, value in zip(pair, split(jnp.concatenate(values, axis=0))):
            ref[at : at + 16, lanes] = value

    every = slice(0, space)
    first, second = slice(0, space), slice(space, 2 * space)
    count = space // parts
    freq = 2 * space // parts
    for k in range(2):
        base = (me ^ k) * (freq // 8)
        pair = outs[2 * k : 2 * k + 2]
        for row in range(0, freq, 16):
            two = [turned_by(base + row // 8 + i, cos, sin) for i in range(2)]
            put(pair, row, every, [v[0] for v in two])
            put(pair, freq + row, every, [-v[1] for v in two])
    pair = outs[4:6]
    for row in range(0, space, 16):
        two = [turned_by(side * (space // 8) + row // 8 + i, cos, sin) for i in range(2)]
        put(pair, row, first, [v[0] for v in two])
        put(pair, row, second, [-v[1] for v in two])
    tiles = []
    which = lax.broadcasted_iota(jnp.int32, cos.shape, 0)
    for part in range(parts):
        start = part * count
        tiles += [turned_by(row // 8, flip_cos, flip_sin) for row in range(start, start + count, 8)]
        edge = []
        for row in (max(start - 1, 0), min(start + count, space - 1)):
            fine = row % 8
            edge.append(turned_by(row // 8, flip_cos[fine : fine + 1], flip_sin[fine : fine + 1]))
        tiles.append(tuple(jnp.where(which == 0, edge[0][i], edge[1][i]) for i in range(2)))
    for row in range(0, 8 * len(tiles), 16):
        two = tiles[row // 8 : row // 8 + 2]
        put(outs[6:8], row, first, [v[0] for v in two])
        put(outs[6:], row, second, [v[1] for v in two])


def tables(at, density, parts):
    space = density.shape[2]
    turn = turn_table(space)
    high = lambda *shape: [jax.ShapeDtypeStruct(shape, jnp.bfloat16)] * 2
    shapes = high(4 * space // parts, space) * 2 + high(space, 2 * space)
    shapes += high(space + 8 * parts, 2 * space)
    shapes += [jax.ShapeDtypeStruct(density.shape, density.dtype)]
    out = pl.pallas_call(
        functools.partial(tables_kernel, space, parts),
        in_specs=[pl.BlockSpec(memory_space=SMEM)] + pieces_spec(2),
        out_specs=pieces_spec(len(shapes)),
        out_shape=shapes,
        compiler_params=pltpu.CompilerParams(vmem_limit_bytes=LIMIT),
        cost_estimate=cost(0, (turn, *shapes)),
        name="tables",
    )(at, turn, density)
    return out[8], *[out[i : i + 2] for i in range(0, 8, 2)]


def forward_half_kernel(at_ref, *refs):
    parts = lax.axis_size("gx")
    group = lax.axis_size("gz") // 2
    me, member = at_ref[0], at_ref[2]
    rows, refs = refs[:parts], refs[parts:]
    yh_ref, yl_ref, th_ref, tl_ref, *refs = refs
    outs, (high_ref, low_ref, res_ref) = refs[:group], refs[group:]
    table_y = (yh_ref[...], yl_ref[...])
    table_x = (th_ref[...], tl_ref[...])
    count = rows[0].shape[1]
    width = count * parts
    for z in range(rows[0].shape[0]):
        both = jnp.concatenate([r[z] for r in rows], axis=0)
        spec = product3(split(both), table_y, ((1,), (1,)))
        wide = spec.shape[1] // 2
        high, low = split(spec)
        for k in range(parts):
            start = pl.multiple_of((me ^ k) * count, count)
            for ref, value in ((high_ref, high), (low_ref, low)):
                value = value[k * count : (k + 1) * count]
                ref[z, pl.ds(start, count), :] = value
                ref[z, pl.ds(width + start, count), :wide] = -value[:, wide:]
                ref[z, pl.ds(width + start, count), wide:] = value[:, :wide]
        res = product3(table_x, (high_ref[z], low_ref[z]), ((1,), (0,)))
        res_ref[z] = res.reshape(res_ref.shape[1:])
        for k in range(group):
            outs[k][z] = res_ref[z, member ^ k]


def cost(flops, arrays):
    size = sum(math.prod(a.shape) * a.dtype.itemsize for a in arrays)
    return pl.CostEstimate(flops=flops, bytes_accessed=size, transcendentals=0)


def forward_half(at, rows, table_y, table_x, group):
    slabs, count, height = rows[0].shape
    width = count * len(rows)
    wide = table_y[0].shape[0]
    kx = width // group
    shape = jax.ShapeDtypeStruct((slabs, kx, wide), jnp.float32)
    ins = (*rows, *table_y, *table_x)
    return pl.pallas_call(
        forward_half_kernel,
        in_specs=[pl.BlockSpec(memory_space=SMEM)] + pieces_spec(len(ins)),
        out_specs=pieces_spec(group),
        out_shape=[shape] * group,
        scratch_shapes=[
            VMEM((slabs, 2 * width, wide), jnp.bfloat16),
            VMEM((slabs, 2 * width, wide), jnp.bfloat16),
            VMEM((slabs, group, kx, wide), jnp.float32),
        ],
        cost_estimate=cost(6 * slabs * width * wide * (height + 2 * width), (*ins, *[shape] * group)),
        compiler_params=pltpu.CompilerParams(vmem_limit_bytes=LIMIT),
        name="forward_half",
    )(at, *ins)


def middle_half_kernel(at_ref, *refs):
    group = lax.axis_size("gz") // 2
    side, member = at_ref[1], at_ref[2]
    ins, (g_ref, h_ref), refs = refs[: 2 * group], refs[2 * group : 2 * group + 2], refs[2 * group + 2 :]
    outs, (in_ref, out_ref) = refs[: 2 * group], refs[2 * group :]
    slabs, kx, wide = ins[0].shape
    half = wide // 2
    place = [(side ^ (k // group)) * group + (member ^ (k % group)) for k in range(2 * group)]
    at = [(z // slabs, z % slabs) for z in range(2 * group * slabs)]

    def tile(i, carry):
        rows = pl.ds(pl.multiple_of(8 * i, 8), 8)
        for k, slab in enumerate(place):
            in_ref[slab] = ins[k][:, rows, :]
        field = [(in_ref[a, b, :, :half], in_ref[a, b, :, half:]) for a, b in at]
        both = lambda ref: lambda k: (ref[0, k, rows, :], ref[1, k, rows, :])
        for (a, b), (re, im) in zip(at, through_z(field, both(g_ref), both(h_ref))):
            out_ref[a, b, :, :half] = re
            out_ref[a, b, :, half:] = im
        for k, slab in enumerate(place):
            outs[k][:, rows, :] = out_ref[slab]
        return carry

    lax.fori_loop(0, kx // 8, tile, 0)


def middle_half(at, field, green, image_green):
    slabs, kx, wide = field[0].shape
    ins = (*field, green, image_green)
    shape = jax.ShapeDtypeStruct(field[0].shape, jnp.float32)
    return pl.pallas_call(
        middle_half_kernel,
        in_specs=[pl.BlockSpec(memory_space=SMEM)] + pieces_spec(len(ins)),
        out_specs=pieces_spec(len(field)),
        out_shape=[shape] * len(field),
        scratch_shapes=[VMEM((len(field), slabs, 8, wide), jnp.float32)] * 2,
        cost_estimate=cost(0, (*ins, *[shape] * len(field))),
        compiler_params=pltpu.CompilerParams(vmem_limit_bytes=LIMIT),
        name="middle_half",
    )(at, *ins)


def inverse_x_half_kernel(at_ref, *refs):
    parts = lax.axis_size("gx")
    group = lax.axis_size("gz") // 2
    me, member = at_ref[0], at_ref[2]
    ins, (th_ref, tl_ref), refs = refs[:group], refs[group : group + 2], refs[group + 2 :]
    outs, (high_ref, low_ref, res_ref) = refs[:parts], refs[parts:]
    table = (th_ref[...], tl_ref[...])
    _, kx, wide = ins[0].shape
    wide //= 2
    for z in range(ins[0].shape[0]):
        for k in range(group):
            start = pl.multiple_of((member ^ k) * kx, kx)
            for ref, value in zip((high_ref, low_ref), split(ins[k][z])):
                ref[z, pl.ds(start, kx), :] = value
                ref[z, pl.ds(group * kx + start, kx), :wide] = -value[:, wide:]
                ref[z, pl.ds(group * kx + start, kx), wide:] = value[:, :wide]
        res = product3(table, (high_ref[z], low_ref[z]), ((1,), (0,)))
        res_ref[z] = res.reshape(res_ref.shape[1:])
        for k in range(parts):
            outs[k][z] = res_ref[z, me ^ k]


def inverse_x_half(at, field, table, parts):
    slabs, kx, wide = field[0].shape
    width = len(field) * kx
    count = width // parts + 8
    shape = jax.ShapeDtypeStruct((slabs, count, wide), jnp.float32)
    ins = (*field, *table)
    return pl.pallas_call(
        inverse_x_half_kernel,
        in_specs=[pl.BlockSpec(memory_space=SMEM)] + pieces_spec(len(ins)),
        out_specs=pieces_spec(parts),
        out_shape=[shape] * parts,
        scratch_shapes=[
            VMEM((slabs, 2 * width, wide), jnp.bfloat16),
            VMEM((slabs, 2 * width, wide), jnp.bfloat16),
            VMEM((slabs, parts, count, wide), jnp.float32),
        ],
        cost_estimate=cost(12 * slabs * parts * count * width * wide, (*ins, *[shape] * parts)),
        compiler_params=pltpu.CompilerParams(vmem_limit_bytes=LIMIT),
        name="inverse_x_half",
    )(at, *ins)


def inverse_y_partial_kernel(chips, *refs):
    slabs, count, wide = refs[0].shape
    total = None
    outs, refs = refs[-chips:], refs[:-chips]
    for k, ins in enumerate((refs[:chips], refs[chips:-4])):
        rows = jnp.concatenate([r[...].reshape(-1, wide) for r in ins], axis=0)
        table = [r[...] for r in refs[len(refs) - 4 :][2 * k : 2 * k + 2]]
        term = product3(split(rows), table, ((1,), (0,)))
        total = term if total is None else total + term
    total = total.reshape(chips, slabs, count, -1)
    for k, ref in enumerate(outs):
        ref[...] = total[k]


def inverse_y_partial(keep, near, table):
    slabs, count, wide = keep[0].shape
    shape = jax.ShapeDtypeStruct((slabs, count, table[0].shape[1]), jnp.float32)
    ins = (*keep, *near, *table)
    return pl.pallas_call(
        functools.partial(inverse_y_partial_kernel, len(keep)),
        in_specs=pieces_spec(len(ins)),
        out_specs=pieces_spec(len(keep)),
        out_shape=[shape] * len(keep),
        cost_estimate=cost(12 * len(keep) * slabs * count * wide * shape.shape[2], (*ins, shape)),
        compiler_params=pltpu.CompilerParams(vmem_limit_bytes=LIMIT),
        name="inverse_y_partial",
    )(*ins)


def combine(mine, near, scale):
    total = (mine + near) * scale
    count = total.shape[1] - 8
    low, high = total[0], total[1]
    odd = lax.axis_index("gz") % 2 == 1
    first = jnp.where(odd, low[:count], high[:count])
    second = jnp.where(odd, high[:count], low[:count])
    return first, second, total[:, count:]


def slopes_kernel(at_ref, first_ref, second_ref, rows_ref, gx_ref, gy_ref):
    parts = lax.axis_size("gx")
    odd = at_ref[2] % 2 == 1
    first, second = first_ref[...], second_ref[...]
    for z, main in enumerate((jnp.where(odd, first, second), jnp.where(odd, second, first))):
        total = jnp.concatenate([main, rows_ref[z]], axis=0)
        differences(total, at_ref[0], parts, gx_ref.at[z], gy_ref.at[z])


def slopes(at, first, second, rows):
    shape = jax.ShapeDtypeStruct((2, *first.shape), jnp.float32)
    return pl.pallas_call(
        slopes_kernel,
        in_specs=[pl.BlockSpec(memory_space=SMEM)] + pieces_spec(3),
        out_specs=pieces_spec(2),
        out_shape=[shape, shape],
        compiler_params=pltpu.CompilerParams(vmem_limit_bytes=LIMIT),
        cost_estimate=cost(0, (first, second, rows, shape, shape)),
        name="slopes",
    )(at, first, second, rows)


def slope_z_pairs(first, second):
    size, mine = lax.axis_size("gz"), lax.axis_index("gz")
    odd, start, end = mine % 2 == 1, mine == 0, mine == size - 1
    near = swap(first, "gz", 1)
    pairs = [(i, i + 1) for i in range(1, size - 1, 2)]
    far = lax.ppermute(second, "gz", pairs + [(b, a) for a, b in pairs])
    low, high = jnp.where(odd, first, second), jnp.where(odd, second, first)
    below, above = jnp.where(odd, near, far), jnp.where(odd, far, near)
    bottom = (high - jnp.where(start, low, below)) * jnp.where(start, 1.0, 0.5)
    top = (jnp.where(end, high, above) - low) * jnp.where(end, 1.0, 0.5)
    return jnp.stack([bottom, top])


def swap(value, axis, mask):
    return lax.ppermute(value, axis, [(s, s ^ mask) for s in range(lax.axis_size(axis))])


def exchange(pieces, axis):
    return [pieces[0]] + [swap(p, axis, k) for k, p in enumerate(pieces) if k > 0]


def after(value, *others):
    return lax.optimization_barrier((value, others))[0]


def sums_y(rows, column, cut):
    near = rows[1::2]
    if cut:
        near = [r[z] for r in near for z in range(r.shape[0])]
    near = [swap(r, "gx", 1) for r in near]
    return inverse_y_partial(rows[0::2], near, column)


def halves_device(density, green, image_green):
    slabs, _, height = density.shape
    gz, gx = lax.axis_size("gz"), lax.axis_size("gx")
    group = gz // 2
    width = density.shape[1] * gx
    at = place()
    other = swap(density, "gz", group)
    raw = exchange([density] * gx, "gx")
    local, near_y, far_y, ahead, back = tables(at, density, gx)
    other = after(other, near_y)
    low, high = swap(other, "gx", 1), swap(other, "gx", 2)
    field = forward_half(at, [local, *raw[1:]], near_y, ahead, group)
    raw = [other, low, high, swap(after(high, field), "gx", 1)]
    field = exchange(field, "gz")
    field += exchange(forward_half(at, raw, near_y, ahead, group), "gz")
    field = middle_half(at, field, green, image_green)
    own, far = field[:group], field[group:]
    column = (*near_y, *far_y)
    far, own = exchange(far, "gz"), exchange(own, "gz")
    part, give = sums_y(inverse_x_half(at, far, back, gx), column, True)
    part = part + swap(give, "gx", 2)
    rows = inverse_x_half(at, own, back, gx)
    mine, give = sums_y((after(rows[0], part), *rows[1:]), column, False)
    mine = after(mine + swap(part, "gz", group))
    scale = 1.0 / (8.0 * slabs * gz * width * height)
    first, second, rows = combine(mine, swap(give, "gx", 2), scale)
    grad_z = slope_z_pairs(first, second)
    return *slopes(at, first, second, rows), grad_z


def per_device(density, green, image_green):
    slabs, count, height = density.shape
    width = count * lax.axis_size("gx")
    if lax.axis_size("gz") == 8 and lax.axis_size("gx") == 4 and slabs == 2 and width == height:
        return halves_device(density, green, image_green)
    gz, gx = lax.axis_size("gz"), lax.axis_size("gx")
    depth = slabs * gz
    column = column_table(height, gx)
    me = lax.axis_index("gx")
    own = tuple(lax.dynamic_index_in_dim(jnp.asarray(t), me, 0, keepdims=False) for t in column)
    rows = lax.all_gather(density, "gx", axis=1, tiled=True)
    field = forward(rows, own, forward_table(width), gz)
    field = lax.all_to_all(field, "gz", split_axis=0, concat_axis=0, tiled=True)
    field = middle(field, green, image_green)
    field = lax.all_to_all(field, "gz", split_axis=0, concat_axis=0, tiled=True)
    part = inverse_x(field, inverse_table(width), gx)
    part = lax.all_to_all(part, "gx", split_axis=0, concat_axis=0, tiled=True)
    scale = 1.0 / (8.0 * depth * width * height)
    pot, grad_x, grad_y = inverse_y(part, column, me.astype(jnp.int32).reshape(1), scale)
    return grad_x, grad_y, slope_z(*pot)


def solution(mesh):
    return jax.shard_map(
        per_device,
        mesh=mesh,
        in_specs=(P("gz", "gx", None), P(None, None, "gz", "gx"), P(None, None, "gz", "gx")),
        out_specs=(P("gz", "gx", None), P("gz", "gx", None), P("gz", "gx", None)),
        check_vma=False,
    )
```

```python
import functools
import math

import jax
import jax.numpy as jnp
import numpy as np
from jax import lax
from jax.experimental import pallas as pl
from jax.experimental.pallas import tpu as pltpu
from jax.sharding import PartitionSpec as P

VMEM = pltpu.VMEM
SMEM = pltpu.SMEM
LIMIT = 16 * 2**20


def halves(table):
    high = table.astype(jnp.bfloat16)
    low = (table - high.astype(np.float64)).astype(jnp.bfloat16)
    return high, low


def split(value):
    high = value.astype(jnp.bfloat16)
    return high, (value - high.astype(jnp.float32)).astype(jnp.bfloat16)


def product3(left, right, dims):
    one = functools.partial(
        lax.dot_general, dimension_numbers=(dims, ((), ())), preferred_element_type=jnp.float32
    )
    return one(left[0], right[0]) + (one(left[1], right[0]) + one(left[0], right[1]))


def turned(value):
    wide = value.shape[1] // 2
    swapped = jnp.concatenate([-value[:, wide:], value[:, :wide]], axis=1)
    return jnp.concatenate([value, swapped], axis=0)


def angles(space, freq):
    turns = np.outer(np.arange(freq), np.arange(space)) % freq
    return turns * (2.0 * math.pi / freq)


def column_table(space, blocks):
    angle = angles(space, 2 * space).reshape(blocks, -1, space)
    return halves(np.concatenate([np.cos(angle), -np.sin(angle)], axis=1))


def forward_table(space):
    angle = angles(space, 2 * space)
    return halves(np.concatenate([np.cos(angle), -np.sin(angle)], axis=1))


def inverse_table(space):
    angle = angles(space, 2 * space).T
    return halves(np.concatenate([np.cos(angle), np.sin(angle)], axis=1))


def times(value, turns, length):
    turns %= length
    re, im = value
    if turns == 0:
        return value
    if 4 * turns == length:
        return -im, re
    if 2 * turns == length:
        return -re, -im
    if 4 * turns == 3 * length:
        return im, -re
    c = math.cos(2.0 * math.pi * turns / length)
    s = math.sin(2.0 * math.pi * turns / length)
    if 8 * turns % length == 0:
        r = math.sqrt(0.5)
        if c * s > 0:
            return math.copysign(r, c) * (re - im), math.copysign(r, c) * (re + im)
        return math.copysign(r, c) * (re + im), math.copysign(r, c) * (im - re)
    return c * re - s * im, c * im + s * re


def add(a, b):
    return a[0] + b[0], a[1] + b[1]


def sub(a, b):
    return a[0] - b[0], a[1] - b[1]


def fft(values, sign):
    count = len(values)
    if count == 1:
        return values
    even, odd = fft(values[0::2], sign), fft(values[1::2], sign)
    odd = [times(v, sign * k, count) for k, v in enumerate(odd)]
    return [add(a, b) for a, b in zip(even, odd)] + [sub(a, b) for a, b in zip(even, odd)]


def forward_kernel(x_ref, yh_ref, yl_ref, th_ref, tl_ref, out_ref):
    table_y = (yh_ref[...], yl_ref[...])
    table_x = (th_ref[...], tl_ref[...])
    spec = product3(split(x_ref[0]), table_y, ((1,), (1,)))
    both = product3(table_x, split(turned(spec)), ((1,), (0,)))
    out_ref[:, 0] = both.reshape(out_ref.shape[0], *out_ref.shape[2:])


def forward(rows, table_y, table_x, blocks):
    slabs, width, height = rows.shape
    wide = table_y[0].shape[0]
    kx = 2 * width // blocks
    whole = lambda a: pl.BlockSpec(a.shape, lambda z: (0,) * a.ndim)
    return pl.pallas_call(
        forward_kernel,
        grid=(slabs,),
        in_specs=[pl.BlockSpec((1, width, height), lambda z: (z, 0, 0))]
        + [whole(a) for a in (*table_y, *table_x)],
        out_specs=pl.BlockSpec((blocks, 1, kx, wide), lambda z: (0, z, 0, 0)),
        out_shape=jax.ShapeDtypeStruct((blocks, slabs, kx, wide), jnp.float32),
        name="forward_xy",
    )(rows, *table_y, *table_x)


def through_z(field, green, image_green):
    depth = len(field)
    length = 2 * depth
    even = fft(field, -1)
    odd = fft([times(v, -z, length) for z, v in enumerate(field)], -1)
    spec = [v for pair in zip(even, odd) for v in pair]
    product = []
    for k in range(length):
        re, im = spec[k]
        mre, mim = times(spec[-k % length], -k * (depth - 1), length)
        (gre, gim), (hre, him) = green(k), image_green(k)
        product.append(
            (
                gre * re - gim * im + hre * mre - him * mim,
                gre * im + gim * re + hre * mim + him * mre,
            )
        )
    even = fft(product[0::2], 1)
    odd = fft(product[1::2], 1)
    return [add(even[z], times(odd[z], z, length)) for z in range(depth)]


def middle_kernel(f_ref, g_ref, h_ref, out_ref):
    slabs = f_ref.shape[1]
    half = f_ref.shape[3] // 2
    at = [(z // slabs, z % slabs) for z in range(f_ref.shape[0] * slabs)]
    field = [(f_ref[a, b, :, :half], f_ref[a, b, :, half:]) for a, b in at]
    both = lambda ref: lambda k: (ref[0, k], ref[1, k])
    for (a, b), (re, im) in zip(at, through_z(field, both(g_ref), both(h_ref))):
        out_ref[a, b, :, :half] = re
        out_ref[a, b, :, half:] = im


def middle(field, green, image_green):
    blocks, slabs, kx, wide = field.shape
    tile = 8
    spec = pl.BlockSpec((blocks, slabs, tile, wide), lambda i: (0, 0, i, 0))
    gspec = pl.BlockSpec((*green.shape[:2], tile, green.shape[3]), lambda i: (0, 0, i, 0))
    return pl.pallas_call(
        middle_kernel,
        grid=(kx // tile,),
        in_specs=[spec, gspec, gspec],
        out_specs=spec,
        out_shape=jax.ShapeDtypeStruct(field.shape, jnp.float32),
        name="middle_z",
    )(field, green, image_green)


def inverse_x_kernel(q_ref, th_ref, tl_ref, out_ref):
    field = q_ref[:, 0].reshape(-1, q_ref.shape[3])
    rows = product3((th_ref[...], tl_ref[...]), split(turned(field)), ((1,), (0,)))
    parts = out_ref.shape[0]
    count = rows.shape[0] // parts
    for part in range(parts):
        start = part * count
        before, after = max(start - 1, 0), min(start + count, rows.shape[0] - 1)
        out_ref[part, 0, :count] = rows[start : start + count]
        out_ref[part, 0, count : count + 8] = jnp.concatenate(
            [rows[before : before + 1], rows[after : after + 1], rows[:6]], axis=0
        )


def inverse_x(field, table, parts):
    blocks, slabs, kx, wide = field.shape
    width = blocks * kx // 2
    whole = lambda a: pl.BlockSpec(a.shape, lambda z: (0,) * a.ndim)
    shape = (parts, slabs, width // parts + 8, wide)
    return pl.pallas_call(
        inverse_x_kernel,
        grid=(slabs,),
        in_specs=[pl.BlockSpec((blocks, 1, kx, wide), lambda z: (0, z, 0, 0))]
        + [whole(a) for a in table],
        out_specs=pl.BlockSpec((parts, 1, *shape[2:]), lambda z: (0, z, 0, 0)),
        out_shape=jax.ShapeDtypeStruct(shape, jnp.float32),
        name="inverse_x",
    )(field, *table)


def differences(total, me, parts, gx_ref, gy_ref):
    count, height = total.shape[0] - 8, total.shape[1]
    main = total[:count]
    row = lax.broadcasted_iota(jnp.int32, main.shape, 0)
    before = jnp.where(row == 0, total[count : count + 1], pltpu.roll(main, 1, 0))
    after = jnp.where(row == count - 1, total[count + 1 : count + 2], pltpu.roll(main, count - 1, 0))
    edge = ((row == 0) & (me == 0)) | ((row == count - 1) & (me == parts - 1))
    gx_ref[...] = (after - before) * jnp.where(edge, 1.0, 0.5)
    col = lax.broadcasted_iota(jnp.int32, main.shape, 1)
    before = jnp.where(col == 0, main, pltpu.roll(main, 1, 1))
    after = jnp.where(col == height - 1, main, pltpu.roll(main, height - 1, 1))
    gy_ref[...] = (after - before) * jnp.where((col == 0) | (col == height - 1), 1.0, 0.5)
    return main


def inverse_y_kernel(scale, parts, me_ref, s_ref, th_ref, tl_ref, pot_ref, gx_ref, gy_ref):
    me = me_ref[0]
    for z in range(s_ref.shape[1]):
        total = None
        for part in range(parts):
            term = product3(
                split(s_ref[part, z]), (th_ref[part], tl_ref[part]), ((1,), (0,))
            )
            total = term if total is None else total + term
        total = total * scale
        main = differences(total, me, parts, gx_ref.at[z], gy_ref.at[z])
        pot_ref[z] = main


def inverse_y(rows, table, me, scale):
    parts, slabs, count, _ = rows.shape
    shape = jax.ShapeDtypeStruct((slabs, count - 8, table[0].shape[2]), jnp.float32)
    vmem = pl.BlockSpec(memory_space=VMEM)
    return pl.pallas_call(
        functools.partial(inverse_y_kernel, scale, parts),
        in_specs=[pl.BlockSpec(memory_space=SMEM), vmem, vmem, vmem],
        out_specs=(vmem, vmem, vmem),
        out_shape=(shape, shape, shape),
        name="inverse_y",
    )(me, rows, *table)


def slope_z(*pot):
    slabs = len(pot)
    size, me = lax.axis_size("gz"), lax.axis_index("gz")
    below = lax.ppermute(pot[-1], "gz", [(i, i + 1) for i in range(size - 1)])
    above = lax.ppermute(pot[0], "gz", [(i + 1, i) for i in range(size - 1)])
    below = jnp.where(me == 0, pot[0], below)
    above = jnp.where(me == size - 1, pot[-1], above)
    padded = jnp.stack([below, *pot, above])
    row = lax.broadcasted_iota(jnp.int32, (slabs, 1, 1), 0)
    edge = ((row == 0) & (me == 0)) | ((row == slabs - 1) & (me == size - 1))
    return (padded[2:] - padded[:-2]) * jnp.where(edge, 1.0, 0.5)


def pieces_spec(count):
    return [pl.BlockSpec(memory_space=VMEM)] * count


def place():
    half = lax.axis_size("gz") // 2
    mine = lax.axis_index("gz")
    return jnp.stack([lax.axis_index("gx"), mine // half, mine % half]).astype(jnp.int32)


def turn_table(space):
    rows = np.concatenate([np.arange(0, 2 * space, 8), np.arange(8)])
    angle = np.outer(rows, np.arange(space)) % (2 * space) * (math.pi / space)
    return np.concatenate([np.cos(angle), np.sin(angle)], axis=1).astype(np.float32)


def shuffled(value, index, block):
    wide = value.shape[1]
    while block < wide:
        if block % 128 == 0:
            parts = [value[:, i : i + block] for i in range(0, wide, block)]
            pairs = [parts[i ^ 1] for i in range(len(parts))]
        else:
            parts = [value[:, i : i + 2 * block] for i in range(0, wide, 2 * block)]
            pairs = [pltpu.roll(p, block, 1) for p in parts]
        value = jnp.where(index % 2 == 1, jnp.concatenate(pairs, axis=1), value)
        index, block = index // 2, 2 * block
    return value


def tables_kernel(space, parts, group, at_ref, turn_ref, density_ref, *refs):
    outs, (x_ref, k_ref) = refs[:9], refs[9:]
    outs[8][...] = density_ref[...]
    me, side, member = at_ref[0], at_ref[1], at_ref[2]
    coarse = 2 * space // 8
    count, block = space // parts, space // group
    for half in (slice(0, space), slice(space, 2 * space)):
        x_ref[:, half] = shuffled(turn_ref[:, half], me, count)
        k_ref[:, half] = shuffled(turn_ref[:, half], member, block)

    def fine(ref):
        return ref[coarse:, :space], ref[coarse:, space:]

    def turned_by(ref, row, cos, sin):
        c, s = ref[pl.ds(row, 1), :space], ref[pl.ds(row, 1), space:]
        return c * cos - s * sin, c * sin + s * cos

    def put(pair, at, lanes, values):
        for ref, value in zip(pair, split(jnp.concatenate(values, axis=0))):
            ref[at : at + 16, lanes] = value

    every = slice(0, space)
    first, second = slice(0, space), slice(space, 2 * space)
    freq = 2 * space // parts
    for k in range(2):
        base = (me ^ k) * (freq // 8)
        pair = outs[2 * k : 2 * k + 2]
        for row in range(0, freq, 16):
            two = [turned_by(turn_ref, base + row // 8 + i, *fine(turn_ref)) for i in range(2)]
            put(pair, row, every, [v[0] for v in two])
            put(pair, freq + row, every, [-v[1] for v in two])
    for row in range(0, space, 16):
        base = side * (space // 8) + (member ^ (row // block)) * (block // 8) + row % block // 8
        two = [turned_by(x_ref, base + i, *fine(x_ref)) for i in range(2)]
        put(outs[4:6], row, first, [v[0] for v in two])
        put(outs[4:6], row, second, [-v[1] for v in two])
    tiles = []
    cos, sin = fine(k_ref)
    which = lax.broadcasted_iota(jnp.int32, cos.shape, 0)
    sign = jnp.where((which % 2 == 1) & (side == 1), -1.0, 1.0)
    cos, sin = cos * sign, sin * sign
    for k in range(parts):
        part = me ^ k
        base = part * (count // 8)
        tiles += [turned_by(k_ref, base + i, cos, sin) for i in range(count // 8)]
        start, end = part == 0, part == parts - 1
        edges = []
        for near, step, inside, outside in ((start, -1, 7, 0), (end, count // 8, 0, 7)):
            row = jnp.where(near, base if step < 0 else base + step - 1, base + step)
            edges.append(
                turned_by(
                    k_ref, row, *[jnp.where(near, v[outside : outside + 1], v[inside : inside + 1]) for v in (cos, sin)]
                )
            )
        tiles.append(tuple(jnp.where(which == 0, edges[0][i], edges[1][i]) for i in range(2)))
    for row in range(0, 8 * len(tiles), 16):
        two = tiles[row // 8 : row // 8 + 2]
        put(outs[6:8], row, first, [v[0] for v in two])
        put(outs[6:8], row, second, [v[1] for v in two])


def tables(at, density, parts, group):
    space = density.shape[2]
    turn = turn_table(space)
    high = lambda *shape: [jax.ShapeDtypeStruct(shape, jnp.bfloat16)] * 2
    shapes = high(4 * space // parts, space) * 2 + high(space, 2 * space)
    shapes += high(space + 8 * parts, 2 * space)
    shapes += [jax.ShapeDtypeStruct(density.shape, density.dtype)]
    out = pl.pallas_call(
        functools.partial(tables_kernel, space, parts, group),
        in_specs=[pl.BlockSpec(memory_space=SMEM)] + pieces_spec(2),
        out_specs=pieces_spec(len(shapes)),
        out_shape=shapes,
        scratch_shapes=[VMEM(turn.shape, jnp.float32)] * 2,
        compiler_params=pltpu.CompilerParams(vmem_limit_bytes=LIMIT),
        cost_estimate=cost(0, (turn, *shapes)),
        name="tables",
    )(at, turn, density)
    return out[8], *[out[i : i + 2] for i in range(0, 8, 2)]


def turned_halves(value):
    return tuple(turned(v) for v in split(value))


def forward_half_kernel(*refs):
    parts = lax.axis_size("gx")
    rows, refs = refs[:parts], refs[parts:]
    yh_ref, yl_ref, th_ref, tl_ref, *outs = refs
    table_y = (yh_ref[...], yl_ref[...])
    table_x = (th_ref[...], tl_ref[...])
    kx = outs[0].shape[1]
    for z in range(rows[0].shape[0]):
        both = jnp.concatenate([r[z] for r in rows], axis=0)
        spec = product3(split(both), table_y, ((1,), (1,)))
        res = product3(table_x, turned_halves(spec), ((1,), (0,)))
        for k, ref in enumerate(outs):
            ref[z] = res[k * kx : (k + 1) * kx]


def cost(flops, arrays):
    size = sum(math.prod(a.shape) * a.dtype.itemsize for a in arrays)
    return pl.CostEstimate(flops=flops, bytes_accessed=size, transcendentals=0)


def forward_half(rows, table_y, table_x, group):
    slabs, count, height = rows[0].shape
    width = count * len(rows)
    wide = table_y[0].shape[0]
    shape = jax.ShapeDtypeStruct((slabs, width // group, wide), jnp.float32)
    ins = (*rows, *table_y, *table_x)
    return pl.pallas_call(
        forward_half_kernel,
        in_specs=pieces_spec(len(ins)),
        out_specs=pieces_spec(group),
        out_shape=[shape] * group,
        compiler_params=pltpu.CompilerParams(vmem_limit_bytes=LIMIT),
        cost_estimate=cost(6 * slabs * width * wide * (height + 2 * width), (*ins, *[shape] * group)),
        name="forward_half",
    )(*ins)


def middle_half_kernel(at_ref, *refs):
    group = lax.axis_size("gz") // 2
    side, member = at_ref[1], at_ref[2]
    ins, (g_ref, h_ref), refs = refs[: 2 * group], refs[2 * group : 2 * group + 2], refs[2 * group + 2 :]
    outs, (in_ref, out_ref) = refs[: 2 * group], refs[2 * group :]
    slabs, kx, wide = ins[0].shape
    half = wide // 2
    place = [(side ^ (k // group)) * group + (member ^ (k % group)) for k in range(2 * group)]
    at = [(z // slabs, z % slabs) for z in range(2 * group * slabs)]

    def tile(i, carry):
        rows = pl.ds(pl.multiple_of(8 * i, 8), 8)
        for k, slab in enumerate(place):
            in_ref[slab] = ins[k][:, rows, :]
        field = [(in_ref[a, b, :, :half], in_ref[a, b, :, half:]) for a, b in at]
        both = lambda ref: lambda k: (ref[0, k, rows, :], ref[1, k, rows, :])
        for (a, b), (re, im) in zip(at, through_z(field, both(g_ref), both(h_ref))):
            out_ref[a, b, :, :half] = re
            out_ref[a, b, :, half:] = im
        for k, slab in enumerate(place):
            outs[k][:, rows, :] = out_ref[slab]
        return carry

    lax.fori_loop(0, kx // 8, tile, 0)


def middle_half(at, field, green, image_green):
    slabs, kx, wide = field[0].shape
    ins = (*field, green, image_green)
    shape = jax.ShapeDtypeStruct(field[0].shape, jnp.float32)
    return pl.pallas_call(
        middle_half_kernel,
        in_specs=[pl.BlockSpec(memory_space=SMEM)] + pieces_spec(len(ins)),
        out_specs=pieces_spec(len(field)),
        out_shape=[shape] * len(field),
        scratch_shapes=[VMEM((len(field), slabs, 8, wide), jnp.float32)] * 2,
        cost_estimate=cost(0, (*ins, *[shape] * len(field))),
        compiler_params=pltpu.CompilerParams(vmem_limit_bytes=LIMIT),
        name="middle_half",
    )(at, *ins)


def inverse_x_half_kernel(*refs):
    group = lax.axis_size("gz") // 2
    ins, (th_ref, tl_ref), outs = refs[:group], refs[group : group + 2], refs[group + 2 :]
    table = (th_ref[...], tl_ref[...])
    count = outs[0].shape[1]
    for z in range(ins[0].shape[0]):
        field = jnp.concatenate([r[z] for r in ins], axis=0)
        res = product3(table, turned_halves(field), ((1,), (0,)))
        for k, ref in enumerate(outs):
            ref[z] = res[k * count : (k + 1) * count]


def inverse_x_half(field, table, parts):
    slabs, kx, wide = field[0].shape
    width = len(field) * kx
    count = width // parts + 8
    shape = jax.ShapeDtypeStruct((slabs, count, wide), jnp.float32)
    ins = (*field, *table)
    return pl.pallas_call(
        inverse_x_half_kernel,
        in_specs=pieces_spec(len(ins)),
        out_specs=pieces_spec(parts),
        out_shape=[shape] * parts,
        cost_estimate=cost(12 * slabs * parts * count * width * wide, (*ins, *[shape] * parts)),
        compiler_params=pltpu.CompilerParams(vmem_limit_bytes=LIMIT),
        name="inverse_x_half",
    )(*ins)


def inverse_y_partial_kernel(chips, *refs):
    slabs, count, wide = refs[0].shape
    total = None
    outs, refs = refs[-chips:], refs[:-chips]
    for k, ins in enumerate((refs[:chips], refs[chips:-4])):
        rows = jnp.concatenate([r[...].reshape(-1, wide) for r in ins], axis=0)
        table = [r[...] for r in refs[len(refs) - 4 :][2 * k : 2 * k + 2]]
        term = product3(split(rows), table, ((1,), (0,)))
        total = term if total is None else total + term
    total = total.reshape(chips, slabs, count, -1)
    for k, ref in enumerate(outs):
        ref[...] = total[k]


def inverse_y_partial(keep, near, table):
    slabs, count, wide = keep[0].shape
    shape = jax.ShapeDtypeStruct((slabs, count, table[0].shape[1]), jnp.float32)
    ins = (*keep, *near, *table)
    return pl.pallas_call(
        functools.partial(inverse_y_partial_kernel, len(keep)),
        in_specs=pieces_spec(len(ins)),
        out_specs=pieces_spec(len(keep)),
        out_shape=[shape] * len(keep),
        cost_estimate=cost(12 * len(keep) * slabs * count * wide * shape.shape[2], (*ins, shape)),
        compiler_params=pltpu.CompilerParams(vmem_limit_bytes=LIMIT),
        name="inverse_y_partial",
    )(*ins)


def combine(mine, near, scale):
    total = (mine + near) * scale
    count = total.shape[1] - 8
    low, high = total[0], total[1]
    odd = lax.axis_index("gz") % 2 == 1
    first = jnp.where(odd, low[:count], high[:count])
    second = jnp.where(odd, high[:count], low[:count])
    return first, second, total[:, count:]


def slopes_kernel(at_ref, first_ref, second_ref, rows_ref, gx_ref, gy_ref):
    parts = lax.axis_size("gx")
    odd = at_ref[2] % 2 == 1
    first, second = first_ref[...], second_ref[...]
    for z, main in enumerate((jnp.where(odd, first, second), jnp.where(odd, second, first))):
        total = jnp.concatenate([main, rows_ref[z]], axis=0)
        differences(total, at_ref[0], parts, gx_ref.at[z], gy_ref.at[z])


def slopes(at, first, second, rows):
    shape = jax.ShapeDtypeStruct((2, *first.shape), jnp.float32)
    return pl.pallas_call(
        slopes_kernel,
        in_specs=[pl.BlockSpec(memory_space=SMEM)] + pieces_spec(3),
        out_specs=pieces_spec(2),
        out_shape=[shape, shape],
        compiler_params=pltpu.CompilerParams(vmem_limit_bytes=LIMIT),
        cost_estimate=cost(0, (first, second, rows, shape, shape)),
        name="slopes",
    )(at, first, second, rows)


def slope_z_pairs(first, second):
    size, mine = lax.axis_size("gz"), lax.axis_index("gz")
    odd, start, end = mine % 2 == 1, mine == 0, mine == size - 1
    near = swap(first, "gz", 1)
    pairs = [(i, i + 1) for i in range(1, size - 1, 2)]
    far = lax.ppermute(second, "gz", pairs + [(b, a) for a, b in pairs])
    low, high = jnp.where(odd, first, second), jnp.where(odd, second, first)
    below, above = jnp.where(odd, near, far), jnp.where(odd, far, near)
    bottom = (high - jnp.where(start, low, below)) * jnp.where(start, 1.0, 0.5)
    top = (jnp.where(end, high, above) - low) * jnp.where(end, 1.0, 0.5)
    return jnp.stack([bottom, top])


def swap(value, axis, mask):
    return lax.ppermute(value, axis, [(s, s ^ mask) for s in range(lax.axis_size(axis))])


def exchange(pieces, axis):
    return [pieces[0]] + [swap(p, axis, k) for k, p in enumerate(pieces) if k > 0]


def after(value, *others):
    return lax.optimization_barrier((value, others))[0]


def sums_y(rows, column, cut):
    near = rows[1::2]
    if cut:
        near = [r[z] for r in near for z in range(r.shape[0])]
    near = [swap(r, "gx", 1) for r in near]
    return inverse_y_partial(rows[0::2], near, column)


def halves_device(density, green, image_green):
    slabs, _, height = density.shape
    gz, gx = lax.axis_size("gz"), lax.axis_size("gx")
    group = gz // 2
    width = density.shape[1] * gx
    at = place()
    other = swap(density, "gz", group)
    raw = exchange([density] * gx, "gx")
    local, near_y, far_y, ahead, back = tables(at, density, gx, group)
    other = after(other, near_y)
    field = forward_half([local, *raw[1:]], near_y, ahead, group)
    raw = exchange([other] * gx, "gx")
    field = exchange(field, "gz")
    field += exchange(forward_half(raw, near_y, ahead, group), "gz")
    field = middle_half(at, field, green, image_green)
    own, far = field[:group], field[group:]
    column = (*near_y, *far_y)
    far, own = exchange(far, "gz"), exchange(own, "gz")
    part, give = sums_y(inverse_x_half(far, back, gx), column, True)
    part = part + swap(give, "gx", 2)
    rows = inverse_x_half(own, back, gx)
    mine, give = sums_y((after(rows[0], part), *rows[1:]), column, False)
    mine = after(mine + swap(part, "gz", group))
    scale = 1.0 / (8.0 * slabs * gz * width * height)
    first, second, rows = combine(mine, swap(give, "gx", 2), scale)
    grad_z = slope_z_pairs(first, second)
    return *slopes(at, first, second, rows), grad_z


def per_device(density, green, image_green):
    slabs, count, height = density.shape
    width = count * lax.axis_size("gx")
    if lax.axis_size("gz") == 8 and lax.axis_size("gx") == 4 and slabs == 2 and width == height == 256:
        return halves_device(density, green, image_green)
    gz, gx = lax.axis_size("gz"), lax.axis_size("gx")
    depth = slabs * gz
    column = column_table(height, gx)
    me = lax.axis_index("gx")
    own = tuple(lax.dynamic_index_in_dim(jnp.asarray(t), me, 0, keepdims=False) for t in column)
    rows = lax.all_gather(density, "gx", axis=1, tiled=True)
    field = forward(rows, own, forward_table(width), gz)
    field = lax.all_to_all(field, "gz", split_axis=0, concat_axis=0, tiled=True)
    field = middle(field, green, image_green)
    field = lax.all_to_all(field, "gz", split_axis=0, concat_axis=0, tiled=True)
    part = inverse_x(field, inverse_table(width), gx)
    part = lax.all_to_all(part, "gx", split_axis=0, concat_axis=0, tiled=True)
    scale = 1.0 / (8.0 * depth * width * height)
    pot, grad_x, grad_y = inverse_y(part, column, me.astype(jnp.int32).reshape(1), scale)
    return grad_x, grad_y, slope_z(*pot)


def solution(mesh):
    return jax.shard_map(
        per_device,
        mesh=mesh,
        in_specs=(P("gz", "gx", None), P(None, None, "gz", "gx"), P(None, None, "gz", "gx")),
        out_specs=(P("gz", "gx", None), P("gz", "gx", None), P("gz", "gx", None)),
        check_vma=False,
    )
```

```python
import functools
import math

import jax
import jax.numpy as jnp
import numpy as np
from jax import lax
from jax.experimental import pallas as pl
from jax.experimental.pallas import tpu as pltpu
from jax.sharding import PartitionSpec as P

VMEM = pltpu.VMEM
SMEM = pltpu.SMEM
LIMIT = 16 * 2**20


def halves(table):
    high = table.astype(jnp.bfloat16)
    low = (table - high.astype(np.float64)).astype(jnp.bfloat16)
    return high, low


def split(value):
    high = value.astype(jnp.bfloat16)
    return high, (value - high.astype(jnp.float32)).astype(jnp.bfloat16)


def product3(left, right, dims):
    one = functools.partial(
        lax.dot_general, dimension_numbers=(dims, ((), ())), preferred_element_type=jnp.float32
    )
    return one(left[0], right[0]) + (one(left[1], right[0]) + one(left[0], right[1]))


def turned(value):
    wide = value.shape[1] // 2
    swapped = jnp.concatenate([-value[:, wide:], value[:, :wide]], axis=1)
    return jnp.concatenate([value, swapped], axis=0)


def angles(space, freq):
    turns = np.outer(np.arange(freq), np.arange(space)) % freq
    return turns * (2.0 * math.pi / freq)


def column_table(space, blocks):
    angle = angles(space, 2 * space).reshape(blocks, -1, space)
    return halves(np.concatenate([np.cos(angle), -np.sin(angle)], axis=1))


def forward_table(space):
    angle = angles(space, 2 * space)
    return halves(np.concatenate([np.cos(angle), -np.sin(angle)], axis=1))


def inverse_table(space):
    angle = angles(space, 2 * space).T
    return halves(np.concatenate([np.cos(angle), np.sin(angle)], axis=1))


def times(value, turns, length):
    turns %= length
    re, im = value
    if turns == 0:
        return value
    if 4 * turns == length:
        return -im, re
    if 2 * turns == length:
        return -re, -im
    if 4 * turns == 3 * length:
        return im, -re
    c = math.cos(2.0 * math.pi * turns / length)
    s = math.sin(2.0 * math.pi * turns / length)
    if 8 * turns % length == 0:
        r = math.sqrt(0.5)
        if c * s > 0:
            return math.copysign(r, c) * (re - im), math.copysign(r, c) * (re + im)
        return math.copysign(r, c) * (re + im), math.copysign(r, c) * (im - re)
    return c * re - s * im, c * im + s * re


def add(a, b):
    return a[0] + b[0], a[1] + b[1]


def sub(a, b):
    return a[0] - b[0], a[1] - b[1]


def fft(values, sign):
    count = len(values)
    if count == 1:
        return values
    even, odd = fft(values[0::2], sign), fft(values[1::2], sign)
    odd = [times(v, sign * k, count) for k, v in enumerate(odd)]
    return [add(a, b) for a, b in zip(even, odd)] + [sub(a, b) for a, b in zip(even, odd)]


def forward_kernel(x_ref, yh_ref, yl_ref, th_ref, tl_ref, out_ref):
    table_y = (yh_ref[...], yl_ref[...])
    table_x = (th_ref[...], tl_ref[...])
    spec = product3(split(x_ref[0]), table_y, ((1,), (1,)))
    both = product3(table_x, split(turned(spec)), ((1,), (0,)))
    out_ref[:, 0] = both.reshape(out_ref.shape[0], *out_ref.shape[2:])


def forward(rows, table_y, table_x, blocks):
    slabs, width, height = rows.shape
    wide = table_y[0].shape[0]
    kx = 2 * width // blocks
    whole = lambda a: pl.BlockSpec(a.shape, lambda z: (0,) * a.ndim)
    return pl.pallas_call(
        forward_kernel,
        grid=(slabs,),
        in_specs=[pl.BlockSpec((1, width, height), lambda z: (z, 0, 0))]
        + [whole(a) for a in (*table_y, *table_x)],
        out_specs=pl.BlockSpec((blocks, 1, kx, wide), lambda z: (0, z, 0, 0)),
        out_shape=jax.ShapeDtypeStruct((blocks, slabs, kx, wide), jnp.float32),
        name="forward_xy",
    )(rows, *table_y, *table_x)


def through_z(field, green, image_green):
    depth = len(field)
    length = 2 * depth
    even = fft(field, -1)
    odd = fft([times(v, -z, length) for z, v in enumerate(field)], -1)
    spec = [v for pair in zip(even, odd) for v in pair]
    product = []
    for k in range(length):
        re, im = spec[k]
        mre, mim = times(spec[-k % length], -k * (depth - 1), length)
        (gre, gim), (hre, him) = green(k), image_green(k)
        product.append(
            (
                gre * re - gim * im + hre * mre - him * mim,
                gre * im + gim * re + hre * mim + him * mre,
            )
        )
    even = fft(product[0::2], 1)
    odd = fft(product[1::2], 1)
    return [add(even[z], times(odd[z], z, length)) for z in range(depth)]


def middle_kernel(f_ref, g_ref, h_ref, out_ref):
    slabs = f_ref.shape[1]
    half = f_ref.shape[3] // 2
    at = [(z // slabs, z % slabs) for z in range(f_ref.shape[0] * slabs)]
    field = [(f_ref[a, b, :, :half], f_ref[a, b, :, half:]) for a, b in at]
    both = lambda ref: lambda k: (ref[0, k], ref[1, k])
    for (a, b), (re, im) in zip(at, through_z(field, both(g_ref), both(h_ref))):
        out_ref[a, b, :, :half] = re
        out_ref[a, b, :, half:] = im


def middle(field, green, image_green):
    blocks, slabs, kx, wide = field.shape
    tile = 8
    spec = pl.BlockSpec((blocks, slabs, tile, wide), lambda i: (0, 0, i, 0))
    gspec = pl.BlockSpec((*green.shape[:2], tile, green.shape[3]), lambda i: (0, 0, i, 0))
    return pl.pallas_call(
        middle_kernel,
        grid=(kx // tile,),
        in_specs=[spec, gspec, gspec],
        out_specs=spec,
        out_shape=jax.ShapeDtypeStruct(field.shape, jnp.float32),
        name="middle_z",
    )(field, green, image_green)


def inverse_x_kernel(q_ref, th_ref, tl_ref, out_ref):
    field = q_ref[:, 0].reshape(-1, q_ref.shape[3])
    rows = product3((th_ref[...], tl_ref[...]), split(turned(field)), ((1,), (0,)))
    parts = out_ref.shape[0]
    count = rows.shape[0] // parts
    for part in range(parts):
        start = part * count
        before, after = max(start - 1, 0), min(start + count, rows.shape[0] - 1)
        out_ref[part, 0, :count] = rows[start : start + count]
        out_ref[part, 0, count : count + 8] = jnp.concatenate(
            [rows[before : before + 1], rows[after : after + 1], rows[:6]], axis=0
        )


def inverse_x(field, table, parts):
    blocks, slabs, kx, wide = field.shape
    width = blocks * kx // 2
    whole = lambda a: pl.BlockSpec(a.shape, lambda z: (0,) * a.ndim)
    shape = (parts, slabs, width // parts + 8, wide)
    return pl.pallas_call(
        inverse_x_kernel,
        grid=(slabs,),
        in_specs=[pl.BlockSpec((blocks, 1, kx, wide), lambda z: (0, z, 0, 0))]
        + [whole(a) for a in table],
        out_specs=pl.BlockSpec((parts, 1, *shape[2:]), lambda z: (0, z, 0, 0)),
        out_shape=jax.ShapeDtypeStruct(shape, jnp.float32),
        name="inverse_x",
    )(field, *table)


def differences(main, outer, me, parts, gx_ref, gy_ref):
    count, height = main.shape
    row = lax.broadcasted_iota(jnp.int32, main.shape, 0)
    before = jnp.where(row == 0, outer[0:1], pltpu.roll(main, 1, 0))
    after = jnp.where(row == count - 1, outer[1:2], pltpu.roll(main, count - 1, 0))
    edge = ((row == 0) & (me == 0)) | ((row == count - 1) & (me == parts - 1))
    gx_ref[...] = (after - before) * jnp.where(edge, 1.0, 0.5)
    col = lax.broadcasted_iota(jnp.int32, main.shape, 1)
    before = jnp.where(col == 0, main, pltpu.roll(main, 1, 1))
    after = jnp.where(col == height - 1, main, pltpu.roll(main, height - 1, 1))
    gy_ref[...] = (after - before) * jnp.where((col == 0) | (col == height - 1), 1.0, 0.5)


def inverse_y_kernel(scale, parts, me_ref, s_ref, th_ref, tl_ref, pot_ref, gx_ref, gy_ref):
    me = me_ref[0]
    for z in range(s_ref.shape[1]):
        total = None
        for part in range(parts):
            term = product3(
                split(s_ref[part, z]), (th_ref[part], tl_ref[part]), ((1,), (0,))
            )
            total = term if total is None else total + term
        total = total * scale
        count = total.shape[0] - 8
        main = total[:count]
        differences(main, total[count:], me, parts, gx_ref.at[z], gy_ref.at[z])
        pot_ref[z] = main


def inverse_y(rows, table, me, scale):
    parts, slabs, count, _ = rows.shape
    shape = jax.ShapeDtypeStruct((slabs, count - 8, table[0].shape[2]), jnp.float32)
    vmem = pl.BlockSpec(memory_space=VMEM)
    return pl.pallas_call(
        functools.partial(inverse_y_kernel, scale, parts),
        in_specs=[pl.BlockSpec(memory_space=SMEM), vmem, vmem, vmem],
        out_specs=(vmem, vmem, vmem),
        out_shape=(shape, shape, shape),
        name="inverse_y",
    )(me, rows, *table)


def slope_z(*pot):
    slabs = len(pot)
    size, me = lax.axis_size("gz"), lax.axis_index("gz")
    below = lax.ppermute(pot[-1], "gz", [(i, i + 1) for i in range(size - 1)])
    above = lax.ppermute(pot[0], "gz", [(i + 1, i) for i in range(size - 1)])
    below = jnp.where(me == 0, pot[0], below)
    above = jnp.where(me == size - 1, pot[-1], above)
    padded = jnp.stack([below, *pot, above])
    row = lax.broadcasted_iota(jnp.int32, (slabs, 1, 1), 0)
    edge = ((row == 0) & (me == 0)) | ((row == slabs - 1) & (me == size - 1))
    return (padded[2:] - padded[:-2]) * jnp.where(edge, 1.0, 0.5)


def pieces_spec(count):
    return [pl.BlockSpec(memory_space=VMEM)] * count


def place():
    half = lax.axis_size("gz") // 2
    mine = lax.axis_index("gz")
    return jnp.stack([lax.axis_index("gx"), mine // half, mine % half]).astype(jnp.int32)


def turn_table(space):
    rows = np.concatenate([np.arange(0, 2 * space, 8), np.arange(8)])
    angle = np.outer(rows, np.arange(space)) % (2 * space) * (math.pi / space)
    return np.concatenate([np.cos(angle), np.sin(angle)], axis=1).astype(np.float32)


def shuffled(value, index, block):
    wide = value.shape[1]
    while block < wide:
        if block % 128 == 0:
            parts = [value[:, i : i + block] for i in range(0, wide, block)]
            pairs = [parts[i ^ 1] for i in range(len(parts))]
        else:
            parts = [value[:, i : i + 2 * block] for i in range(0, wide, 2 * block)]
            pairs = [pltpu.roll(p, block, 1) for p in parts]
        value = jnp.where(index % 2 == 1, jnp.concatenate(pairs, axis=1), value)
        index, block = index // 2, 2 * block
    return value


def tables_kernel(space, parts, group, at_ref, turn_ref, density_ref, *refs):
    outs, (x_ref, k_ref) = refs[:9], refs[9:]
    outs[8][...] = density_ref[...]
    me, side, member = at_ref[0], at_ref[1], at_ref[2]
    coarse = 2 * space // 8
    count, block = space // parts, space // group
    for half in (slice(0, space), slice(space, 2 * space)):
        x_ref[:, half] = shuffled(turn_ref[:, half], me, count)
        k_ref[:, half] = shuffled(turn_ref[:, half], member, block)

    def fine(ref):
        return ref[coarse:, :space], ref[coarse:, space:]

    def turned_by(ref, row, cos, sin):
        c, s = ref[pl.ds(row, 1), :space], ref[pl.ds(row, 1), space:]
        return c * cos - s * sin, c * sin + s * cos

    def put(pair, at, lanes, values):
        for ref, value in zip(pair, split(jnp.concatenate(values, axis=0))):
            ref[at : at + 16, lanes] = value

    every = slice(0, space)
    first, second = slice(0, space), slice(space, 2 * space)
    freq = 2 * space // parts
    for k in range(2):
        base = (me ^ k) * (freq // 8)
        pair = outs[2 * k : 2 * k + 2]
        for row in range(0, freq, 16):
            two = [turned_by(turn_ref, base + row // 8 + i, *fine(turn_ref)) for i in range(2)]
            put(pair, row, every, [v[0] for v in two])
            put(pair, freq + row, every, [-v[1] for v in two])
    for row in range(0, space, 16):
        base = side * (space // 8) + (member ^ (row // block)) * (block // 8) + row % block // 8
        two = [turned_by(x_ref, base + i, *fine(x_ref)) for i in range(2)]
        put(outs[4:6], row, first, [v[0] for v in two])
        put(outs[4:6], row, second, [-v[1] for v in two])
    tiles, edges = [], []
    cos, sin = fine(k_ref)
    which = lax.broadcasted_iota(jnp.int32, cos.shape, 0)
    sign = jnp.where((which % 2 == 1) & (side == 1), -1.0, 1.0)
    cos, sin = cos * sign, sin * sign
    for k in range(parts):
        part = me ^ k
        base = part * (count // 8)
        tiles += [turned_by(k_ref, base + i, cos, sin) for i in range(count // 8)]
        start, end = part == 0, part == parts - 1
        for near, step, inside, outside in ((start, -1, 7, 0), (end, count // 8, 0, 7)):
            row = jnp.where(near, base if step < 0 else base + step - 1, base + step)
            edges.append(
                turned_by(
                    k_ref, row, *[jnp.where(near, v[outside : outside + 1], v[inside : inside + 1]) for v in (cos, sin)]
                )
            )
    last = tuple(jnp.broadcast_to(v, cos.shape) for v in edges[0])
    for i, edge in enumerate(edges[1:]):
        last = tuple(jnp.where(which == i + 1, e, v) for e, v in zip(edge, last))
    tiles += [last, last]
    for row in range(0, 8 * len(tiles), 16):
        two = tiles[row // 8 : row // 8 + 2]
        put(outs[6:8], row, first, [v[0] for v in two])
        put(outs[6:8], row, second, [v[1] for v in two])


def tables(at, density, parts, group):
    space = density.shape[2]
    turn = turn_table(space)
    high = lambda *shape: [jax.ShapeDtypeStruct(shape, jnp.bfloat16)] * 2
    shapes = high(4 * space // parts, space) * 2 + high(space, 2 * space)
    shapes += high(space + 16, 2 * space)
    shapes += [jax.ShapeDtypeStruct(density.shape, density.dtype)]
    out = pl.pallas_call(
        functools.partial(tables_kernel, space, parts, group),
        in_specs=[pl.BlockSpec(memory_space=SMEM)] + pieces_spec(2),
        out_specs=pieces_spec(len(shapes)),
        out_shape=shapes,
        scratch_shapes=[VMEM(turn.shape, jnp.float32)] * 2,
        compiler_params=pltpu.CompilerParams(vmem_limit_bytes=LIMIT),
        cost_estimate=cost(0, (turn, *shapes)),
        name="tables",
    )(at, turn, density)
    return out[8], *[out[i : i + 2] for i in range(0, 8, 2)]


def turned_halves(value):
    return tuple(turned(v) for v in split(value))


def forward_half_kernel(*refs):
    parts = lax.axis_size("gx")
    rows, refs = refs[:parts], refs[parts:]
    yh_ref, yl_ref, th_ref, tl_ref, *outs = refs
    table_y = (yh_ref[...], yl_ref[...])
    table_x = (th_ref[...], tl_ref[...])
    kx = outs[0].shape[1]
    for z in range(rows[0].shape[0]):
        both = jnp.concatenate([r[z] for r in rows], axis=0)
        spec = product3(split(both), table_y, ((1,), (1,)))
        res = product3(table_x, turned_halves(spec), ((1,), (0,)))
        for k, ref in enumerate(outs):
            ref[z] = res[k * kx : (k + 1) * kx]


def cost(flops, arrays):
    size = sum(math.prod(a.shape) * a.dtype.itemsize for a in arrays)
    return pl.CostEstimate(flops=flops, bytes_accessed=size, transcendentals=0)


def forward_half(rows, table_y, table_x, group):
    slabs, count, height = rows[0].shape
    width = count * len(rows)
    wide = table_y[0].shape[0]
    shape = jax.ShapeDtypeStruct((slabs, width // group, wide), jnp.float32)
    ins = (*rows, *table_y, *table_x)
    return pl.pallas_call(
        forward_half_kernel,
        in_specs=pieces_spec(len(ins)),
        out_specs=pieces_spec(group),
        out_shape=[shape] * group,
        compiler_params=pltpu.CompilerParams(vmem_limit_bytes=LIMIT),
        cost_estimate=cost(6 * slabs * width * wide * (height + 2 * width), (*ins, *[shape] * group)),
        name="forward_half",
    )(*ins)


def middle_half_kernel(at_ref, *refs):
    group = lax.axis_size("gz") // 2
    side, member = at_ref[1], at_ref[2]
    ins, (g_ref, h_ref), refs = refs[: 2 * group], refs[2 * group : 2 * group + 2], refs[2 * group + 2 :]
    outs, (in_ref, out_ref) = refs[: 2 * group], refs[2 * group :]
    slabs, kx, wide = ins[0].shape
    half = wide // 2
    place = [(side ^ (k // group)) * group + (member ^ (k % group)) for k in range(2 * group)]
    at = [(z // slabs, z % slabs) for z in range(2 * group * slabs)]

    def tile(i, carry):
        rows = pl.ds(pl.multiple_of(8 * i, 8), 8)
        for k, slab in enumerate(place):
            in_ref[slab] = ins[k][:, rows, :]
        field = [(in_ref[a, b, :, :half], in_ref[a, b, :, half:]) for a, b in at]
        both = lambda ref: lambda k: (ref[0, k, rows, :], ref[1, k, rows, :])
        for (a, b), (re, im) in zip(at, through_z(field, both(g_ref), both(h_ref))):
            out_ref[a, b, :, :half] = re
            out_ref[a, b, :, half:] = im
        for k, slab in enumerate(place):
            outs[k][:, rows, :] = out_ref[slab]
        return carry

    lax.fori_loop(0, kx // 8, tile, 0, unroll=2)


def middle_half(at, field, green, image_green):
    slabs, kx, wide = field[0].shape
    ins = (*field, green, image_green)
    shape = jax.ShapeDtypeStruct(field[0].shape, jnp.float32)
    return pl.pallas_call(
        middle_half_kernel,
        in_specs=[pl.BlockSpec(memory_space=SMEM)] + pieces_spec(len(ins)),
        out_specs=pieces_spec(len(field)),
        out_shape=[shape] * len(field),
        scratch_shapes=[VMEM((len(field), slabs, 8, wide), jnp.float32)] * 2,
        cost_estimate=cost(0, (*ins, *[shape] * len(field))),
        compiler_params=pltpu.CompilerParams(vmem_limit_bytes=LIMIT),
        name="middle_half",
    )(at, *ins)


def inverse_x_half_kernel(*refs):
    group = lax.axis_size("gz") // 2
    ins, (th_ref, tl_ref), outs = refs[:group], refs[group : group + 2], refs[group + 2 :]
    table = (th_ref[...], tl_ref[...])
    slabs = ins[0].shape[0]
    count = (outs[0].shape[0] - 8) // slabs
    inner = count * len(outs)
    for z in range(slabs):
        field = jnp.concatenate([r[z] for r in ins], axis=0)
        res = product3(table, turned_halves(field), ((1,), (0,)))
        for k, ref in enumerate(outs):
            ref[z * count : (z + 1) * count] = res[k * count : (k + 1) * count]
            if z == 0:
                ref[slabs * count :] = res[inner : inner + 8]
            at = slabs * count + 2 * z
            ref[at : at + 2] = res[inner + 2 * k : inner + 2 * k + 2]


def inverse_x_half(field, table, parts):
    slabs, kx, wide = field[0].shape
    width = len(field) * kx
    shape = jax.ShapeDtypeStruct((slabs * width // parts + 8, wide), jnp.float32)
    ins = (*field, *table)
    return pl.pallas_call(
        inverse_x_half_kernel,
        in_specs=pieces_spec(len(ins)),
        out_specs=pieces_spec(parts),
        out_shape=[shape] * parts,
        cost_estimate=cost(12 * slabs * (width + 8 * parts) * width * wide, (*ins, *[shape] * parts)),
        compiler_params=pltpu.CompilerParams(vmem_limit_bytes=LIMIT),
        name="inverse_x_half",
    )(*ins)


def inverse_y_partial_kernel(chips, *refs):
    total = None
    outs, refs = refs[-chips:], refs[:-chips]
    for k, ins in enumerate((refs[:chips], refs[chips:-4])):
        rows = jnp.concatenate([r[...] for r in ins], axis=0)
        table = [r[...] for r in refs[len(refs) - 4 :][2 * k : 2 * k + 2]]
        term = product3(split(rows), table, ((1,), (0,)))
        total = term if total is None else total + term
    for k, ref in enumerate(outs):
        ref[...] = total[k * ref.shape[0] : (k + 1) * ref.shape[0]]


def inverse_y_partial(keep, near, table):
    count, wide = keep[0].shape
    shape = jax.ShapeDtypeStruct((count, table[0].shape[1]), jnp.float32)
    ins = (*keep, *near, *table)
    return pl.pallas_call(
        functools.partial(inverse_y_partial_kernel, len(keep)),
        in_specs=pieces_spec(len(ins)),
        out_specs=pieces_spec(len(keep)),
        out_shape=[shape] * len(keep),
        cost_estimate=cost(12 * len(keep) * (count + 8) * wide * shape.shape[1], (*ins, shape, shape)),
        compiler_params=pltpu.CompilerParams(vmem_limit_bytes=LIMIT),
        name="inverse_y_partial",
    )(*ins)


def combine(mine, near, scale):
    total = (mine + near) * scale
    count = (total.shape[0] - 8) // 2
    low, high = total[:count], total[count : 2 * count]
    odd = lax.axis_index("gz") % 2 == 1
    return jnp.where(odd, low, high), jnp.where(odd, high, low), total[2 * count :]


def slopes_kernel(at_ref, first_ref, second_ref, outer_ref, gx_ref, gy_ref):
    parts = lax.axis_size("gx")
    odd = at_ref[2] % 2 == 1
    first, second, outer = first_ref[...], second_ref[...], outer_ref[...]
    for z, main in enumerate((jnp.where(odd, first, second), jnp.where(odd, second, first))):
        differences(main, outer[2 * z :], at_ref[0], parts, gx_ref.at[z], gy_ref.at[z])


def slopes(at, first, second, rows):
    shape = jax.ShapeDtypeStruct((2, *first.shape), jnp.float32)
    return pl.pallas_call(
        slopes_kernel,
        in_specs=[pl.BlockSpec(memory_space=SMEM)] + pieces_spec(3),
        out_specs=pieces_spec(2),
        out_shape=[shape, shape],
        compiler_params=pltpu.CompilerParams(vmem_limit_bytes=LIMIT),
        cost_estimate=cost(0, (first, second, rows, shape, shape)),
        name="slopes",
    )(at, first, second, rows)


def slope_z_pairs(first, second):
    size, mine = lax.axis_size("gz"), lax.axis_index("gz")
    odd, start, end = mine % 2 == 1, mine == 0, mine == size - 1
    near = swap(first, "gz", 1)
    pairs = [(i, i + 1) for i in range(1, size - 1, 2)]
    far = lax.ppermute(second, "gz", pairs + [(b, a) for a, b in pairs])
    low, high = jnp.where(odd, first, second), jnp.where(odd, second, first)
    below, above = jnp.where(odd, near, far), jnp.where(odd, far, near)
    bottom = (high - jnp.where(start, low, below)) * jnp.where(start, 1.0, 0.5)
    top = (jnp.where(end, high, above) - low) * jnp.where(end, 1.0, 0.5)
    return jnp.stack([bottom, top])


def swap(value, axis, mask):
    return lax.ppermute(value, axis, [(s, s ^ mask) for s in range(lax.axis_size(axis))])


def exchange(pieces, axis):
    return [pieces[0]] + [swap(p, axis, k) for k, p in enumerate(pieces) if k > 0]


def after(value, *others):
    return lax.optimization_barrier((value, others))[0]


def sums_y(rows, column, cut):
    near = rows[1::2]
    if cut:
        near = [part for r in near for part in (r[:68], r[68:])]
    near = [swap(r, "gx", 1) for r in near]
    return inverse_y_partial(rows[0::2], near, column)


def halves_device(density, green, image_green):
    slabs, _, height = density.shape
    gz, gx = lax.axis_size("gz"), lax.axis_size("gx")
    group = gz // 2
    width = density.shape[1] * gx
    at = place()
    other = swap(density, "gz", group)
    raw = exchange([density] * gx, "gx")
    local, near_y, far_y, ahead, back = tables(at, density, gx, group)
    other = after(other, near_y)
    field = forward_half([local, *raw[1:]], near_y, ahead, group)
    raw = exchange([other] * gx, "gx")
    field = exchange(field, "gz")
    field += exchange(forward_half(raw, near_y, ahead, group), "gz")
    field = middle_half(at, field, green, image_green)
    own, far = field[:group], field[group:]
    column = (*near_y, *far_y)
    far, own = exchange(far, "gz"), exchange(own, "gz")
    part, give = sums_y(inverse_x_half(far, back, gx), column, True)
    part = part + swap(give, "gx", 2)
    rows = inverse_x_half(own, back, gx)
    mine, give = sums_y((after(rows[0], part), *rows[1:]), column, False)
    mine = after(mine + swap(part, "gz", group))
    scale = 1.0 / (8.0 * slabs * gz * width * height)
    first, second, rows = combine(mine, swap(give, "gx", 2), scale)
    grad_z = slope_z_pairs(first, second)
    return *slopes(at, first, second, rows), grad_z


def per_device(density, green, image_green):
    slabs, count, height = density.shape
    width = count * lax.axis_size("gx")
    if lax.axis_size("gz") == 8 and lax.axis_size("gx") == 4 and slabs == 2 and width == height == 256:
        return halves_device(density, green, image_green)
    gz, gx = lax.axis_size("gz"), lax.axis_size("gx")
    depth = slabs * gz
    column = column_table(height, gx)
    me = lax.axis_index("gx")
    own = tuple(lax.dynamic_index_in_dim(jnp.asarray(t), me, 0, keepdims=False) for t in column)
    rows = lax.all_gather(density, "gx", axis=1, tiled=True)
    field = forward(rows, own, forward_table(width), gz)
    field = lax.all_to_all(field, "gz", split_axis=0, concat_axis=0, tiled=True)
    field = middle(field, green, image_green)
    field = lax.all_to_all(field, "gz", split_axis=0, concat_axis=0, tiled=True)
    part = inverse_x(field, inverse_table(width), gx)
    part = lax.all_to_all(part, "gx", split_axis=0, concat_axis=0, tiled=True)
    scale = 1.0 / (8.0 * depth * width * height)
    pot, grad_x, grad_y = inverse_y(part, column, me.astype(jnp.int32).reshape(1), scale)
    return grad_x, grad_y, slope_z(*pot)


def solution(mesh):
    return jax.shard_map(
        per_device,
        mesh=mesh,
        in_specs=(P("gz", "gx", None), P(None, None, "gz", "gx"), P(None, None, "gz", "gx")),
        out_specs=(P("gz", "gx", None), P("gz", "gx", None), P("gz", "gx", None)),
        check_vma=False,
    )
```

```python
import functools
import math

import jax
import jax.numpy as jnp
import numpy as np
from jax import lax
from jax.experimental import pallas as pl
from jax.experimental.pallas import tpu as pltpu
from jax.sharding import PartitionSpec as P

VMEM = pltpu.VMEM
SMEM = pltpu.SMEM
LIMIT = 16 * 2**20


def halves(table):
    high = table.astype(jnp.bfloat16)
    low = (table - high.astype(np.float64)).astype(jnp.bfloat16)
    return high, low


def split(value):
    high = value.astype(jnp.bfloat16)
    return high, (value - high.astype(jnp.float32)).astype(jnp.bfloat16)


def product3(left, right, dims):
    one = functools.partial(
        lax.dot_general, dimension_numbers=(dims, ((), ())), preferred_element_type=jnp.float32
    )
    return one(left[0], right[0]) + (one(left[1], right[0]) + one(left[0], right[1]))


def turned(value):
    wide = value.shape[1] // 2
    swapped = jnp.concatenate([-value[:, wide:], value[:, :wide]], axis=1)
    return jnp.concatenate([value, swapped], axis=0)


def angles(space, freq):
    turns = np.outer(np.arange(freq), np.arange(space)) % freq
    return turns * (2.0 * math.pi / freq)


def column_table(space, blocks):
    angle = angles(space, 2 * space).reshape(blocks, -1, space)
    return halves(np.concatenate([np.cos(angle), -np.sin(angle)], axis=1))


def forward_table(space):
    angle = angles(space, 2 * space)
    return halves(np.concatenate([np.cos(angle), -np.sin(angle)], axis=1))


def inverse_table(space):
    angle = angles(space, 2 * space).T
    return halves(np.concatenate([np.cos(angle), np.sin(angle)], axis=1))


def times(value, turns, length):
    turns %= length
    re, im = value
    if turns == 0:
        return value
    if 4 * turns == length:
        return -im, re
    if 2 * turns == length:
        return -re, -im
    if 4 * turns == 3 * length:
        return im, -re
    c = math.cos(2.0 * math.pi * turns / length)
    s = math.sin(2.0 * math.pi * turns / length)
    if 8 * turns % length == 0:
        r = math.sqrt(0.5)
        if c * s > 0:
            return math.copysign(r, c) * (re - im), math.copysign(r, c) * (re + im)
        return math.copysign(r, c) * (re + im), math.copysign(r, c) * (im - re)
    return c * re - s * im, c * im + s * re


def add(a, b):
    return a[0] + b[0], a[1] + b[1]


def sub(a, b):
    return a[0] - b[0], a[1] - b[1]


def fft(values, sign):
    count = len(values)
    if count == 1:
        return values
    even, odd = fft(values[0::2], sign), fft(values[1::2], sign)
    odd = [times(v, sign * k, count) for k, v in enumerate(odd)]
    return [add(a, b) for a, b in zip(even, odd)] + [sub(a, b) for a, b in zip(even, odd)]


def forward_kernel(x_ref, yh_ref, yl_ref, th_ref, tl_ref, out_ref):
    table_y = (yh_ref[...], yl_ref[...])
    table_x = (th_ref[...], tl_ref[...])
    spec = product3(split(x_ref[0]), table_y, ((1,), (1,)))
    both = product3(table_x, split(turned(spec)), ((1,), (0,)))
    out_ref[:, 0] = both.reshape(out_ref.shape[0], *out_ref.shape[2:])


def forward(rows, table_y, table_x, blocks):
    slabs, width, height = rows.shape
    wide = table_y[0].shape[0]
    kx = 2 * width // blocks
    whole = lambda a: pl.BlockSpec(a.shape, lambda z: (0,) * a.ndim)
    return pl.pallas_call(
        forward_kernel,
        grid=(slabs,),
        in_specs=[pl.BlockSpec((1, width, height), lambda z: (z, 0, 0))]
        + [whole(a) for a in (*table_y, *table_x)],
        out_specs=pl.BlockSpec((blocks, 1, kx, wide), lambda z: (0, z, 0, 0)),
        out_shape=jax.ShapeDtypeStruct((blocks, slabs, kx, wide), jnp.float32),
        name="forward_xy",
    )(rows, *table_y, *table_x)


def through_z(field, green, image_green):
    depth = len(field)
    length = 2 * depth
    even = fft(field, -1)
    odd = fft([times(v, -z, length) for z, v in enumerate(field)], -1)
    spec = [v for pair in zip(even, odd) for v in pair]
    product = []
    for k in range(length):
        re, im = spec[k]
        mre, mim = times(spec[-k % length], -k * (depth - 1), length)
        (gre, gim), (hre, him) = green(k), image_green(k)
        product.append(
            (
                gre * re - gim * im + hre * mre - him * mim,
                gre * im + gim * re + hre * mim + him * mre,
            )
        )
    even = fft(product[0::2], 1)
    odd = fft(product[1::2], 1)
    return [add(even[z], times(odd[z], z, length)) for z in range(depth)]


def middle_kernel(f_ref, g_ref, h_ref, out_ref):
    slabs = f_ref.shape[1]
    half = f_ref.shape[3] // 2
    at = [(z // slabs, z % slabs) for z in range(f_ref.shape[0] * slabs)]
    field = [(f_ref[a, b, :, :half], f_ref[a, b, :, half:]) for a, b in at]
    both = lambda ref: lambda k: (ref[0, k], ref[1, k])
    for (a, b), (re, im) in zip(at, through_z(field, both(g_ref), both(h_ref))):
        out_ref[a, b, :, :half] = re
        out_ref[a, b, :, half:] = im


def middle(field, green, image_green):
    blocks, slabs, kx, wide = field.shape
    tile = 8
    spec = pl.BlockSpec((blocks, slabs, tile, wide), lambda i: (0, 0, i, 0))
    gspec = pl.BlockSpec((*green.shape[:2], tile, green.shape[3]), lambda i: (0, 0, i, 0))
    return pl.pallas_call(
        middle_kernel,
        grid=(kx // tile,),
        in_specs=[spec, gspec, gspec],
        out_specs=spec,
        out_shape=jax.ShapeDtypeStruct(field.shape, jnp.float32),
        name="middle_z",
    )(field, green, image_green)


def inverse_x_kernel(q_ref, th_ref, tl_ref, out_ref):
    field = q_ref[:, 0].reshape(-1, q_ref.shape[3])
    rows = product3((th_ref[...], tl_ref[...]), split(turned(field)), ((1,), (0,)))
    parts = out_ref.shape[0]
    count = rows.shape[0] // parts
    for part in range(parts):
        start = part * count
        before, after = max(start - 1, 0), min(start + count, rows.shape[0] - 1)
        out_ref[part, 0, :count] = rows[start : start + count]
        out_ref[part, 0, count : count + 8] = jnp.concatenate(
            [rows[before : before + 1], rows[after : after + 1], rows[:6]], axis=0
        )


def inverse_x(field, table, parts):
    blocks, slabs, kx, wide = field.shape
    width = blocks * kx // 2
    whole = lambda a: pl.BlockSpec(a.shape, lambda z: (0,) * a.ndim)
    shape = (parts, slabs, width // parts + 8, wide)
    return pl.pallas_call(
        inverse_x_kernel,
        grid=(slabs,),
        in_specs=[pl.BlockSpec((blocks, 1, kx, wide), lambda z: (0, z, 0, 0))]
        + [whole(a) for a in table],
        out_specs=pl.BlockSpec((parts, 1, *shape[2:]), lambda z: (0, z, 0, 0)),
        out_shape=jax.ShapeDtypeStruct(shape, jnp.float32),
        name="inverse_x",
    )(field, *table)


def differences(main, outer, me, parts, gx_ref, gy_ref):
    count, height = main.shape
    row = lax.broadcasted_iota(jnp.int32, main.shape, 0)
    before = jnp.where(row == 0, outer[0:1], pltpu.roll(main, 1, 0))
    after = jnp.where(row == count - 1, outer[1:2], pltpu.roll(main, count - 1, 0))
    edge = ((row == 0) & (me == 0)) | ((row == count - 1) & (me == parts - 1))
    gx_ref[...] = (after - before) * jnp.where(edge, 1.0, 0.5)
    col = lax.broadcasted_iota(jnp.int32, main.shape, 1)
    before = jnp.where(col == 0, main, pltpu.roll(main, 1, 1))
    after = jnp.where(col == height - 1, main, pltpu.roll(main, height - 1, 1))
    gy_ref[...] = (after - before) * jnp.where((col == 0) | (col == height - 1), 1.0, 0.5)


def inverse_y_kernel(scale, parts, me_ref, s_ref, th_ref, tl_ref, pot_ref, gx_ref, gy_ref):
    me = me_ref[0]
    for z in range(s_ref.shape[1]):
        total = None
        for part in range(parts):
            term = product3(
                split(s_ref[part, z]), (th_ref[part], tl_ref[part]), ((1,), (0,))
            )
            total = term if total is None else total + term
        total = total * scale
        count = total.shape[0] - 8
        main = total[:count]
        differences(main, total[count:], me, parts, gx_ref.at[z], gy_ref.at[z])
        pot_ref[z] = main


def inverse_y(rows, table, me, scale):
    parts, slabs, count, _ = rows.shape
    shape = jax.ShapeDtypeStruct((slabs, count - 8, table[0].shape[2]), jnp.float32)
    vmem = pl.BlockSpec(memory_space=VMEM)
    return pl.pallas_call(
        functools.partial(inverse_y_kernel, scale, parts),
        in_specs=[pl.BlockSpec(memory_space=SMEM), vmem, vmem, vmem],
        out_specs=(vmem, vmem, vmem),
        out_shape=(shape, shape, shape),
        name="inverse_y",
    )(me, rows, *table)


def slope_z(*pot):
    slabs = len(pot)
    size, me = lax.axis_size("gz"), lax.axis_index("gz")
    below = lax.ppermute(pot[-1], "gz", [(i, i + 1) for i in range(size - 1)])
    above = lax.ppermute(pot[0], "gz", [(i + 1, i) for i in range(size - 1)])
    below = jnp.where(me == 0, pot[0], below)
    above = jnp.where(me == size - 1, pot[-1], above)
    padded = jnp.stack([below, *pot, above])
    row = lax.broadcasted_iota(jnp.int32, (slabs, 1, 1), 0)
    edge = ((row == 0) & (me == 0)) | ((row == slabs - 1) & (me == size - 1))
    return (padded[2:] - padded[:-2]) * jnp.where(edge, 1.0, 0.5)


def pieces_spec(count):
    return [pl.BlockSpec(memory_space=VMEM)] * count


def place():
    half = lax.axis_size("gz") // 2
    mine = lax.axis_index("gz")
    return jnp.stack([lax.axis_index("gx"), mine // half, mine % half]).astype(jnp.int32)


def turn_table(space):
    rows = np.concatenate([np.arange(0, 2 * space, 8), np.arange(8)])
    angle = np.outer(rows, np.arange(space)) % (2 * space) * (math.pi / space)
    return np.concatenate([np.cos(angle), np.sin(angle)], axis=1).astype(np.float32)


def shuffled(value, index, block):
    wide = value.shape[1]
    while block < wide:
        if block % 128 == 0:
            parts = [value[:, i : i + block] for i in range(0, wide, block)]
            pairs = [parts[i ^ 1] for i in range(len(parts))]
        else:
            parts = [value[:, i : i + 2 * block] for i in range(0, wide, 2 * block)]
            pairs = [pltpu.roll(p, block, 1) for p in parts]
        value = jnp.where(index % 2 == 1, jnp.concatenate(pairs, axis=1), value)
        index, block = index // 2, 2 * block
    return value


def tables_kernel(space, parts, group, at_ref, turn_ref, density_ref, *refs):
    outs, (x_ref, k_ref) = refs[:9], refs[9:]
    outs[8][...] = density_ref[...]
    me, side, member = at_ref[0], at_ref[1], at_ref[2]
    coarse = 2 * space // 8
    count, block = space // parts, space // group
    for half in (slice(0, space), slice(space, 2 * space)):
        x_ref[:, half] = shuffled(turn_ref[:, half], me, count)
        k_ref[:, half] = shuffled(turn_ref[:, half], member, block)

    def fine(ref):
        return ref[coarse:, :space], ref[coarse:, space:]

    def turned_by(ref, row, cos, sin):
        c, s = ref[pl.ds(row, 1), :space], ref[pl.ds(row, 1), space:]
        return c * cos - s * sin, c * sin + s * cos

    def put(pair, at, lanes, values):
        for ref, value in zip(pair, split(jnp.concatenate(values, axis=0))):
            ref[at : at + 16, lanes] = value

    every = slice(0, space)
    first, second = slice(0, space), slice(space, 2 * space)
    freq = 2 * space // parts
    for k in range(2):
        base = (me ^ k) * (freq // 8)
        pair = outs[2 * k : 2 * k + 2]
        for row in range(0, freq, 16):
            two = [turned_by(turn_ref, base + row // 8 + i, *fine(turn_ref)) for i in range(2)]
            put(pair, row, every, [v[0] for v in two])
            put(pair, freq + row, every, [-v[1] for v in two])
    for row in range(0, space, 16):
        base = side * (space // 8) + (member ^ (row // block)) * (block // 8) + row % block // 8
        two = [turned_by(x_ref, base + i, *fine(x_ref)) for i in range(2)]
        put(outs[4:6], row, first, [v[0] for v in two])
        put(outs[4:6], row, second, [-v[1] for v in two])
    tiles, edges = [], []
    cos, sin = fine(k_ref)
    which = lax.broadcasted_iota(jnp.int32, cos.shape, 0)
    sign = jnp.where((which % 2 == 1) & (side == 1), -1.0, 1.0)
    cos, sin = cos * sign, sin * sign
    for k in range(parts):
        part = me ^ k
        base = part * (count // 8)
        tiles += [turned_by(k_ref, base + i, cos, sin) for i in range(count // 8)]
        start, end = part == 0, part == parts - 1
        for near, step, inside, outside in ((start, -1, 7, 0), (end, count // 8, 0, 7)):
            row = jnp.where(near, base if step < 0 else base + step - 1, base + step)
            edges.append(
                turned_by(
                    k_ref, row, *[jnp.where(near, v[outside : outside + 1], v[inside : inside + 1]) for v in (cos, sin)]
                )
            )
    last = tuple(jnp.broadcast_to(v, cos.shape) for v in edges[0])
    for i, edge in enumerate(edges[1:]):
        last = tuple(jnp.where(which == i + 1, e, v) for e, v in zip(edge, last))
    tiles += [last, last]
    for row in range(0, 8 * len(tiles), 16):
        two = tiles[row // 8 : row // 8 + 2]
        put(outs[6:8], row, first, [v[0] for v in two])
        put(outs[6:8], row, second, [v[1] for v in two])


def tables(at, density, parts, group):
    space = density.shape[2]
    turn = turn_table(space)
    high = lambda *shape: [jax.ShapeDtypeStruct(shape, jnp.bfloat16)] * 2
    shapes = high(4 * space // parts, space) * 2 + high(space, 2 * space)
    shapes += high(space + 16, 2 * space)
    shapes += [jax.ShapeDtypeStruct(density.shape, density.dtype)]
    out = pl.pallas_call(
        functools.partial(tables_kernel, space, parts, group),
        in_specs=[pl.BlockSpec(memory_space=SMEM)] + pieces_spec(2),
        out_specs=pieces_spec(len(shapes)),
        out_shape=shapes,
        scratch_shapes=[VMEM(turn.shape, jnp.float32)] * 2,
        compiler_params=pltpu.CompilerParams(vmem_limit_bytes=LIMIT),
        cost_estimate=cost(0, (turn, *shapes)),
        name="tables",
    )(at, turn, density)
    return out[8], *[out[i : i + 2] for i in range(0, 8, 2)]


def turned_halves(value):
    return tuple(turned(v) for v in split(value))


def forward_half_kernel(*refs):
    parts = lax.axis_size("gx")
    rows, refs = refs[:parts], refs[parts:]
    yh_ref, yl_ref, th_ref, tl_ref, *outs = refs
    table_y = (yh_ref[...], yl_ref[...])
    table_x = (th_ref[...], tl_ref[...])
    kx = outs[0].shape[1]
    slabs = rows[0].shape[0]
    both = jnp.concatenate([r[z] for z in range(slabs) for r in rows], axis=0)
    spec = product3(split(both), table_y, ((1,), (1,)))
    width = spec.shape[0] // slabs
    for z in range(slabs):
        res = product3(table_x, turned_halves(spec[z * width : (z + 1) * width]), ((1,), (0,)))
        for k, ref in enumerate(outs):
            ref[z] = res[k * kx : (k + 1) * kx]


def cost(flops, arrays):
    size = sum(math.prod(a.shape) * a.dtype.itemsize for a in arrays)
    return pl.CostEstimate(flops=flops, bytes_accessed=size, transcendentals=0)


def forward_half(rows, table_y, table_x, group):
    slabs, count, height = rows[0].shape
    width = count * len(rows)
    wide = table_y[0].shape[0]
    shape = jax.ShapeDtypeStruct((slabs, width // group, wide), jnp.float32)
    ins = (*rows, *table_y, *table_x)
    return pl.pallas_call(
        forward_half_kernel,
        in_specs=pieces_spec(len(ins)),
        out_specs=pieces_spec(group),
        out_shape=[shape] * group,
        compiler_params=pltpu.CompilerParams(vmem_limit_bytes=LIMIT),
        cost_estimate=cost(6 * slabs * width * wide * (height + 2 * width), (*ins, *[shape] * group)),
        name="forward_half",
    )(*ins)


def middle_half_kernel(at_ref, *refs):
    group = lax.axis_size("gz") // 2
    side, member = at_ref[1], at_ref[2]
    ins, (g_ref, h_ref), refs = refs[: 2 * group], refs[2 * group : 2 * group + 2], refs[2 * group + 2 :]
    outs, (in_ref, out_ref) = refs[: 2 * group], refs[2 * group :]
    slabs, kx, wide = ins[0].shape
    half = wide // 2
    place = [(side ^ (k // group)) * group + (member ^ (k % group)) for k in range(2 * group)]
    at = [(z // slabs, z % slabs) for z in range(2 * group * slabs)]

    def tile(i, carry):
        rows = pl.ds(pl.multiple_of(8 * i, 8), 8)
        for k, slab in enumerate(place):
            in_ref[slab] = ins[k][:, rows, :]
        field = [(in_ref[a, b, :, :half], in_ref[a, b, :, half:]) for a, b in at]
        both = lambda ref: lambda k: (ref[0, k, rows, :], ref[1, k, rows, :])
        for (a, b), (re, im) in zip(at, through_z(field, both(g_ref), both(h_ref))):
            out_ref[a, b, :, :half] = re
            out_ref[a, b, :, half:] = im
        for k, slab in enumerate(place):
            outs[k][:, rows, :] = out_ref[slab]
        return carry

    lax.fori_loop(0, kx // 8, tile, 0, unroll=2)


def middle_half(at, field, green, image_green):
    slabs, kx, wide = field[0].shape
    ins = (*field, green, image_green)
    shape = jax.ShapeDtypeStruct(field[0].shape, jnp.float32)
    return pl.pallas_call(
        middle_half_kernel,
        in_specs=[pl.BlockSpec(memory_space=SMEM)] + pieces_spec(len(ins)),
        out_specs=pieces_spec(len(field)),
        out_shape=[shape] * len(field),
        scratch_shapes=[VMEM((len(field), slabs, 8, wide), jnp.float32)] * 2,
        cost_estimate=cost(0, (*ins, *[shape] * len(field))),
        compiler_params=pltpu.CompilerParams(vmem_limit_bytes=LIMIT),
        name="middle_half",
    )(at, *ins)


def inverse_x_half_kernel(*refs):
    group = lax.axis_size("gz") // 2
    ins, (th_ref, tl_ref), outs = refs[:group], refs[group : group + 2], refs[group + 2 :]
    table = (th_ref[...], tl_ref[...])
    slabs = ins[0].shape[0]
    count = (outs[0].shape[0] - 8) // slabs
    inner = count * len(outs)
    for z in range(slabs):
        field = jnp.concatenate([r[z] for r in ins], axis=0)
        res = product3(table, turned_halves(field), ((1,), (0,)))
        for k, ref in enumerate(outs):
            ref[z * count : (z + 1) * count] = res[k * count : (k + 1) * count]
            if z == 0:
                ref[slabs * count :] = res[inner : inner + 8]
            at = slabs * count + 2 * z
            ref[at : at + 2] = res[inner + 2 * k : inner + 2 * k + 2]


def inverse_x_half(field, table, parts):
    slabs, kx, wide = field[0].shape
    width = len(field) * kx
    shape = jax.ShapeDtypeStruct((slabs * width // parts + 8, wide), jnp.float32)
    ins = (*field, *table)
    return pl.pallas_call(
        inverse_x_half_kernel,
        in_specs=pieces_spec(len(ins)),
        out_specs=pieces_spec(parts),
        out_shape=[shape] * parts,
        cost_estimate=cost(12 * slabs * (width + 8 * parts) * width * wide, (*ins, *[shape] * parts)),
        compiler_params=pltpu.CompilerParams(vmem_limit_bytes=LIMIT),
        name="inverse_x_half",
    )(*ins)


def inverse_y_partial_kernel(chips, *refs):
    total = None
    outs, refs = refs[-chips:], refs[:-chips]
    for k, ins in enumerate((refs[:chips], refs[chips:-4])):
        rows = jnp.concatenate([r[...] for r in ins], axis=0)
        table = [r[...] for r in refs[len(refs) - 4 :][2 * k : 2 * k + 2]]
        term = product3(split(rows), table, ((1,), (0,)))
        total = term if total is None else total + term
    for k, ref in enumerate(outs):
        ref[...] = total[k * ref.shape[0] : (k + 1) * ref.shape[0]]


def inverse_y_partial(keep, near, table):
    count, wide = keep[0].shape
    shape = jax.ShapeDtypeStruct((count, table[0].shape[1]), jnp.float32)
    ins = (*keep, *near, *table)
    return pl.pallas_call(
        functools.partial(inverse_y_partial_kernel, len(keep)),
        in_specs=pieces_spec(len(ins)),
        out_specs=pieces_spec(len(keep)),
        out_shape=[shape] * len(keep),
        cost_estimate=cost(12 * len(keep) * (count + 8) * wide * shape.shape[1], (*ins, shape, shape)),
        compiler_params=pltpu.CompilerParams(vmem_limit_bytes=LIMIT),
        name="inverse_y_partial",
    )(*ins)


def combine(mine, near, scale):
    total = (mine + near) * scale
    count = (total.shape[0] - 8) // 2
    low, high = total[:count], total[count : 2 * count]
    odd = lax.axis_index("gz") % 2 == 1
    return jnp.where(odd, low, high), jnp.where(odd, high, low), total[2 * count :]


def slopes_kernel(at_ref, first_ref, second_ref, outer_ref, gx_ref, gy_ref):
    parts = lax.axis_size("gx")
    odd = at_ref[2] % 2 == 1
    first, second, outer = first_ref[...], second_ref[...], outer_ref[...]
    for z, main in enumerate((jnp.where(odd, first, second), jnp.where(odd, second, first))):
        differences(main, outer[2 * z :], at_ref[0], parts, gx_ref.at[z], gy_ref.at[z])


def slopes(at, first, second, rows):
    shape = jax.ShapeDtypeStruct((2, *first.shape), jnp.float32)
    return pl.pallas_call(
        slopes_kernel,
        in_specs=[pl.BlockSpec(memory_space=SMEM)] + pieces_spec(3),
        out_specs=pieces_spec(2),
        out_shape=[shape, shape],
        compiler_params=pltpu.CompilerParams(vmem_limit_bytes=LIMIT),
        cost_estimate=cost(0, (first, second, rows, shape, shape)),
        name="slopes",
    )(at, first, second, rows)


def slope_z_pairs(first, second):
    size, mine = lax.axis_size("gz"), lax.axis_index("gz")
    odd, start, end = mine % 2 == 1, mine == 0, mine == size - 1
    near = swap(first, "gz", 1)
    pairs = [(i, i + 1) for i in range(1, size - 1, 2)]
    far = lax.ppermute(second, "gz", pairs + [(b, a) for a, b in pairs])
    low, high = jnp.where(odd, first, second), jnp.where(odd, second, first)
    below, above = jnp.where(odd, near, far), jnp.where(odd, far, near)
    bottom = (high - jnp.where(start, low, below)) * jnp.where(start, 1.0, 0.5)
    top = (jnp.where(end, high, above) - low) * jnp.where(end, 1.0, 0.5)
    return jnp.stack([bottom, top])


def swap(value, axis, mask):
    return lax.ppermute(value, axis, [(s, s ^ mask) for s in range(lax.axis_size(axis))])


def exchange(pieces, axis):
    return [pieces[0]] + [swap(p, axis, k) for k, p in enumerate(pieces) if k > 0]


def after(value, *others):
    return lax.optimization_barrier((value, others))[0]


def sums_y(rows, column, cut):
    near = rows[1::2]
    if cut:
        near = [part for r in near for part in (r[:68], r[68:])]
    near = [swap(r, "gx", 1) for r in near]
    return inverse_y_partial(rows[0::2], near, column)


def halves_device(density, green, image_green):
    slabs, _, height = density.shape
    gz, gx = lax.axis_size("gz"), lax.axis_size("gx")
    group = gz // 2
    width = density.shape[1] * gx
    at = place()
    other = swap(density, "gz", group)
    raw = exchange([density] * gx, "gx")
    local, near_y, far_y, ahead, back = tables(at, density, gx, group)
    other = after(other, near_y)
    field = forward_half([local, *raw[1:]], near_y, ahead, group)
    raw = exchange([other] * gx, "gx")
    field = exchange(field, "gz")
    field += exchange(forward_half(raw, near_y, ahead, group), "gz")
    field = middle_half(at, field, green, image_green)
    own, far = field[:group], field[group:]
    column = (*near_y, *far_y)
    far, own = exchange(far, "gz"), exchange(own, "gz")
    part, give = sums_y(inverse_x_half(far, back, gx), column, True)
    part = part + swap(give, "gx", 2)
    rows = inverse_x_half(own, back, gx)
    mine, give = sums_y((after(rows[0], part), *rows[1:]), column, False)
    mine = after(mine + swap(part, "gz", group))
    scale = 1.0 / (8.0 * slabs * gz * width * height)
    first, second, rows = combine(mine, swap(give, "gx", 2), scale)
    grad_z = slope_z_pairs(first, second)
    return *slopes(at, first, second, rows), grad_z


def per_device(density, green, image_green):
    slabs, count, height = density.shape
    width = count * lax.axis_size("gx")
    if lax.axis_size("gz") == 8 and lax.axis_size("gx") == 4 and slabs == 2 and width == height == 256:
        return halves_device(density, green, image_green)
    gz, gx = lax.axis_size("gz"), lax.axis_size("gx")
    depth = slabs * gz
    column = column_table(height, gx)
    me = lax.axis_index("gx")
    own = tuple(lax.dynamic_index_in_dim(jnp.asarray(t), me, 0, keepdims=False) for t in column)
    rows = lax.all_gather(density, "gx", axis=1, tiled=True)
    field = forward(rows, own, forward_table(width), gz)
    field = lax.all_to_all(field, "gz", split_axis=0, concat_axis=0, tiled=True)
    field = middle(field, green, image_green)
    field = lax.all_to_all(field, "gz", split_axis=0, concat_axis=0, tiled=True)
    part = inverse_x(field, inverse_table(width), gx)
    part = lax.all_to_all(part, "gx", split_axis=0, concat_axis=0, tiled=True)
    scale = 1.0 / (8.0 * depth * width * height)
    pot, grad_x, grad_y = inverse_y(part, column, me.astype(jnp.int32).reshape(1), scale)
    return grad_x, grad_y, slope_z(*pot)


def solution(mesh):
    return jax.shard_map(
        per_device,
        mesh=mesh,
        in_specs=(P("gz", "gx", None), P(None, None, "gz", "gx"), P(None, None, "gz", "gx")),
        out_specs=(P("gz", "gx", None), P("gz", "gx", None), P("gz", "gx", None)),
        check_vma=False,
    )
```

```python
import functools
import math

import jax
import jax.numpy as jnp
import numpy as np
from jax import lax
from jax.experimental import pallas as pl
from jax.experimental.pallas import tpu as pltpu
from jax.sharding import PartitionSpec as P

VMEM = pltpu.VMEM
SMEM = pltpu.SMEM
LIMIT = 16 * 2**20


def halves(table):
    high = table.astype(jnp.bfloat16)
    low = (table - high.astype(np.float64)).astype(jnp.bfloat16)
    return high, low


def split(value):
    high = value.astype(jnp.bfloat16)
    return high, (value - high.astype(jnp.float32)).astype(jnp.bfloat16)


def product3(left, right, dims):
    one = functools.partial(
        lax.dot_general, dimension_numbers=(dims, ((), ())), preferred_element_type=jnp.float32
    )
    return one(left[0], right[0]) + (one(left[1], right[0]) + one(left[0], right[1]))


def turned(value):
    wide = value.shape[1] // 2
    swapped = jnp.concatenate([-value[:, wide:], value[:, :wide]], axis=1)
    return jnp.concatenate([value, swapped], axis=0)


def angles(space, freq):
    turns = np.outer(np.arange(freq), np.arange(space)) % freq
    return turns * (2.0 * math.pi / freq)


def column_table(space, blocks):
    angle = angles(space, 2 * space).reshape(blocks, -1, space)
    return halves(np.concatenate([np.cos(angle), -np.sin(angle)], axis=1))


def forward_table(space):
    angle = angles(space, 2 * space)
    return halves(np.concatenate([np.cos(angle), -np.sin(angle)], axis=1))


def inverse_table(space):
    angle = angles(space, 2 * space).T
    return halves(np.concatenate([np.cos(angle), np.sin(angle)], axis=1))


def times(value, turns, length):
    turns %= length
    re, im = value
    if turns == 0:
        return value
    if 4 * turns == length:
        return -im, re
    if 2 * turns == length:
        return -re, -im
    if 4 * turns == 3 * length:
        return im, -re
    c = math.cos(2.0 * math.pi * turns / length)
    s = math.sin(2.0 * math.pi * turns / length)
    if 8 * turns % length == 0:
        r = math.sqrt(0.5)
        if c * s > 0:
            return math.copysign(r, c) * (re - im), math.copysign(r, c) * (re + im)
        return math.copysign(r, c) * (re + im), math.copysign(r, c) * (im - re)
    return c * re - s * im, c * im + s * re


def add(a, b):
    return a[0] + b[0], a[1] + b[1]


def sub(a, b):
    return a[0] - b[0], a[1] - b[1]


def fft(values, sign):
    count = len(values)
    if count == 1:
        return values
    even, odd = fft(values[0::2], sign), fft(values[1::2], sign)
    odd = [times(v, sign * k, count) for k, v in enumerate(odd)]
    return [add(a, b) for a, b in zip(even, odd)] + [sub(a, b) for a, b in zip(even, odd)]


def forward_kernel(x_ref, yh_ref, yl_ref, th_ref, tl_ref, out_ref):
    table_y = (yh_ref[...], yl_ref[...])
    table_x = (th_ref[...], tl_ref[...])
    spec = product3(split(x_ref[0]), table_y, ((1,), (1,)))
    both = product3(table_x, split(turned(spec)), ((1,), (0,)))
    out_ref[:, 0] = both.reshape(out_ref.shape[0], *out_ref.shape[2:])


def forward(rows, table_y, table_x, blocks):
    slabs, width, height = rows.shape
    wide = table_y[0].shape[0]
    kx = 2 * width // blocks
    whole = lambda a: pl.BlockSpec(a.shape, lambda z: (0,) * a.ndim)
    return pl.pallas_call(
        forward_kernel,
        grid=(slabs,),
        in_specs=[pl.BlockSpec((1, width, height), lambda z: (z, 0, 0))]
        + [whole(a) for a in (*table_y, *table_x)],
        out_specs=pl.BlockSpec((blocks, 1, kx, wide), lambda z: (0, z, 0, 0)),
        out_shape=jax.ShapeDtypeStruct((blocks, slabs, kx, wide), jnp.float32),
        name="forward_xy",
    )(rows, *table_y, *table_x)


def through_z(field, green, image_green):
    depth = len(field)
    length = 2 * depth
    even = fft(field, -1)
    odd = fft([times(v, -z, length) for z, v in enumerate(field)], -1)
    spec = [v for pair in zip(even, odd) for v in pair]
    product = []
    for k in range(length):
        re, im = spec[k]
        mre, mim = times(spec[-k % length], -k * (depth - 1), length)
        (gre, gim), (hre, him) = green(k), image_green(k)
        product.append(
            (
                gre * re - gim * im + hre * mre - him * mim,
                gre * im + gim * re + hre * mim + him * mre,
            )
        )
    even = fft(product[0::2], 1)
    odd = fft(product[1::2], 1)
    return [add(even[z], times(odd[z], z, length)) for z in range(depth)]


def middle_kernel(f_ref, g_ref, h_ref, out_ref):
    slabs = f_ref.shape[1]
    half = f_ref.shape[3] // 2
    at = [(z // slabs, z % slabs) for z in range(f_ref.shape[0] * slabs)]
    field = [(f_ref[a, b, :, :half], f_ref[a, b, :, half:]) for a, b in at]
    both = lambda ref: lambda k: (ref[0, k], ref[1, k])
    for (a, b), (re, im) in zip(at, through_z(field, both(g_ref), both(h_ref))):
        out_ref[a, b, :, :half] = re
        out_ref[a, b, :, half:] = im


def middle(field, green, image_green):
    blocks, slabs, kx, wide = field.shape
    tile = 8
    spec = pl.BlockSpec((blocks, slabs, tile, wide), lambda i: (0, 0, i, 0))
    gspec = pl.BlockSpec((*green.shape[:2], tile, green.shape[3]), lambda i: (0, 0, i, 0))
    return pl.pallas_call(
        middle_kernel,
        grid=(kx // tile,),
        in_specs=[spec, gspec, gspec],
        out_specs=spec,
        out_shape=jax.ShapeDtypeStruct(field.shape, jnp.float32),
        name="middle_z",
    )(field, green, image_green)


def inverse_x_kernel(q_ref, th_ref, tl_ref, out_ref):
    field = q_ref[:, 0].reshape(-1, q_ref.shape[3])
    rows = product3((th_ref[...], tl_ref[...]), split(turned(field)), ((1,), (0,)))
    parts = out_ref.shape[0]
    count = rows.shape[0] // parts
    for part in range(parts):
        start = part * count
        before, after = max(start - 1, 0), min(start + count, rows.shape[0] - 1)
        out_ref[part, 0, :count] = rows[start : start + count]
        out_ref[part, 0, count : count + 8] = jnp.concatenate(
            [rows[before : before + 1], rows[after : after + 1], rows[:6]], axis=0
        )


def inverse_x(field, table, parts):
    blocks, slabs, kx, wide = field.shape
    width = blocks * kx // 2
    whole = lambda a: pl.BlockSpec(a.shape, lambda z: (0,) * a.ndim)
    shape = (parts, slabs, width // parts + 8, wide)
    return pl.pallas_call(
        inverse_x_kernel,
        grid=(slabs,),
        in_specs=[pl.BlockSpec((blocks, 1, kx, wide), lambda z: (0, z, 0, 0))]
        + [whole(a) for a in table],
        out_specs=pl.BlockSpec((parts, 1, *shape[2:]), lambda z: (0, z, 0, 0)),
        out_shape=jax.ShapeDtypeStruct(shape, jnp.float32),
        name="inverse_x",
    )(field, *table)


def differences(main, outer, me, parts, gx_ref, gy_ref):
    count, height = main.shape
    row = lax.broadcasted_iota(jnp.int32, main.shape, 0)
    before = jnp.where(row == 0, outer[0:1], pltpu.roll(main, 1, 0))
    after = jnp.where(row == count - 1, outer[1:2], pltpu.roll(main, count - 1, 0))
    edge = ((row == 0) & (me == 0)) | ((row == count - 1) & (me == parts - 1))
    gx_ref[...] = (after - before) * jnp.where(edge, 1.0, 0.5)
    col = lax.broadcasted_iota(jnp.int32, main.shape, 1)
    before = jnp.where(col == 0, main, pltpu.roll(main, 1, 1))
    after = jnp.where(col == height - 1, main, pltpu.roll(main, height - 1, 1))
    gy_ref[...] = (after - before) * jnp.where((col == 0) | (col == height - 1), 1.0, 0.5)


def inverse_y_kernel(scale, parts, me_ref, s_ref, th_ref, tl_ref, pot_ref, gx_ref, gy_ref):
    me = me_ref[0]
    for z in range(s_ref.shape[1]):
        total = None
        for part in range(parts):
            term = product3(
                split(s_ref[part, z]), (th_ref[part], tl_ref[part]), ((1,), (0,))
            )
            total = term if total is None else total + term
        total = total * scale
        count = total.shape[0] - 8
        main = total[:count]
        differences(main, total[count:], me, parts, gx_ref.at[z], gy_ref.at[z])
        pot_ref[z] = main


def inverse_y(rows, table, me, scale):
    parts, slabs, count, _ = rows.shape
    shape = jax.ShapeDtypeStruct((slabs, count - 8, table[0].shape[2]), jnp.float32)
    vmem = pl.BlockSpec(memory_space=VMEM)
    return pl.pallas_call(
        functools.partial(inverse_y_kernel, scale, parts),
        in_specs=[pl.BlockSpec(memory_space=SMEM), vmem, vmem, vmem],
        out_specs=(vmem, vmem, vmem),
        out_shape=(shape, shape, shape),
        name="inverse_y",
    )(me, rows, *table)


def slope_z(*pot):
    slabs = len(pot)
    size, me = lax.axis_size("gz"), lax.axis_index("gz")
    below = lax.ppermute(pot[-1], "gz", [(i, i + 1) for i in range(size - 1)])
    above = lax.ppermute(pot[0], "gz", [(i + 1, i) for i in range(size - 1)])
    below = jnp.where(me == 0, pot[0], below)
    above = jnp.where(me == size - 1, pot[-1], above)
    padded = jnp.stack([below, *pot, above])
    row = lax.broadcasted_iota(jnp.int32, (slabs, 1, 1), 0)
    edge = ((row == 0) & (me == 0)) | ((row == slabs - 1) & (me == size - 1))
    return (padded[2:] - padded[:-2]) * jnp.where(edge, 1.0, 0.5)


def diagonal_first(pieces):
    return [pieces[0], *pieces[:0:-1]]


def pieces_spec(count):
    return [pl.BlockSpec(memory_space=VMEM)] * count


def place():
    half = lax.axis_size("gz") // 2
    mine = lax.axis_index("gz")
    return jnp.stack([lax.axis_index("gx"), mine // half, mine % half]).astype(jnp.int32)


def turn_table(space):
    rows = np.concatenate([np.arange(0, 2 * space, 8), np.arange(8)])
    angle = np.outer(rows, np.arange(space)) % (2 * space) * (math.pi / space)
    return np.concatenate([np.cos(angle), np.sin(angle)], axis=1).astype(np.float32)


def shuffled(value, index, block):
    wide = value.shape[1]
    while block < wide:
        if block % 128 == 0:
            parts = [value[:, i : i + block] for i in range(0, wide, block)]
            pairs = [parts[i ^ 1] for i in range(len(parts))]
        else:
            parts = [value[:, i : i + 2 * block] for i in range(0, wide, 2 * block)]
            pairs = [pltpu.roll(p, block, 1) for p in parts]
        value = jnp.where(index % 2 == 1, jnp.concatenate(pairs, axis=1), value)
        index, block = index // 2, 2 * block
    return value


def tables_kernel(space, parts, group, at_ref, turn_ref, density_ref, *refs):
    outs, (x_ref, k_ref) = refs[:9], refs[9:]
    outs[8][...] = density_ref[...]
    me, side, member = at_ref[0], at_ref[1], at_ref[2]
    coarse = 2 * space // 8
    count, block = space // parts, space // group
    for half in (slice(0, space), slice(space, 2 * space)):
        x_ref[:, half] = shuffled(turn_ref[:, half], me, count)
        k_ref[:, half] = shuffled(turn_ref[:, half], member, block)

    def fine(ref):
        return ref[coarse:, :space], ref[coarse:, space:]

    def turned_by(ref, row, cos, sin):
        c, s = ref[pl.ds(row, 1), :space], ref[pl.ds(row, 1), space:]
        return c * cos - s * sin, c * sin + s * cos

    def put(pair, at, lanes, values):
        for ref, value in zip(pair, split(jnp.concatenate(values, axis=0))):
            ref[at : at + 16, lanes] = value

    every = slice(0, space)
    first, second = slice(0, space), slice(space, 2 * space)
    freq = 2 * space // parts
    for k in range(2):
        base = (me ^ k) * (freq // 8)
        pair = outs[2 * k : 2 * k + 2]
        for row in range(0, freq, 16):
            two = [turned_by(turn_ref, base + row // 8 + i, *fine(turn_ref)) for i in range(2)]
            put(pair, row, every, [v[0] for v in two])
            put(pair, freq + row, every, [-v[1] for v in two])
    for row in range(0, space, 16):
        base = side * (space // 8) + (member ^ (row // block)) * (block // 8) + row % block // 8
        two = [turned_by(x_ref, base + i, *fine(x_ref)) for i in range(2)]
        put(outs[4:6], row, first, [v[0] for v in two])
        put(outs[4:6], row, second, [-v[1] for v in two])
    tiles, edges = [], []
    cos, sin = fine(k_ref)
    which = lax.broadcasted_iota(jnp.int32, cos.shape, 0)
    sign = jnp.where((which % 2 == 1) & (side == 1), -1.0, 1.0)
    cos, sin = cos * sign, sin * sign
    for k in range(parts):
        part = me ^ k
        base = part * (count // 8)
        tiles += [turned_by(k_ref, base + i, cos, sin) for i in range(count // 8)]
        start, end = part == 0, part == parts - 1
        for near, step, inside, outside in ((start, -1, 7, 0), (end, count // 8, 0, 7)):
            row = jnp.where(near, base if step < 0 else base + step - 1, base + step)
            edges.append(
                turned_by(
                    k_ref, row, *[jnp.where(near, v[outside : outside + 1], v[inside : inside + 1]) for v in (cos, sin)]
                )
            )
    last = tuple(jnp.broadcast_to(v, cos.shape) for v in edges[0])
    for i, edge in enumerate(edges[1:]):
        last = tuple(jnp.where(which == i + 1, e, v) for e, v in zip(edge, last))
    tiles += [last, last]
    for row in range(0, 8 * len(tiles), 16):
        two = tiles[row // 8 : row // 8 + 2]
        put(outs[6:8], row, first, [v[0] for v in two])
        put(outs[6:8], row, second, [v[1] for v in two])


def tables(at, density, parts, group):
    space = density.shape[2]
    turn = turn_table(space)
    high = lambda *shape: [jax.ShapeDtypeStruct(shape, jnp.bfloat16)] * 2
    shapes = high(4 * space // parts, space) * 2 + high(space, 2 * space)
    shapes += high(space + 16, 2 * space)
    shapes += [jax.ShapeDtypeStruct(density.shape, density.dtype)]
    out = pl.pallas_call(
        functools.partial(tables_kernel, space, parts, group),
        in_specs=[pl.BlockSpec(memory_space=SMEM)] + pieces_spec(2),
        out_specs=pieces_spec(len(shapes)),
        out_shape=shapes,
        scratch_shapes=[VMEM(turn.shape, jnp.float32)] * 2,
        compiler_params=pltpu.CompilerParams(vmem_limit_bytes=LIMIT),
        cost_estimate=cost(0, (turn, *shapes)),
        name="tables",
    )(at, turn, density)
    return out[8], *[out[i : i + 2] for i in range(0, 8, 2)]


def turned_halves(value):
    return tuple(turned(v) for v in split(value))


def forward_half_kernel(*refs):
    parts = lax.axis_size("gx")
    rows, refs = refs[:parts], refs[parts:]
    yh_ref, yl_ref, th_ref, tl_ref, *outs = refs
    table_y = (yh_ref[...], yl_ref[...])
    table_x = (th_ref[...], tl_ref[...])
    kx = outs[0].shape[1]
    slabs = rows[0].shape[0]
    both = jnp.concatenate([r[z] for z in range(slabs) for r in rows], axis=0)
    spec = product3(split(both), table_y, ((1,), (1,)))
    width = spec.shape[0] // slabs
    for z in range(slabs):
        res = product3(table_x, turned_halves(spec[z * width : (z + 1) * width]), ((1,), (0,)))
        for k, ref in enumerate(outs):
            ref[z] = res[k * kx : (k + 1) * kx]


def cost(flops, arrays):
    size = sum(math.prod(a.shape) * a.dtype.itemsize for a in arrays)
    return pl.CostEstimate(flops=flops, bytes_accessed=size, transcendentals=0)


def forward_half(rows, table_y, table_x, group):
    slabs, count, height = rows[0].shape
    width = count * len(rows)
    wide = table_y[0].shape[0]
    shape = jax.ShapeDtypeStruct((slabs, width // group, wide), jnp.float32)
    ins = (*rows, *table_y, *table_x)
    return pl.pallas_call(
        forward_half_kernel,
        in_specs=pieces_spec(len(ins)),
        out_specs=pieces_spec(group),
        out_shape=[shape] * group,
        compiler_params=pltpu.CompilerParams(vmem_limit_bytes=LIMIT),
        cost_estimate=cost(6 * slabs * width * wide * (height + 2 * width), (*ins, *[shape] * group)),
        name="forward_half",
    )(*ins)


def middle_half_kernel(at_ref, *refs):
    group = lax.axis_size("gz") // 2
    side, member = at_ref[1], at_ref[2]
    ins, (g_ref, h_ref), refs = refs[: 2 * group], refs[2 * group : 2 * group + 2], refs[2 * group + 2 :]
    outs, (in_ref, out_ref) = refs[: 2 * group], refs[2 * group :]
    slabs, kx, wide = ins[0].shape
    half = wide // 2
    place = [(side ^ (k // group)) * group + (member ^ (k % group)) for k in range(2 * group)]
    at = [(z // slabs, z % slabs) for z in range(2 * group * slabs)]

    def tile(i, carry):
        rows = pl.ds(pl.multiple_of(8 * i, 8), 8)
        for ref, slab in zip(ins, diagonal_first(place[:group]) + diagonal_first(place[group:])):
            in_ref[slab] = ref[:, rows, :]
        field = [(in_ref[a, b, :, :half], in_ref[a, b, :, half:]) for a, b in at]
        both = lambda ref: lambda k: (ref[0, k, rows, :], ref[1, k, rows, :])
        for (a, b), (re, im) in zip(at, through_z(field, both(g_ref), both(h_ref))):
            out_ref[a, b, :, :half] = re
            out_ref[a, b, :, half:] = im
        for k, slab in enumerate(place):
            outs[k][:, rows, :] = out_ref[slab]
        return carry

    lax.fori_loop(0, kx // 8, tile, 0, unroll=2)


def middle_half(at, field, green, image_green):
    slabs, kx, wide = field[0].shape
    group = len(field) // 2
    ins = (*diagonal_first(field[:group]), *diagonal_first(field[group:]), green, image_green)
    shape = jax.ShapeDtypeStruct(field[0].shape, jnp.float32)
    return pl.pallas_call(
        middle_half_kernel,
        in_specs=[pl.BlockSpec(memory_space=SMEM)] + pieces_spec(len(ins)),
        out_specs=pieces_spec(len(field)),
        out_shape=[shape] * len(field),
        scratch_shapes=[VMEM((len(field), slabs, 8, wide), jnp.float32)] * 2,
        cost_estimate=cost(0, (*ins, *[shape] * len(field))),
        compiler_params=pltpu.CompilerParams(vmem_limit_bytes=LIMIT),
        name="middle_half",
    )(at, *ins)


def inverse_x_half_kernel(*refs):
    group = lax.axis_size("gz") // 2
    ins, (th_ref, tl_ref), outs = refs[:group], refs[group : group + 2], refs[group + 2 :]
    table = (th_ref[...], tl_ref[...])
    slabs = ins[0].shape[0]
    count = (outs[0].shape[0] - 8) // slabs
    inner = count * len(outs)
    for z in range(slabs):
        field = jnp.concatenate([r[z] for r in ins], axis=0)
        res = product3(table, turned_halves(field), ((1,), (0,)))
        for k, ref in enumerate(outs):
            ref[z * count : (z + 1) * count] = res[k * count : (k + 1) * count]
            if z == 0:
                ref[slabs * count :] = res[inner : inner + 8]
            at = slabs * count + 2 * z
            ref[at : at + 2] = res[inner + 2 * k : inner + 2 * k + 2]


def inverse_x_half(field, table, parts):
    slabs, kx, wide = field[0].shape
    width = len(field) * kx
    shape = jax.ShapeDtypeStruct((slabs * width // parts + 8, wide), jnp.float32)
    ins = (*field, *table)
    return pl.pallas_call(
        inverse_x_half_kernel,
        in_specs=pieces_spec(len(ins)),
        out_specs=pieces_spec(parts),
        out_shape=[shape] * parts,
        cost_estimate=cost(12 * slabs * (width + 8 * parts) * width * wide, (*ins, *[shape] * parts)),
        compiler_params=pltpu.CompilerParams(vmem_limit_bytes=LIMIT),
        name="inverse_x_half",
    )(*ins)


def inverse_y_partial_kernel(chips, *refs):
    total = None
    outs, refs = refs[-chips:], refs[:-chips]
    for k, ins in enumerate((refs[:chips], refs[chips:-4])):
        rows = jnp.concatenate([r[...] for r in ins], axis=0)
        table = [r[...] for r in refs[len(refs) - 4 :][2 * k : 2 * k + 2]]
        term = product3(split(rows), table, ((1,), (0,)))
        total = term if total is None else total + term
    for k, ref in enumerate(outs):
        ref[...] = total[k * ref.shape[0] : (k + 1) * ref.shape[0]]


def inverse_y_partial(keep, near, table):
    count, wide = keep[0].shape
    shape = jax.ShapeDtypeStruct((count, table[0].shape[1]), jnp.float32)
    ins = (*keep, *near, *table)
    return pl.pallas_call(
        functools.partial(inverse_y_partial_kernel, len(keep)),
        in_specs=pieces_spec(len(ins)),
        out_specs=pieces_spec(len(keep)),
        out_shape=[shape] * len(keep),
        cost_estimate=cost(12 * len(keep) * (count + 8) * wide * shape.shape[1], (*ins, shape, shape)),
        compiler_params=pltpu.CompilerParams(vmem_limit_bytes=LIMIT),
        name="inverse_y_partial",
    )(*ins)


def combine(mine, near, scale):
    total = (mine + near) * scale
    count = (total.shape[0] - 8) // 2
    low, high = total[:count], total[count : 2 * count]
    odd = lax.axis_index("gz") % 2 == 1
    return jnp.where(odd, low, high), jnp.where(odd, high, low), total[2 * count :]


def slopes_kernel(at_ref, first_ref, second_ref, outer_ref, gx_ref, gy_ref):
    parts = lax.axis_size("gx")
    odd = at_ref[2] % 2 == 1
    first, second, outer = first_ref[...], second_ref[...], outer_ref[...]
    for z, main in enumerate((jnp.where(odd, first, second), jnp.where(odd, second, first))):
        differences(main, outer[2 * z :], at_ref[0], parts, gx_ref.at[z], gy_ref.at[z])


def slopes(at, first, second, rows):
    shape = jax.ShapeDtypeStruct((2, *first.shape), jnp.float32)
    return pl.pallas_call(
        slopes_kernel,
        in_specs=[pl.BlockSpec(memory_space=SMEM)] + pieces_spec(3),
        out_specs=pieces_spec(2),
        out_shape=[shape, shape],
        compiler_params=pltpu.CompilerParams(vmem_limit_bytes=LIMIT),
        cost_estimate=cost(0, (first, second, rows, shape, shape)),
        name="slopes",
    )(at, first, second, rows)


def slope_z_pairs(first, second):
    size, mine = lax.axis_size("gz"), lax.axis_index("gz")
    odd, start, end = mine % 2 == 1, mine == 0, mine == size - 1
    near = swap(first, "gz", 1)
    pairs = [(i, i + 1) for i in range(1, size - 1, 2)]
    far = lax.ppermute(second, "gz", pairs + [(b, a) for a, b in pairs])
    low, high = jnp.where(odd, first, second), jnp.where(odd, second, first)
    below, above = jnp.where(odd, near, far), jnp.where(odd, far, near)
    bottom = (high - jnp.where(start, low, below)) * jnp.where(start, 1.0, 0.5)
    top = (jnp.where(end, high, above) - low) * jnp.where(end, 1.0, 0.5)
    return jnp.stack([bottom, top])


def swap(value, axis, mask):
    return lax.ppermute(value, axis, [(s, s ^ mask) for s in range(lax.axis_size(axis))])


def exchange(pieces, axis):
    return [pieces[0]] + [swap(p, axis, k) for k, p in enumerate(pieces) if k > 0]


def after(value, *others):
    return lax.optimization_barrier((value, others))[0]


def sums_y(rows, column, cut):
    near = rows[1::2]
    if cut:
        near = [part for r in near for part in (r[:68], r[68:])]
    near = [swap(r, "gx", 1) for r in near]
    return inverse_y_partial(rows[0::2], near, column)


def halves_device(density, green, image_green):
    slabs, _, height = density.shape
    gz, gx = lax.axis_size("gz"), lax.axis_size("gx")
    group = gz // 2
    width = density.shape[1] * gx
    at = place()
    other = swap(density, "gz", group)
    raw = exchange([density] * gx, "gx")
    local, near_y, far_y, ahead, back = tables(at, density, gx, group)
    other = after(other, near_y)
    field = forward_half([local, *raw[1:]], near_y, ahead, group)
    raw = exchange([other] * gx, "gx")
    field = exchange(field, "gz")
    field += exchange(forward_half(raw, near_y, ahead, group), "gz")
    field = middle_half(at, field, green, image_green)
    own, far = field[:group], field[group:]
    column = (*near_y, *far_y)
    far, own = exchange(far, "gz"), exchange(own, "gz")
    part, give = sums_y(inverse_x_half(far, back, gx), column, True)
    part = part + swap(give, "gx", 2)
    rows = inverse_x_half(own, back, gx)
    mine, give = sums_y((after(rows[0], part), *rows[1:]), column, False)
    mine = after(mine + swap(part, "gz", group))
    scale = 1.0 / (8.0 * slabs * gz * width * height)
    first, second, rows = combine(mine, swap(give, "gx", 2), scale)
    grad_z = slope_z_pairs(first, second)
    return *slopes(at, first, second, rows), grad_z


def per_device(density, green, image_green):
    slabs, count, height = density.shape
    width = count * lax.axis_size("gx")
    if lax.axis_size("gz") == 8 and lax.axis_size("gx") == 4 and slabs == 2 and width == height == 256:
        return halves_device(density, green, image_green)
    gz, gx = lax.axis_size("gz"), lax.axis_size("gx")
    depth = slabs * gz
    column = column_table(height, gx)
    me = lax.axis_index("gx")
    own = tuple(lax.dynamic_index_in_dim(jnp.asarray(t), me, 0, keepdims=False) for t in column)
    rows = lax.all_gather(density, "gx", axis=1, tiled=True)
    field = forward(rows, own, forward_table(width), gz)
    field = lax.all_to_all(field, "gz", split_axis=0, concat_axis=0, tiled=True)
    field = middle(field, green, image_green)
    field = lax.all_to_all(field, "gz", split_axis=0, concat_axis=0, tiled=True)
    part = inverse_x(field, inverse_table(width), gx)
    part = lax.all_to_all(part, "gx", split_axis=0, concat_axis=0, tiled=True)
    scale = 1.0 / (8.0 * depth * width * height)
    pot, grad_x, grad_y = inverse_y(part, column, me.astype(jnp.int32).reshape(1), scale)
    return grad_x, grad_y, slope_z(*pot)


def solution(mesh):
    return jax.shard_map(
        per_device,
        mesh=mesh,
        in_specs=(P("gz", "gx", None), P(None, None, "gz", "gx"), P(None, None, "gz", "gx")),
        out_specs=(P("gz", "gx", None), P("gz", "gx", None), P("gz", "gx", None)),
        check_vma=False,
    )
```
